32 devices in a mesh: section: 4 (over y, x), rows: 8 (over z, core).
Axes of the slice: x: 2, y: 2, z: 4, core: 2. Of those that a mesh axis runs over, the one named last changes fastest.
Arguments:
- tokens: bfloat16 [8, 2048, 768], P(None, 'rows'), may hold values from -6 to 6
- cotangent: bfloat16 [8, 2048, 768], P(None, 'rows'), may hold values from -6 to 6
- segment_ids: int32 [8, 2048], replicated, may hold values from 0 to 15, never falling along the last dimension, each value on 1 to 256 neighbouring positions
- slabs: bfloat16 [4, 768, 3072], P('section'), as said below
- ffn_down: bfloat16 [2, 3072, 768], replicated, may hold values from -0.109375 to 0.109375
- ad_down: float32 [4, 768, 64], P('section'), may hold values from -0.21875 to 0.21875
- ad_down_bias: float32 [4, 64], P('section'), may hold values from -3 to 3
- ad_up: float32 [4, 64, 768], P('section'), may hold values from -0.75 to 0.75
- ad_up_bias: float32 [4, 768], P('section'), may hold values from -2 to 2
- ln_gain: float32 [4, 768], P('section'), may hold values from 0.5 to 1.5
- ln_bias: float32 [4, 768], P('section'), may hold values from -2 to 2
Outputs:
- block_outputs: bfloat16 [4, 8, 2048, 768], P('section', None, 'rows')
- input_grads: bfloat16 [4, 8, 2048, 768], P('section', None, 'rows')
- grad_ad_down: float32 [4, 768, 64], P('section')
- grad_ad_down_bias: float32 [4, 64], P('section')
- grad_ad_up: float32 [4, 64, 768], P('section')
- grad_ad_up_bias: float32 [4, 768], P('section')
- grad_ln_gain: float32 [4, 768], P('section')
- grad_ln_bias: float32 [4, 768], P('section')
The draws below stay inside these ranges and needn't reach their ends.
Inputs may be any that keep to these rules, and one draw needn't show every extreme that they name: `segment_ids`: along each micro-batch the ids never fall; every id of 0 to 15 appears, each segment covers 1 to 256 rows and one covers exactly 256. For even b, columns 2304 to 3072 of slabs[b] are an output projection of larger entries than the other columns.
All inputs are finite; a program needn't handle non-finite values.
Results may differ from the reference program's by a relative error of at most 0.02.
Values may be sent and summed in bfloat16 or wider, within the bound.
No kernel may reach another device: no remote copies, remote signals or barrier semaphores. Data moves between devices by JAX's collectives and lax.ppermute only.
A program may use at most 192 MiB of HBM per device.

```python
import math
import jax
import jax.numpy as jnp
import numpy as np
from jax import lax

D = 768
HEADS = 12
HEAD = 64
FF = 3072
ADAPT = 64
LAYERS = 2
ITEM = 512
MICRO = 8
TOKENS_MB = 2048
SEGS = 16
N_SECTION = 4


def draw_slabs(key, part):
    columns = jnp.arange(FF)
    blocks = jnp.arange(2 * LAYERS)
    wide_cols = (blocks[:, None] % 2 == 0) & (columns[None, :] >= 3 * D)
    col_scale = jnp.where(wide_cols, 32.0 ** 0.5, 1.0) * D ** (-0.5)
    entries = jax.random.normal(key, (2 * LAYERS, D, FF), jnp.float32)
    return (entries * col_scale[:, None, :]).astype(jnp.bfloat16)


def block_scale(own_key, dims, cuts, low, top_value):
    def one(dim, blocks):
        steps = jax.random.uniform(jax.random.fold_in(jax.random.fold_in(own_key, 6), dim), (blocks,), jnp.float32, low / len(cuts), top_value / len(cuts))
        return jnp.repeat(jnp.exp(steps), dims[dim] // blocks).reshape((-1,) + (1,) * (len(dims) - dim - 1))

    loudness = one(*cuts[0])
    for cut in cuts[1:]:
        loudness = loudness * one(*cut)
    return loudness


def profile(count, total, bound, skew):
    loads = [(1 << 20) // math.isqrt(standing ** skew) + 1 for standing in range(2, count + 1)]
    rest, counts = total - bound - (count - 1), [1] * (count - 1)
    while rest > 0:
        movable = [i for i in range(count - 1) if counts[i] < bound]
        whole, budget = sum([loads[i] for i in movable]), rest
        for i in movable:
            addition = min(bound - counts[i], max(1, budget * loads[i] // whole), rest)
            counts[i] = counts[i] + addition
            rest = rest - addition
    return np.array([bound] + counts)


def ragged(key, amount, total, most, slope):
    if amount == 2:
        one = jax.random.randint(key, (), max(1, total - most), min(most, total - 1) + 1)
        return jnp.stack([one, total - one])
    tallies = jnp.asarray(profile(amount, total, most, slope), jnp.int32)
    pairs = (amount - 1) // 2
    giver, sink = tallies[1:1 + 2 * pairs:2], tallies[2:2 + 2 * pairs:2]
    slack = jnp.minimum(giver - 1, most - sink)
    moved = jax.random.randint(jax.random.fold_in(key, 1), (pairs,), 0, 1 << 20) % (slack + 1)
    tallies = tallies.at[1:1 + 2 * pairs:2].set(giver - moved).at[2:2 + 2 * pairs:2].set(sink + moved)
    return tallies[jax.random.permutation(jax.random.fold_in(key, 2), amount)]


def noise(stream_key, extent, width, reach, cuts=(), held_as=jnp.bfloat16):
    drawn = jax.random.normal(stream_key, extent, jnp.float32) * width
    if len(cuts) > 0:
        drawn = block_scale(stream_key, extent, cuts, -0.22, 0.18) * drawn
    return jnp.clip(drawn, min=-reach, max=reach).astype(held_as)


def setup_inputs(seed: int = 0) -> dict:
    arg_keys = jax.random.split(jax.random.key(seed), 12)
    tokens = noise(arg_keys[0], (MICRO, TOKENS_MB, D), 1.0, 6.0, ((1, 8),))
    cotangent = noise(arg_keys[1], (MICRO, TOKENS_MB, D), 1.0, 6.0, ((1, 8),))
    segment_ids = jax.vmap(lambda own: jnp.searchsorted(jnp.cumsum(ragged(own, SEGS, TOKENS_MB, ITEM // 2, 2)), jnp.arange(TOKENS_MB), side="right"))(jax.random.split(arg_keys[2], MICRO)).reshape((MICRO, TOKENS_MB)).astype(jnp.int32)
    slabs = draw_slabs(jax.random.fold_in(arg_keys[11], 71), 0)
    ffn_down = noise(arg_keys[4], (LAYERS, FF, D), FF ** -0.5, 0.109375)
    ad_down = noise(arg_keys[5], (N_SECTION, D, ADAPT), D ** -0.5, 0.21875, ((0, 4),), jnp.float32)
    ad_down_bias = noise(arg_keys[6], (N_SECTION, ADAPT), 0.5, 3.0, ((0, 4),), jnp.float32)
    ad_up = noise(arg_keys[7], (N_SECTION, ADAPT, D), ADAPT ** -0.5, 0.75, ((0, 4),), jnp.float32)
    ad_up_bias = noise(arg_keys[8], (N_SECTION, D), 0.3, 2.0, ((0, 4),), jnp.float32)
    ln_gain = jnp.clip(1.0 + 0.1 * jax.random.normal(arg_keys[9], (N_SECTION, D), jnp.float32), 0.5, 1.5)
    ln_bias = noise(arg_keys[10], (N_SECTION, D), 0.3, 2.0, ((0, 4),), jnp.float32)
    return {"tokens": tokens, "cotangent": cotangent, "segment_ids": segment_ids, "slabs": slabs, "ffn_down": ffn_down, "ad_down": ad_down, "ad_down_bias": ad_down_bias, "ad_up": ad_up, "ad_up_bias": ad_up_bias, "ln_gain": ln_gain, "ln_bias": ln_bias}


@jax.custom_vjp
def low(v):
    return lax.optimization_barrier(v.astype(jnp.bfloat16)).astype(jnp.float32)

@jax.custom_vjp
def low_back(v):
    return v

def low_keep(v):
    return (low(v), None)

def low_pass(kept, grad):
    return (grad,)

def back_keep(v):
    return (v, None)

def back_low(kept, grad):
    return (low(grad),)
low.defvjp(low_keep, low_pass)
low_back.defvjp(back_keep, back_low)
highest = lax.Precision.HIGHEST

def matmul(left, right):
    return jnp.dot(left, right, precision=highest, preferred_element_type=jnp.float32)

def layer_norm(mixed, gain_row, bias_row):
    center = mixed - lax.optimization_barrier(jnp.mean(mixed, axis=-1, keepdims=True))
    spread = lax.optimization_barrier(jnp.mean(center * center, axis=-1, keepdims=True))
    return center * lax.rsqrt(spread + 1e-05) * gain_row + bias_row

def post_block(hidden, branch, down_mat, down_bias, up_mat, up_bias, gain_row, bias_row):
    inner = jax.nn.gelu(matmul(branch, down_mat) + down_bias, approximate=False)
    mixed = hidden + branch + matmul(inner, up_mat) + up_bias
    return layer_norm(mixed, gain_row, bias_row)

def item_attention(pieces):
    queries, key_rows, val_rows, segment = pieces
    scores = low_back(jnp.einsum('qhd,khd->hqk', queries, key_rows, precision=highest))
    allowed = segment[:, None] == segment[None, :]
    weights = jax.nn.softmax(jnp.where(allowed[None], scores, -1000000000.0), axis=-1)
    return jnp.einsum('hqk,khd->qhd', low(weights), val_rows, precision=highest)

def attention_block(hidden, slab, segment, params):
    factor = HEAD ** (-0.5)
    mixed = matmul(hidden, slab[:, :3 * D])
    queries = low(low_back(mixed[:, :D] * factor))
    key_rows = low(low_back(mixed[:, D:2 * D]))
    val_rows = low(low_back(mixed[:, 2 * D:3 * D]))
    layout = (-1, ITEM, HEADS, HEAD)
    context = lax.map(jax.checkpoint(item_attention), (queries.reshape(layout), key_rows.reshape(layout), val_rows.reshape(layout), segment.reshape(-1, ITEM)))
    context = low(low_back(context.reshape(-1, D)))
    branch = low_back(matmul(context, slab[:, 3 * D:]))
    return post_block(hidden, branch, *params)

def ffn_block(hidden, slab, down_proj, params):
    pre_act = low_back(matmul(hidden, slab))
    act_low = low(jax.nn.gelu(pre_act, approximate=False))
    branch = low_back(matmul(act_low, down_proj))
    return post_block(hidden, branch, *params)

def forward(span_tokens, probes, trainable, slabs, ffn_down, segment):
    hidden = span_tokens
    outputs = []
    for block_no in range(N_SECTION):
        hidden = low_back(hidden + probes[block_no])
        params = tuple((param[block_no] for param in trainable))
        if block_no % 2 == 0:
            result = attention_block(hidden, slabs[block_no], segment, params)
        else:
            result = ffn_block(hidden, slabs[block_no], ffn_down[block_no // 2], params)
        hidden = low(low_back(result))
        outputs.append(hidden)
    return (hidden, jnp.stack(outputs))

def reference(tokens, cotangent, segment_ids, slabs, ffn_down, ad_down, ad_down_bias, ad_up, ad_up_bias, ln_gain, ln_bias):
    total_items = MICRO * TOKENS_MB // ITEM
    per_span = max((divisor for divisor in range(1, 9) if total_items % divisor == 0))
    rows_span = per_span * ITEM
    n_spans = total_items // per_span
    flat_tokens = tokens.astype(jnp.float32).reshape(n_spans, rows_span, D)
    flat_cot = cotangent.astype(jnp.float32).reshape(n_spans, rows_span, D)
    flat_seg = segment_ids.reshape(n_spans, rows_span)
    trainable = (ad_down, ad_down_bias, ad_up, ad_up_bias, ln_gain, ln_bias)
    frozen_slabs = slabs.astype(jnp.float32)
    frozen_down = ffn_down.astype(jnp.float32)

    def span_step(totals, pieces):
        span_tokens, span_cot, span_seg = pieces
        probes = jnp.zeros((N_SECTION, rows_span, D), jnp.float32)

        def run_blocks(probe_arg, train_arg):
            return forward(span_tokens, probe_arg, train_arg, frozen_slabs, frozen_down, span_seg)
        (final_rows, outputs), pull = jax.vjp(run_blocks, probes, trainable)
        d_probes, d_train = pull((span_cot, jnp.zeros_like(outputs)))
        totals = jax.tree.map(lambda left, right: left + right, totals, d_train)
        return (totals, (outputs, d_probes))
    zeros_init = jax.tree.map(jnp.zeros_like, trainable)
    totals, (outputs, d_probes) = lax.scan(span_step, zeros_init, (flat_tokens, flat_cot, flat_seg))
    block_outputs = jnp.transpose(outputs, (1, 0, 2, 3)).reshape(N_SECTION, MICRO, TOKENS_MB, D).astype(jnp.bfloat16)
    input_grads = jnp.transpose(d_probes, (1, 0, 2, 3)).reshape(N_SECTION, MICRO, TOKENS_MB, D).astype(jnp.bfloat16)
    return (block_outputs, input_grads, totals[0], totals[1], totals[2], totals[3], totals[4], totals[5])
```

```python
import jax
import jax.numpy as jnp
from jax import lax
from jax.sharding import PartitionSpec as P

HEADS = 12
GROUP = 2
BF = jnp.bfloat16
F32 = jnp.float32


def dot(left, right):
    return jnp.dot(left, right, preferred_element_type=F32)


def dot_t(left, right):
    return lax.dot_general(left, right, (((1,), (1,)), ((), ())), preferred_element_type=F32)


def t_dot(left, right):
    return lax.dot_general(left, right, (((0,), (0,)), ((), ())), preferred_element_type=F32)


def gelu_pair(h):
    phi = 0.5 * (1.0 + lax.erf(h * 0.7071067811865476))
    return h * phi, phi + h * (0.3989422804014327 * jnp.exp(-0.5 * h * h))


def post_forward(hidden, branch, down_mat, down_bias, up_mat, up_bias, gain, bias):
    pre = dot(branch.astype(BF), down_mat.astype(BF)) + down_bias
    inner, slope = gelu_pair(pre)
    mixed = hidden.astype(F32) + branch + dot(inner.astype(BF), up_mat.astype(BF)) + up_bias
    center = mixed - jnp.mean(mixed, axis=-1, keepdims=True)
    rstd = lax.rsqrt(jnp.mean(center * center, axis=-1, keepdims=True) + 1e-05)
    zhat = center * rstd
    out = (zhat * gain + bias).astype(BF)
    return out, (branch.astype(BF), inner.astype(BF), slope, zhat.astype(BF), rstd)


def post_backward(d_out, saved, down_mat, up_mat, gain):
    branch, inner, slope, zhat_low, rstd = saved
    zhat = zhat_low.astype(F32)
    d_out = d_out.astype(F32)
    g_bias = jnp.sum(d_out, axis=0)
    g_gain = jnp.sum(d_out * zhat, axis=0)
    dz = d_out * gain
    dz = rstd * (dz - jnp.mean(dz, axis=-1, keepdims=True)
                 - zhat * jnp.mean(dz * zhat, axis=-1, keepdims=True))
    dz_low = dz.astype(BF)
    g_upb = jnp.sum(dz, axis=0)
    g_up = t_dot(inner, dz_low)
    d_pre = dot_t(dz_low, up_mat.astype(BF)) * slope
    d_pre_low = d_pre.astype(BF)
    g_downb = jnp.sum(d_pre, axis=0)
    g_down_t = t_dot(d_pre_low, branch)
    d_branch = (dz + dot_t(d_pre_low, down_mat.astype(BF))).astype(BF)
    width = dz.shape[1]
    small = jnp.stack([g_upb, g_gain, g_bias, jnp.pad(g_downb, (0, width - g_downb.shape[0]))])
    packed = jnp.concatenate([g_down_t, g_up, small, jnp.zeros((12, width), F32)], axis=0)
    return dz, d_branch, packed.astype(BF)


def heads_of(x):
    return x.reshape(x.shape[0], HEADS, -1)


def attn_forward(hidden, slab, seg, params):
    rows, width = hidden.shape
    qkv = dot(hidden, slab[:, : 3 * width])
    factor = (width // HEADS) ** (-0.5)
    q = (qkv[:, :width] * factor).astype(BF)
    k = qkv[:, width : 2 * width].astype(BF)
    v = qkv[:, 2 * width :].astype(BF)
    s = jnp.einsum("qhd,khd->hqk", heads_of(q), heads_of(k), preferred_element_type=F32)
    s = jnp.where((seg[:, None] == seg[None, :])[None], s, -1e9)
    p = jax.nn.softmax(s, axis=-1).astype(BF)
    c = jnp.einsum("hqk,khd->qhd", p, heads_of(v), preferred_element_type=F32)
    c = c.reshape(rows, width).astype(BF)
    branch = dot(c, slab[:, 3 * width :])
    out, saved = post_forward(hidden, branch, *params)
    return out, (q, k, v, p, c) + saved


def attn_backward(d_out, saved, slab, params):
    q, k, v, p, c = saved[:5]
    rows, width = q.shape
    dz, d_branch, packed = post_backward(d_out, saved[5:], params[0], params[2], params[4])
    dc = dot_t(d_branch, slab[:, 3 * width :]).astype(BF)
    dch = heads_of(dc)
    dp = jnp.einsum("qhd,khd->hqk", dch, heads_of(v), preferred_element_type=F32)
    delta = jnp.sum(heads_of(c).astype(F32) * dch.astype(F32), axis=-1)
    ds = (p.astype(F32) * (dp - delta.T[:, :, None])).astype(BF)
    factor = (width // HEADS) ** (-0.5)
    dq = jnp.einsum("hqk,khd->qhd", ds, heads_of(k), preferred_element_type=F32)
    dk = jnp.einsum("hqk,qhd->khd", ds, heads_of(q), preferred_element_type=F32)
    dv = jnp.einsum("hqk,qhd->khd", p, dch, preferred_element_type=F32)
    flat = jnp.concatenate([(dq * factor).reshape(rows, width), dk.reshape(rows, width),
                            dv.reshape(rows, width)], axis=1).astype(BF)
    return (dz + dot_t(flat, slab[:, : 3 * width])).astype(BF), packed


def ffn_forward(hidden, slab, down, params):
    act, slope = gelu_pair(dot(hidden, slab))
    branch = dot(act.astype(BF), down)
    out, saved = post_forward(hidden, branch, *params)
    return out, (slope.astype(BF),) + saved


def ffn_backward(d_out, saved, slab, down, params):
    dz, d_branch, packed = post_backward(d_out, saved[1:], params[0], params[2], params[4])
    df = (dot_t(d_branch, down) * saved[0].astype(F32)).astype(BF)
    return (dz + dot_t(df, slab)).astype(BF), packed


def per_device(tokens, cotangent, segment_ids, slabs, ffn_down,
               ad_down, ad_down_bias, ad_up, ad_up_bias, ln_gain, ln_bias):
    n_section = lax.axis_size("section")
    n_rows = lax.axis_size("rows")
    s = lax.axis_index("section")
    r = lax.axis_index("rows")
    core = r % GROUP
    n_micro, rows_dev, width = tokens.shape

    def sect(x, apart):
        return lax.ppermute(x, "section", [(i, i ^ apart) for i in range(n_section)])

    def peer(x, apart=1):
        return lax.ppermute(x, "rows", [(i, i ^ apart) for i in range(n_rows)])

    own_micro = s * GROUP + core
    peer_micro = s * GROUP + 1 - core

    def gather_item(x):
        mine = lax.dynamic_index_in_dim(x, own_micro, 0, keepdims=False)
        given = lax.dynamic_index_in_dim(x, peer_micro, 0, keepdims=False)
        return jnp.concatenate([mine, peer(given)], axis=0)

    hidden = gather_item(tokens)
    cot = gather_item(cotangent)
    seg_a = lax.dynamic_slice(segment_ids, (own_micro, r * rows_dev), (1, rows_dev))[0]
    seg_b = lax.dynamic_slice(segment_ids, (own_micro, (r ^ 1) * rows_dev), (1, rows_dev))[0]
    seg = jnp.concatenate([seg_a, seg_b])

    slab = slabs[0]
    half = slab.shape[0] // GROUP
    own_half = lax.dynamic_slice_in_dim(slab, core * half, half, 0)
    got = [slab]
    for apart in range(1, n_section):
        mine = sect(own_half, apart)
        other = peer(mine)
        got.append(jnp.where(core == 0, jnp.concatenate([mine, other], axis=0),
                             jnp.concatenate([other, mine], axis=0)))
    stack = jnp.stack(got)
    small = []
    for part in (ad_down, ad_down_bias, ad_up, ad_up_bias, ln_gain, ln_bias):
        pieces = jnp.stack([part[0]] + [sect(part[0], d) for d in range(1, n_section)])
        small.append(pieces)

    def pick(pieces, b):
        return lax.dynamic_index_in_dim(pieces, s ^ b, 0, keepdims=False)

    w = [pick(stack, b) for b in range(n_section)]
    params = [tuple(pick(pieces, b) for pieces in small) for b in range(n_section)]

    outs, saves = [], []
    for b in range(n_section):
        if b % 2 == 0:
            hidden, saved = attn_forward(hidden, w[b], seg, params[b])
        else:
            hidden, saved = ffn_forward(hidden, w[b], ffn_down[b // 2], params[b])
        outs.append(hidden)
        saves.append(saved)

    def distribute(pieces):
        all_b = jnp.stack(pieces)
        other = peer(all_b[:, rows_dev:])
        mine = all_b[:, :rows_dev]
        both = jnp.where(core == 0, jnp.stack([mine, other], axis=1), jnp.stack([other, mine], axis=1))
        got = [pick(both, 0)]
        got = [lax.dynamic_index_in_dim(both, s, 0, keepdims=False)]
        for d in range(1, n_section):
            got.append(sect(lax.dynamic_index_in_dim(both, s ^ d, 0, keepdims=False), d))
        got = jnp.stack(got)
        return jnp.concatenate([pick(got, q) for q in range(n_section)], axis=0)[None]

    block_outputs = distribute(outs)
    grad = cot
    grads, packs = [None] * n_section, [None] * n_section
    for b in reversed(range(n_section)):
        if b % 2 == 0:
            grad, packs[b] = attn_backward(grad, saves[b], w[b], params[b])
        else:
            grad, packs[b] = ffn_backward(grad, saves[b], w[b], ffn_down[b // 2], params[b])
        grads[b] = grad
    input_grads = distribute(grads)

    total = jnp.stack(packs)
    apart = n_section // 2
    index = s
    while apart >= 1:
        high = (s // apart) % 2
        keep = lax.dynamic_slice_in_dim(total, high * apart, apart, 0)
        give = lax.dynamic_slice_in_dim(total, (1 - high) * apart, apart, 0)
        total = (keep.astype(F32) + sect(give, apart).astype(F32)).astype(BF)
        apart //= 2
    total = total[0]
    apart = 1
    while apart < n_rows:
        total = (total.astype(F32) + peer(total, apart).astype(F32)).astype(BF)
        apart *= 2
    total = total.astype(F32)
    adapt = ad_down.shape[2]
    return (block_outputs, input_grads, total[:adapt].T[None], total[2 * adapt + 3, :adapt][None],
            total[adapt : 2 * adapt][None], total[2 * adapt][None], total[2 * adapt + 1][None],
            total[2 * adapt + 2][None])


def solution(mesh):
    in_specs = (
        P(None, "rows", None), P(None, "rows", None), P(), P("section", None, None), P(),
        P("section", None, None), P("section", None), P("section", None, None),
        P("section", None), P("section", None), P("section", None),
    )
    out_specs = (
        P("section", None, "rows", None), P("section", None, "rows", None),
        P("section", None, None), P("section", None), P("section", None, None),
        P("section", None), P("section", None), P("section", None),
    )
    return jax.shard_map(
        per_device, mesh=mesh, in_specs=in_specs, out_specs=out_specs, check_vma=False
    )
```

```python
import functools

import jax
import jax.numpy as jnp
from jax import lax
from jax.experimental import pallas as pl
from jax.experimental.pallas import tpu as pltpu
from jax.sharding import PartitionSpec as P

HEADS = 12
GROUP = 2
EXTRA = 32
BF = jnp.bfloat16
F32 = jnp.float32
VMEM = pl.BlockSpec(memory_space=pltpu.VMEM)
ANY = pl.BlockSpec(memory_space=pl.ANY)
SMEM = pl.BlockSpec(memory_space=pltpu.SMEM)
LIMIT = 56 * 1024 * 1024


def dot(left, right):
    return jnp.dot(left, right, preferred_element_type=F32)


def dot_t(left, right):
    return lax.dot_general(left, right, (((1,), (1,)), ((), ())), preferred_element_type=F32)


def gelu_pair(x):
    t = 1.0 / (1.0 + 0.23164188 * jnp.abs(x))
    poly = t * (0.127414796 + t * (-0.142248368 + t * (0.710706871 + t * (
        -0.726576014 + t * 0.530702715))))
    bell = jnp.exp(-0.5 * (x * x))
    tail = poly * bell
    phi = jnp.where(x < 0, tail, 1.0 - tail)
    return x * phi, phi + x * (0.3989422804014327 * bell)


class Weights:
    def __init__(self, src, own_slab, own_pack, bufs, slab_v, pack_v, sem):
        self.args = (src, own_slab, own_pack, bufs, slab_v, pack_v, sem)

    def start(self):
        src, own_slab, own_pack, bufs, slab_v, pack_v, sem = self.args
        half = own_slab.shape[0] // GROUP
        for h in range(GROUP):
            rows = pl.ds(h * half, half)

            @pl.when(src[h] == 0)
            def _():
                pltpu.make_async_copy(own_pack.at[h], pack_v.at[h], sem.at[h]).start()
                pltpu.make_async_copy(own_slab.at[rows], slab_v.at[rows], sem.at[2 + h]).start()

            for i, buf in enumerate(bufs):
                @pl.when(src[h] == i + 1)
                def _():
                    pltpu.make_async_copy(buf.at[pl.ds(half, EXTRA)], pack_v.at[h], sem.at[h]).start()
                    pltpu.make_async_copy(buf.at[pl.ds(0, half)], slab_v.at[rows], sem.at[2 + h]).start()

    def wait_slab(self):
        src, own_slab, own_pack, bufs, slab_v, pack_v, sem = self.args
        half = own_slab.shape[0] // GROUP
        for h in range(GROUP):
            rows = pl.ds(h * half, half)
            pltpu.make_async_copy(own_slab.at[rows], slab_v.at[rows], sem.at[2 + h]).wait()

    def wait_pack(self):
        src, own_slab, own_pack, bufs, slab_v, pack_v, sem = self.args
        for h in range(GROUP):
            pltpu.make_async_copy(own_pack.at[h], pack_v.at[h], sem.at[h]).wait()

    def adapters(self, width, adapt):
        pack_v = self.args[5]
        rows = [pack_v[0, :, i * width : (i + 1) * width] for i in range(4)]
        zeros = jnp.zeros((128 - adapt, width), BF)
        per = adapt // EXTRA
        down_t = jnp.concatenate(rows[:per] + [zeros], axis=0)
        up = jnp.concatenate(rows[per : 2 * per] + [zeros], axis=0)
        return down_t, up

    def small(self, i, width):
        pack_v = self.args[5]
        low = 2 * i
        return (pack_v[1, low : low + 1, :width].astype(F32)
                + pack_v[1, low + 1 : low + 2, :width].astype(F32))


def post_forward(wts, x_ref, b_ref, y_ref, saved, adapt):
    low_ref, ut_ref, slope_ref, zhat_ref, rstd_ref = saved
    rows, width = x_ref.shape
    wts.wait_pack()
    down_t, up = wts.adapters(width, adapt)
    down_bias, up_bias, gain, bias = [wts.small(i, width) for i in range(4)]
    step = 128

    def body(i, carry):
        at = pl.ds(pl.multiple_of(i * step, step), step)
        branch = b_ref[at, :]
        low = branch.astype(BF)
        low_ref[at, :] = low
        pre = dot_t(low, down_t) + down_bias[:, :128]
        inner, slope = gelu_pair(pre)
        slope_ref[at, :] = slope
        ut_ref[:, at] = inner.T.astype(BF)
        mixed = x_ref[at, :].astype(F32) + branch + dot(inner.astype(BF), up) + up_bias
        center = mixed - jnp.mean(mixed, axis=-1, keepdims=True)
        rstd = lax.rsqrt(jnp.mean(center * center, axis=-1, keepdims=True) + 1e-05)
        zhat = center * rstd
        y_ref[at, :] = (zhat * gain + bias).astype(BF)
        zhat_ref[at, :] = zhat.astype(BF)
        rstd_ref[at, :] = jnp.broadcast_to(rstd, (step, 128))
        return carry

    lax.fori_loop(0, rows // step, body, 0)


def post_backward(wts, dy_ref, saved, dz_ref, db_ref, grads_ref, dpt_ref, adapt):
    low_ref, ut_ref, slope_ref, zhat_ref, rstd_ref = saved
    rows, width = dy_ref.shape
    wts.wait_pack()
    down_t, up = wts.adapters(width, adapt)
    gain = wts.small(2, width)
    step = 128

    def fold(v):
        return jnp.sum(v.reshape(v.shape[0] // 8, 8, v.shape[1]), axis=0)

    def body(i, carry):
        s_bias, s_gain, s_upb, s_downb = carry
        at = pl.ds(pl.multiple_of(i * step, step), step)
        d_out = dy_ref[at, :].astype(F32)
        zhat = zhat_ref[at, :].astype(F32)
        s_bias = s_bias + fold(d_out)
        s_gain = s_gain + fold(d_out * zhat)
        dz = d_out * gain
        dz = rstd_ref[at, :1] * (dz - jnp.mean(dz, axis=-1, keepdims=True)
                                 - zhat * jnp.mean(dz * zhat, axis=-1, keepdims=True))
        s_upb = s_upb + fold(dz)
        low = dz.astype(BF)
        db_ref[at, :] = low
        d_pre = dot_t(low, up) * slope_ref[at, :]
        s_downb = s_downb + fold(d_pre)
        dpt_ref[:, at] = d_pre.T.astype(BF)
        dz_ref[at, :] = dz
        return s_bias, s_gain, s_upb, s_downb

    zero = jnp.zeros((8, width), F32)
    s_bias, s_gain, s_upb, s_downb = lax.fori_loop(
        0, rows // step, body, (zero, zero, zero, jnp.zeros((8, 128), F32)))
    g_down = dot(dpt_ref[...], low_ref[...])
    g_up = dot(ut_ref[...], db_ref[...])
    grads_ref[0:adapt, :] = g_down[:adapt].astype(BF)
    grads_ref[adapt : 2 * adapt, :] = g_up[:adapt].astype(BF)
    tail = jnp.concatenate(
        [jnp.sum(v, axis=0, keepdims=True) for v in (s_upb, s_gain, s_bias)]
        + [jnp.concatenate([jnp.sum(s_downb, axis=0, keepdims=True),
                            jnp.zeros((1, width - 128), F32)], axis=1),
           jnp.zeros((12, width), F32)], axis=0)
    grads_ref[2 * adapt :, :] = tail.astype(BF)

    def body2(i, carry):
        at = pl.ds(pl.multiple_of(i * step, step), step)
        d_pre = dpt_ref[:, at].astype(F32).T.astype(BF)
        db_ref[at, :] = (dz_ref[at, :] + dot(d_pre, down_t)).astype(BF)
        return carry

    lax.fori_loop(0, rows // step, body2, 0)


def saved_shapes(rows, width):
    return [
        jax.ShapeDtypeStruct((rows, width), BF),
        jax.ShapeDtypeStruct((128, rows), BF),
        jax.ShapeDtypeStruct((rows, 128), F32),
        jax.ShapeDtypeStruct((rows, width), BF),
        jax.ShapeDtypeStruct((rows, 128), F32),
    ]


def weight_scratch(slab):
    return [
        pltpu.VMEM(slab.shape, BF),
        pltpu.VMEM((GROUP, EXTRA, slab.shape[1]), BF),
        pltpu.SemaphoreType.DMA((2 * GROUP,)),
    ]


def call(body, outs, out_specs, scratch, n_smem, in_specs, flops, nbytes, trans, name):
    return pl.pallas_call(
        body,
        out_shape=outs,
        in_specs=[SMEM] * n_smem + in_specs,
        out_specs=out_specs,
        scratch_shapes=scratch,
        name=name,
        cost_estimate=pl.CostEstimate(flops=flops, bytes_accessed=nbytes, transcendentals=trans),
        compiler_params=pltpu.CompilerParams(vmem_limit_bytes=LIMIT),
    )


def ffn_forward(x, src, weights, down, adapt):
    own_slab, own_pack, bufs = weights
    rows, width = x.shape
    ff = own_slab.shape[1]
    chunk = 512
    n_buf = len(bufs)

    def body(src_ref, x_ref, own_ref, pack_ref, *rest):
        bufs_ref, rest = rest[:n_buf], rest[n_buf:]
        down_ref, y_ref, act_ref, *rest = rest
        saved, (slab_v, pack_v, sem, down_v, down_sem, acc) = rest[:5], rest[5:]
        wts = Weights(src_ref, own_ref, pack_ref, bufs_ref, slab_v, pack_v, sem)
        wts.start()
        copy = pltpu.make_async_copy(down_ref, down_v, down_sem)
        copy.start()
        wts.wait_slab()
        copy.wait()

        def step(j, carry):
            cols = pl.ds(pl.multiple_of(j * chunk, chunk), chunk)
            act, slope = gelu_pair(dot(x_ref[...], slab_v[:, cols]))
            act_ref[:, cols] = slope.astype(BF)
            part = dot(act.astype(BF), down_v[cols, :])

            @pl.when(j == 0)
            def _():
                acc[...] = part

            @pl.when(j > 0)
            def _():
                acc[...] += part
            return carry

        lax.fori_loop(0, ff // chunk, step, 0)
        post_forward(wts, x_ref, acc, y_ref, saved, adapt)

    outs = [jax.ShapeDtypeStruct((rows, width), BF), jax.ShapeDtypeStruct((rows, ff), BF)]
    outs += saved_shapes(rows, width)
    scratch = weight_scratch(own_slab) + [
        pltpu.VMEM((ff, width), BF), pltpu.SemaphoreType.DMA, pltpu.VMEM((rows, width), F32)]
    res = call(body, outs, [VMEM] * len(outs), scratch, 1,
               [VMEM, ANY, ANY] + [ANY] * n_buf + [ANY],
               4 * rows * width * ff, 4 * width * ff + 16 * rows * width, rows * ff, "ffn_forward")(
        src, x, own_slab, own_pack, *bufs, down)
    return res[0], tuple(res[1:])


def ffn_backward(dy, saved, src, weights, down, adapt):
    own_slab, own_pack, bufs = weights
    rows, width = dy.shape
    ff = own_slab.shape[1]
    chunk = 512
    n_buf = len(bufs)
    act, saved = saved[0], saved[1:]

    def body(src_ref, dy_ref, *rest):
        saved_ref, rest = rest[:5], rest[5:]
        act_ref, own_ref, pack_ref, *rest = rest
        bufs_ref, rest = rest[:n_buf], rest[n_buf:]
        (down_ref, dx_ref, grads_ref, slab_v, pack_v, sem, down_v, act_v, big_sem, acc, db,
         dpt) = rest
        wts = Weights(src_ref, own_ref, pack_ref, bufs_ref, slab_v, pack_v, sem)
        wts.start()
        copy_down = pltpu.make_async_copy(down_ref, down_v, big_sem.at[0])
        copy_down.start()
        copy_act = pltpu.make_async_copy(act_ref, act_v, big_sem.at[1])
        copy_act.start()
        post_backward(wts, dy_ref, saved_ref, acc, db, grads_ref, dpt, adapt)
        wts.wait_slab()
        copy_down.wait()
        copy_act.wait()

        def step(j, carry):
            cols = pl.ds(pl.multiple_of(j * chunk, chunk), chunk)
            dg = dot_t(db[...], down_v[cols, :])
            df = (dg * act_v[:, cols].astype(F32)).astype(BF)
            acc[...] += dot_t(df, slab_v[:, cols])
            return carry

        lax.fori_loop(0, ff // chunk, step, 0)
        dx_ref[...] = acc[...].astype(BF)

    outs = [jax.ShapeDtypeStruct((rows, width), BF),
            jax.ShapeDtypeStruct((2 * adapt + 16, width), BF)]
    scratch = weight_scratch(own_slab) + [
        pltpu.VMEM((ff, width), BF), pltpu.VMEM((rows, ff), BF), pltpu.SemaphoreType.DMA((2,)),
        pltpu.VMEM((rows, width), F32), pltpu.VMEM((rows, width), BF),
        pltpu.VMEM((128, rows), BF)]
    return call(body, outs, [VMEM] * 2, scratch, 1,
                [VMEM] * 6 + [ANY] * (3 + n_buf) + [ANY],
                4 * rows * width * ff, 4 * width * ff + 16 * rows * width, 0, "ffn_backward")(
        src, dy, *saved, act, own_slab, own_pack, *bufs, down)


def attn_forward(x, seg, src, weights, adapt):
    own_slab, own_pack, bufs = weights
    rows, width = x.shape
    n_buf = len(bufs)
    head = width // HEADS
    pairs = HEADS // 2
    cols_step = 256

    def body(src_ref, x_ref, segc_ref, segr_ref, own_ref, pack_ref, *rest):
        bufs_ref, rest = rest[:n_buf], rest[n_buf:]
        y_ref, qkv_ref, p_ref, c_ref, *rest = rest
        saved, (slab_v, pack_v, sem, acc, bias_v, p_v, p_sem) = rest[:5], rest[5:]
        wts = Weights(src_ref, own_ref, pack_ref, bufs_ref, slab_v, pack_v, sem)
        wts.start()
        bias_v[...] = jnp.where(segc_ref[...] == segr_ref[...], 0.0, -1e30)
        wts.wait_slab()

        def project(j, carry):
            cols = pl.ds(pl.multiple_of(j * cols_step, cols_step), cols_step)
            scale = jnp.where(j < width // cols_step, head ** -0.5, 1.0)
            qkv_ref[:, cols] = (dot(x_ref[...], slab_v[:, cols]) * scale).astype(BF)
            return carry

        lax.fori_loop(0, 3 * width // cols_step, project, 0)
        lower = lax.broadcasted_iota(jnp.int32, (rows, 2 * head), 1) < head

        def attend(i, carry):
            def cols_of(part):
                return pl.ds(pl.multiple_of(part * width + i * 2 * head, 2 * head), 2 * head)

            q, k, v = qkv_ref[:, cols_of(0)], qkv_ref[:, cols_of(1)], qkv_ref[:, cols_of(2)]
            parts = []
            for h in range(2):
                q_h = jnp.where(lower == (h == 0), q, jnp.zeros_like(q))
                s = dot_t(q_h, k) + bias_v[...]
                e = jnp.exp(s - jnp.max(s, axis=-1, keepdims=True))
                p = (e * (1.0 / jnp.sum(e, axis=-1, keepdims=True))).astype(BF)
                p_v[2 * i + h] = p
                pltpu.make_async_copy(p_v.at[2 * i + h], p_ref.at[2 * i + h], p_sem).start()
                parts.append(dot(p, v))
            c_ref[:, pl.ds(pl.multiple_of(i * 2 * head, 2 * head), 2 * head)] = jnp.where(
                lower, parts[0], parts[1]).astype(BF)
            return carry

        lax.fori_loop(0, pairs, attend, 0)

        def output(j, carry):
            cols = pl.ds(pl.multiple_of(j * cols_step, cols_step), cols_step)
            acc[:, cols] = dot(c_ref[...], slab_v[:, pl.ds(
                pl.multiple_of(3 * width + j * cols_step, cols_step), cols_step)])
            return carry

        lax.fori_loop(0, width // cols_step, output, 0)
        post_forward(wts, x_ref, acc, y_ref, saved, adapt)
        pltpu.make_async_copy(p_v, p_ref, p_sem).wait()

    outs = [jax.ShapeDtypeStruct((rows, width), BF), jax.ShapeDtypeStruct((rows, 3 * width), BF),
            jax.ShapeDtypeStruct((HEADS, rows, rows), BF), jax.ShapeDtypeStruct((rows, width), BF)]
    specs = [VMEM, VMEM, ANY, VMEM] + [VMEM] * 5
    outs += saved_shapes(rows, width)
    scratch = weight_scratch(own_slab) + [
        pltpu.VMEM((rows, width), F32), pltpu.VMEM((rows, rows), F32),
        pltpu.VMEM((HEADS, rows, rows), BF), pltpu.SemaphoreType.DMA]
    res = call(body, outs, specs, scratch, 1, [VMEM] * 3 + [ANY] * (2 + n_buf),
               8 * rows * width * width + 4 * rows * rows * width,
               8 * width * width + 2 * HEADS * rows * rows + 16 * rows * width,
               HEADS * rows * rows, "attn_forward")(
        src, x, seg[:, None], seg[None, :], own_slab, own_pack, *bufs)
    return res[0], tuple(res[1:])


def attn_backward(dy, saved, src, weights, adapt):
    own_slab, own_pack, bufs = weights
    rows, width = dy.shape
    n_buf = len(bufs)
    head = width // HEADS
    pairs = HEADS // 2
    cols_step = 256
    qkv, probs, ctx = saved[:3]
    saved = saved[3:]

    def body(src_ref, dy_ref, *rest):
        saved_ref, rest = rest[:5], rest[5:]
        qkv_ref, c_ref, p_ref, own_ref, pack_ref, *rest = rest
        bufs_ref, rest = rest[:n_buf], rest[n_buf:]
        (dx_ref, grads_ref, slab_v, pack_v, sem, p_v, p_sem, dz, db, dpt, dc_v, dqkv) = rest
        wts = Weights(src_ref, own_ref, pack_ref, bufs_ref, slab_v, pack_v, sem)
        wts.start()
        copy_p = pltpu.make_async_copy(p_ref, p_v, p_sem)
        copy_p.start()
        post_backward(wts, dy_ref, saved_ref, dz, db, grads_ref, dpt, adapt)
        wts.wait_slab()

        def context(j, carry):
            cols = pl.ds(pl.multiple_of(j * cols_step, cols_step), cols_step)
            dc_v[:, cols] = dot_t(db[...], slab_v[cols, 3 * width :]).astype(BF)
            return carry

        lax.fori_loop(0, width // cols_step, context, 0)
        copy_p.wait()
        lower = lax.broadcasted_iota(jnp.int32, (rows, 2 * head), 1) < head

        def attend(i, carry):
            def cols_of(part):
                return pl.ds(pl.multiple_of(part * width + i * 2 * head, 2 * head), 2 * head)

            q, k, v = qkv_ref[:, cols_of(0)], qkv_ref[:, cols_of(1)], qkv_ref[:, cols_of(2)]
            dc = dc_v[:, cols_of(0)]
            dc_wide = dc.astype(F32)
            prod = dc_wide * c_ref[:, cols_of(0)].astype(F32)
            q_t = q.astype(F32).T.astype(BF)
            dc_t = dc_wide.T.astype(BF)
            dq, dk, dv = [], [], []
            for h in range(2):
                mine = lower == (h == 0)
                p = p_v[2 * i + h]
                delta = jnp.sum(jnp.where(mine, prod, 0.0), axis=-1, keepdims=True)
                dp = dot_t(jnp.where(mine, dc, jnp.zeros_like(dc)), v)
                ds = (p.astype(F32) * (dp - delta)).astype(BF)
                dq.append(dot(ds, k))
                dk.append(dot(q_t[h * head : (h + 1) * head], ds))
                dv.append(dot(dc_t[h * head : (h + 1) * head], p))
            dqkv[:, cols_of(0)] = (jnp.where(lower, dq[0], dq[1]) * head ** -0.5).astype(BF)
            dqkv[:, cols_of(1)] = jnp.concatenate(dk, axis=0).T.astype(BF)
            dqkv[:, cols_of(2)] = jnp.concatenate(dv, axis=0).T.astype(BF)
            return carry

        lax.fori_loop(0, pairs, attend, 0)

        def output(j, carry):
            cols = pl.ds(pl.multiple_of(j * cols_step, cols_step), cols_step)
            dx_ref[:, cols] = (dz[:, cols] + dot_t(dqkv[...], slab_v[cols, : 3 * width])).astype(BF)
            return carry

        lax.fori_loop(0, width // cols_step, output, 0)

    outs = [jax.ShapeDtypeStruct((rows, width), BF),
            jax.ShapeDtypeStruct((2 * adapt + 16, width), BF)]
    scratch = weight_scratch(own_slab) + [
        pltpu.VMEM((HEADS, rows, rows), BF), pltpu.SemaphoreType.DMA,
        pltpu.VMEM((rows, width), F32), pltpu.VMEM((rows, width), BF),
        pltpu.VMEM((128, rows), BF), pltpu.VMEM((rows, width), BF),
        pltpu.VMEM((rows, 3 * width), BF)]
    return call(body, outs, [VMEM] * 2, scratch, 1,
                [VMEM] * 8 + [ANY] * (3 + n_buf),
                8 * rows * width * width + 8 * rows * rows * width,
                8 * width * width + 2 * HEADS * rows * rows + 16 * rows * width, 0,
                "attn_backward")(
        src, dy, *saved, qkv, ctx, probs, own_slab, own_pack, *bufs)


def split_rows(v):
    high = v.astype(BF)
    return high, (v - high.astype(F32)).astype(BF)


def pack_adapters(ad_down, down_bias, ad_up, up_bias, gain, bias):
    width, adapt = ad_down.shape
    mats = jnp.concatenate([ad_down.T, ad_up], axis=0).astype(BF)
    mats = jnp.concatenate([mats[i : i + EXTRA] for i in range(0, 2 * adapt, EXTRA)], axis=1)
    rows = []
    for v in (jnp.pad(down_bias, (0, width - adapt)), up_bias, gain, bias):
        rows += list(split_rows(v))
    rows = jnp.pad(jnp.stack(rows), ((0, EXTRA - len(rows)), (0, mats.shape[1] - width)))
    return jnp.stack([mats, rows])


def per_device(tokens, cotangent, segment_ids, slabs, ffn_down,
               ad_down, ad_down_bias, ad_up, ad_up_bias, ln_gain, ln_bias):
    n_section = lax.axis_size("section")
    n_rows = lax.axis_size("rows")
    s = lax.axis_index("section")
    r = lax.axis_index("rows")
    core = r % GROUP
    n_micro, rows_dev, width = tokens.shape
    adapt = ad_down.shape[2]

    def sect(x, apart):
        return lax.ppermute(x, "section", [(i, i ^ apart) for i in range(n_section)])

    def peer(x, apart=1):
        return lax.ppermute(x, "rows", [(i, i ^ apart) for i in range(n_rows)])

    own_micro = s * GROUP + core
    peer_micro = s * GROUP + 1 - core

    def gather_item(x):
        mine = lax.dynamic_index_in_dim(x, own_micro, 0, keepdims=False)
        given = lax.dynamic_index_in_dim(x, peer_micro, 0, keepdims=False)
        return jnp.concatenate([mine, peer(given)], axis=0)

    hidden = gather_item(tokens)
    cot = gather_item(cotangent)
    seg_a = lax.dynamic_slice(segment_ids, (own_micro, r * rows_dev), (1, rows_dev))[0]
    seg_b = lax.dynamic_slice(segment_ids, (own_micro, (r ^ 1) * rows_dev), (1, rows_dev))[0]
    seg = jnp.concatenate([seg_a, seg_b])

    slab = slabs[0]
    half = slab.shape[0] // GROUP
    own_pack = pack_adapters(ad_down[0], ad_down_bias[0], ad_up[0], ad_up_bias[0], ln_gain[0],
                             ln_bias[0])
    given = jnp.concatenate([
        lax.dynamic_slice_in_dim(slab, core * half, half, 0),
        lax.dynamic_index_in_dim(own_pack, core, 0, keepdims=False)], axis=0)
    mine = [sect(given, d) for d in range(1, n_section)]
    other = [peer(x) for x in mine]
    weights = (slab, own_pack, tuple(mine + other))

    def source(b):
        d = s ^ b
        at = [jnp.where(d == 0, 0, jnp.where(core == h, d, d + n_section - 1)) for h in range(GROUP)]
        return jnp.stack(at).astype(jnp.int32)

    src = [source(b) for b in range(n_section)]
    outs, saves = [], []
    for b in range(n_section):
        if b % 2 == 0:
            hidden, saved = attn_forward(hidden, seg, src[b], weights, adapt)
        else:
            hidden, saved = ffn_forward(hidden, src[b], weights, ffn_down[b // 2], adapt)
        outs.append(hidden)
        saves.append(saved)

    def pick(pieces, b):
        return lax.dynamic_index_in_dim(pieces, s ^ b, 0, keepdims=False)

    def distribute(pieces):
        all_b = jnp.stack(pieces)
        other = peer(all_b[:, rows_dev:])
        mine = all_b[:, :rows_dev]
        both = jnp.where(core == 0, jnp.stack([mine, other], axis=1), jnp.stack([other, mine], axis=1))
        got = [pick(both, 0)]
        got = [lax.dynamic_index_in_dim(both, s, 0, keepdims=False)]
        for d in range(1, n_section):
            got.append(sect(lax.dynamic_index_in_dim(both, s ^ d, 0, keepdims=False), d))
        got = jnp.stack(got)
        return jnp.concatenate([pick(got, q) for q in range(n_section)], axis=0)[None]

    block_outputs = distribute(outs)
    grad = cot
    grads, packs = [None] * n_section, [None] * n_section
    for b in reversed(range(n_section)):
        if b % 2 == 0:
            grad, packs[b] = attn_backward(grad, saves[b], src[b], weights, adapt)
        else:
            grad, packs[b] = ffn_backward(grad, saves[b], src[b], weights, ffn_down[b // 2], adapt)
        grads[b] = grad
    input_grads = distribute(grads)

    total = jnp.stack(packs)
    apart = n_section // 2
    while apart >= 1:
        high = (s // apart) % 2
        keep = lax.dynamic_slice_in_dim(total, high * apart, apart, 0)
        give = lax.dynamic_slice_in_dim(total, (1 - high) * apart, apart, 0)
        total = (keep.astype(F32) + sect(give, apart).astype(F32)).astype(BF)
        apart //= 2
    total = total[0]
    apart = 1
    while apart < n_rows:
        total = (total.astype(F32) + peer(total, apart).astype(F32)).astype(BF)
        apart *= 2
    total = total.astype(F32)
    return (block_outputs, input_grads, total[:adapt].T[None], total[2 * adapt + 3, :adapt][None],
            total[adapt : 2 * adapt][None], total[2 * adapt][None], total[2 * adapt + 1][None],
            total[2 * adapt + 2][None])


def solution(mesh):
    in_specs = (
        P(None, "rows", None), P(None, "rows", None), P(), P("section", None, None), P(),
        P("section", None, None), P("section", None), P("section", None, None),
        P("section", None), P("section", None), P("section", None),
    )
    out_specs = (
        P("section", None, "rows", None), P("section", None, "rows", None),
        P("section", None, None), P("section", None), P("section", None, None),
        P("section", None), P("section", None), P("section", None),
    )
    return jax.shard_map(
        per_device, mesh=mesh, in_specs=in_specs, out_specs=out_specs, check_vma=False
    )
```

```python
import jax
import jax.numpy as jnp
from jax import lax
from jax.experimental import pallas as pl
from jax.experimental.pallas import tpu as pltpu
from jax.sharding import PartitionSpec as P

HEADS = 12
GROUP = 2
PIECES = 2
EXTRA = 32
COST = 1e8
BF = jnp.bfloat16
F32 = jnp.float32
VMEM = pl.BlockSpec(memory_space=pltpu.VMEM)
ANY = pl.BlockSpec(memory_space=pl.ANY)
SMEM = pl.BlockSpec(memory_space=pltpu.SMEM)
LIMIT = 56 * 1024 * 1024


def dot(left, right):
    return jnp.dot(left, right, preferred_element_type=F32)


def dot_t(left, right):
    return lax.dot_general(left, right, (((1,), (1,)), ((), ())), preferred_element_type=F32)


def gelu_pair(x):
    t = 1.0 / (1.0 + 0.23164188 * jnp.abs(x))
    poly = t * (0.127414796 + t * (-0.142248368 + t * (0.710706871 + t * (
        -0.726576014 + t * 0.530702715))))
    bell = jnp.exp(-0.5 * (x * x))
    tail = poly * bell
    phi = jnp.where(x < 0, tail, 1.0 - tail)
    return x * phi, phi + x * (0.3989422804014327 * bell)


def like(shape, dtype=BF):
    return jax.ShapeDtypeStruct(shape, dtype)


def run(body, ins, outs, stacks, scratch, name, micros, nbytes=0):
    ins, outs = list(ins), list(outs)
    made = [isinstance(x, jax.ShapeDtypeStruct) for x in stacks]
    aliases = {}
    kept = 0
    for i, stack in enumerate(stacks):
        if not made[i]:
            aliases[len(ins) + kept] = len(outs) + i
            kept += 1
    arrays = [a for a, _ in ins] + [x for x, m in zip(stacks, made) if not m]
    specs = [sp for _, sp in ins] + [ANY] * kept
    n_in, n_out, n_stack = len(ins), len(outs), len(stacks)

    def wrapped(*refs):
        got_in = refs[:n_in]
        rest = refs[n_in + kept :]
        body(got_in, rest[:n_out], rest[n_out : n_out + n_stack], rest[n_out + n_stack :])

    res = pl.pallas_call(
        wrapped,
        out_shape=[sh for sh, _ in outs] + [like(x.shape, x.dtype) for x in stacks],
        in_specs=specs,
        out_specs=[sp for _, sp in outs] + [ANY] * n_stack,
        scratch_shapes=scratch,
        name=name,
        input_output_aliases=aliases,
        cost_estimate=pl.CostEstimate(flops=int(micros * COST), bytes_accessed=nbytes,
                                      transcendentals=0),
        compiler_params=pltpu.CompilerParams(vmem_limit_bytes=LIMIT),
    )(*arrays)
    return tuple(res[:n_out]), tuple(res[n_out:])


class Weights:
    def __init__(self, ins, scratch):
        self.src, self.own, self.own_pack = ins[:3]
        self.bufs = ins[3:]
        self.slab, self.pack, self.sem = scratch
        self.rows = self.own.shape[0] // (GROUP * PIECES)

    def start(self):
        sources = len(self.bufs) // PIECES
        size = self.own_pack.shape[0]

        @pl.when(self.src[GROUP] == 0)
        def _():
            pltpu.make_async_copy(self.own_pack, self.pack, self.sem.at[0]).start()

        for i in range(sources // 2):
            @pl.when(self.src[GROUP] == i + 1)
            def _():
                pltpu.make_async_copy(self.bufs[i * PIECES + PIECES - 1].at[pl.ds(self.rows, size)],
                                      self.pack, self.sem.at[0]).start()

        for h in range(GROUP):
            for k in range(PIECES):
                rows = pl.ds((h * PIECES + k) * self.rows, self.rows)

                @pl.when(self.src[h] == 0)
                def _():
                    pltpu.make_async_copy(
                        self.own.at[rows], self.slab.at[rows], self.sem.at[1]).start()

                for i in range(sources):
                    @pl.when(self.src[h] == i + 1)
                    def _():
                        pltpu.make_async_copy(self.bufs[i * PIECES + k].at[pl.ds(0, self.rows)],
                                              self.slab.at[rows], self.sem.at[1]).start()

    def wait_slab(self):
        pltpu.make_async_copy(self.own, self.slab, self.sem.at[1]).wait()

    def wait_pack(self):
        pltpu.make_async_copy(self.own_pack, self.pack, self.sem.at[0]).wait()

    def adapters(self, width, adapt):
        rows = [self.pack[:EXTRA, i * width : (i + 1) * width] for i in range(2 * adapt // EXTRA)]
        zeros = jnp.zeros((128 - adapt, width), BF)
        per = adapt // EXTRA
        down_t = jnp.concatenate(rows[:per] + [zeros], axis=0)
        up = jnp.concatenate(rows[per:] + [zeros], axis=0)
        return down_t, up

    def small(self, i, width):
        low = EXTRA + 2 * i
        return (self.pack[low : low + 1, :width].astype(F32)
                + self.pack[low + 1 : low + 2, :width].astype(F32))


def weight_ins(weights):
    src, own, own_pack, bufs = weights
    return [(src, SMEM), (own, ANY), (own_pack, ANY)] + [(x, ANY) for x in bufs]


def weight_scratch(weights):
    return [pltpu.VMEM(weights[1].shape, BF), pltpu.VMEM(weights[2].shape, BF),
            pltpu.SemaphoreType.DMA((2,))]


def send_out(value_ref, apart, outs, sem):
    half = value_ref.shape[0] // GROUP
    for d in range(len(outs) // GROUP):
        @pl.when(apart == d)
        def _():
            for i in range(GROUP):
                pltpu.make_async_copy(value_ref.at[pl.ds(i * half, half)], outs[GROUP * d + i],
                                      sem).start()

    def wait():
        for i in range(GROUP):
            pltpu.make_async_copy(value_ref.at[pl.ds(i * half, half)], outs[i], sem).wait()
    return wait


def post_forward(wts, x_ref, b_ref, y_ref, saved, adapt):
    low_ref, ut_ref, slope_ref, zhat_ref, rstd_ref = saved
    rows, width = x_ref.shape
    wts.wait_pack()
    down_t, up = wts.adapters(width, adapt)
    down_bias, up_bias, gain, bias = [wts.small(i, width) for i in range(4)]
    step = 128

    def body(i, carry):
        at = pl.ds(pl.multiple_of(i * step, step), step)
        branch = b_ref[at, :]
        low = branch.astype(BF)
        low_ref[at, :] = low
        pre = dot_t(low, down_t) + down_bias[:, :128]
        inner, slope = gelu_pair(pre)
        slope_ref[at, :] = slope
        ut_ref[:, at] = inner.T.astype(BF)
        mixed = x_ref[at, :].astype(F32) + branch + dot(inner.astype(BF), up) + up_bias
        center = mixed - jnp.mean(mixed, axis=-1, keepdims=True)
        rstd = lax.rsqrt(jnp.mean(center * center, axis=-1, keepdims=True) + 1e-05)
        zhat = center * rstd
        y_ref[at, :] = (zhat * gain + bias).astype(BF)
        zhat_ref[at, :] = zhat.astype(BF)
        rstd_ref[at, :] = jnp.broadcast_to(rstd, (step, 128))
        return carry

    lax.fori_loop(0, rows // step, body, 0)


def post_backward(wts, dy_ref, saved, dz_ref, db_ref, grads_ref, dpt_ref, adapt):
    low_ref, ut_ref, slope_ref, zhat_ref, rstd_ref = saved
    rows, width = dy_ref.shape
    wts.wait_pack()
    down_t, up = wts.adapters(width, adapt)
    gain = wts.small(2, width)
    step = 128

    def fold(v):
        return jnp.sum(v.reshape(v.shape[0] // 8, 8, v.shape[1]), axis=0)

    def body(i, carry):
        s_bias, s_gain, s_upb, s_downb = carry
        at = pl.ds(pl.multiple_of(i * step, step), step)
        d_out = dy_ref[at, :].astype(F32)
        zhat = zhat_ref[at, :].astype(F32)
        s_bias = s_bias + fold(d_out)
        s_gain = s_gain + fold(d_out * zhat)
        dz = d_out * gain
        dz = rstd_ref[at, :1] * (dz - jnp.mean(dz, axis=-1, keepdims=True)
                                 - zhat * jnp.mean(dz * zhat, axis=-1, keepdims=True))
        s_upb = s_upb + fold(dz)
        low = dz.astype(BF)
        db_ref[at, :] = low
        d_pre = dot_t(low, up) * slope_ref[at, :]
        s_downb = s_downb + fold(d_pre)
        dpt_ref[:, at] = d_pre.T.astype(BF)
        dz_ref[at, :] = dz
        return s_bias, s_gain, s_upb, s_downb

    zero = jnp.zeros((8, width), F32)
    s_bias, s_gain, s_upb, s_downb = lax.fori_loop(
        0, rows // step, body, (zero, zero, zero, jnp.zeros((8, 128), F32)))
    g_down = dot(dpt_ref[...], low_ref[...])
    g_up = dot(ut_ref[...], db_ref[...])
    grads_ref[0:adapt, :] = g_down[:adapt].astype(BF)
    grads_ref[adapt : 2 * adapt, :] = g_up[:adapt].astype(BF)
    tail = jnp.concatenate(
        [jnp.sum(v, axis=0, keepdims=True) for v in (s_upb, s_gain, s_bias)]
        + [jnp.concatenate([jnp.sum(s_downb, axis=0, keepdims=True),
                            jnp.zeros((1, width - 128), F32)], axis=1),
           jnp.zeros((EXTRA - 4, width), F32)], axis=0)
    grads_ref[2 * adapt :, :] = tail.astype(BF)

    def body2(i, carry):
        at = pl.ds(pl.multiple_of(i * step, step), step)
        d_pre = dpt_ref[:, at].astype(F32).T.astype(BF)
        db_ref[at, :] = (dz_ref[at, :] + dot(d_pre, down_t)).astype(BF)
        return carry

    lax.fori_loop(0, rows // step, body2, 0)


def saved_outs(rows, width):
    return [(like((rows, width)), VMEM), (like((128, rows)), VMEM), (like((rows, 128), F32), VMEM),
            (like((rows, width)), VMEM), (like((rows, 128), F32), VMEM)]


def ffn_forward(x, block, weights, down, adapt, stacks):
    rows, width = x.shape
    ff = weights[1].shape[1]
    chunk = 512
    n_w = len(weight_ins(weights))

    def body(ins, outs, stack_refs, scratch):
        x_ref, down_ref = ins[n_w:]
        y_ref, act_ref, *saved = outs
        down_v, acc, sems = scratch[3:]
        wts = Weights(ins[:n_w], scratch[:3])
        wts.start()
        copy = pltpu.make_async_copy(down_ref.at[block // 2], down_v, sems.at[0])
        copy.start()
        wts.wait_slab()
        copy.wait()

        def step(j, carry):
            cols = pl.ds(pl.multiple_of(j * chunk, chunk), chunk)
            act, slope = gelu_pair(dot(x_ref[...], wts.slab[:, cols]))
            act_ref[:, cols] = slope.astype(BF)
            part = dot(act.astype(BF), down_v[cols, :])

            @pl.when(j == 0)
            def _():
                acc[...] = part

            @pl.when(j > 0)
            def _():
                acc[...] += part
            return carry

        lax.fori_loop(0, ff // chunk, step, 0)
        post_forward(wts, x_ref, acc, y_ref, saved, adapt)
        send_out(y_ref, ins[0][GROUP], stack_refs, sems.at[1])()

    outs = [(like((rows, width)), VMEM), (like((rows, ff)), VMEM)] + saved_outs(rows, width)
    scratch = weight_scratch(weights) + [
        pltpu.VMEM((ff, width), BF), pltpu.VMEM((rows, width), F32),
        pltpu.SemaphoreType.DMA((2,))]
    res, stacks = run(body, weight_ins(weights) + [(x, VMEM), (down, ANY)], outs, stacks, scratch,
                      "ffn_forward", 20)
    return res[0], res[1:], stacks


def ffn_backward(dy, saved, block, weights, down, adapt, stacks):
    rows, width = dy.shape
    ff = weights[1].shape[1]
    chunk = 512
    n_w = len(weight_ins(weights))
    act, saved = saved[0], saved[1:]

    def body(ins, outs, stack_refs, scratch):
        dy_ref, act_ref, down_ref, *saved_ref = ins[n_w:]
        (dx_ref,) = outs
        down_v, act_v, acc, db, dpt, grads, sems = scratch[3:]
        wts = Weights(ins[:n_w], scratch[:3])
        wts.start()
        copy_down = pltpu.make_async_copy(down_ref.at[block // 2], down_v, sems.at[0])
        copy_down.start()
        copy_act = pltpu.make_async_copy(act_ref, act_v, sems.at[1])
        copy_act.start()
        post_backward(wts, dy_ref, saved_ref, acc, db, grads, dpt, adapt)
        copy_grads = pltpu.make_async_copy(grads, stack_refs[-1].at[block], sems.at[2])
        copy_grads.start()
        wts.wait_slab()
        copy_down.wait()
        copy_act.wait()

        def step(j, carry):
            cols = pl.ds(pl.multiple_of(j * chunk, chunk), chunk)
            dg = dot_t(db[...], down_v[cols, :])
            df = (dg * act_v[:, cols].astype(F32)).astype(BF)
            acc[...] += dot_t(df, wts.slab[:, cols])
            return carry

        lax.fori_loop(0, ff // chunk, step, 0)
        dx_ref[...] = acc[...].astype(BF)
        send_out(dx_ref, ins[0][GROUP], stack_refs[:-1], sems.at[3])()
        copy_grads.wait()

    scratch = weight_scratch(weights) + [
        pltpu.VMEM((ff, width), BF), pltpu.VMEM((rows, ff), BF), pltpu.VMEM((rows, width), F32),
        pltpu.VMEM((rows, width), BF), pltpu.VMEM((128, rows), BF),
        pltpu.VMEM((2 * adapt + EXTRA, width), BF), pltpu.SemaphoreType.DMA((4,))]
    res, stacks = run(
        body, weight_ins(weights) + [(dy, VMEM), (act, ANY), (down, ANY)] + [(x, VMEM) for x in saved],
        [(like((rows, width)), VMEM)], stacks, scratch, "ffn_backward", 15)
    return res[0], stacks


def attn_forward(x, seg, block, weights, adapt, stacks):
    rows, width = x.shape
    head = width // HEADS
    pairs = HEADS // 2
    cols_step = 256
    n_w = len(weight_ins(weights))

    def body(ins, outs, stack_refs, scratch):
        x_ref, segc_ref, segr_ref = ins[n_w:]
        y_ref, qkv_ref, p_ref, c_ref, *saved = outs
        acc, bias_v, p_v, sems = scratch[3:]
        wts = Weights(ins[:n_w], scratch[:3])
        wts.start()
        bias_v[...] = jnp.where(segc_ref[...] == segr_ref[...], 0.0, -1e30)
        wts.wait_slab()

        def project(j, carry):
            cols = pl.ds(pl.multiple_of(j * cols_step, cols_step), cols_step)
            scale = jnp.where(j < width // cols_step, head ** -0.5, 1.0)
            qkv_ref[:, cols] = (dot(x_ref[...], wts.slab[:, cols]) * scale).astype(BF)
            return carry

        lax.fori_loop(0, 3 * width // cols_step, project, 0)
        lower = lax.broadcasted_iota(jnp.int32, (rows, 2 * head), 1) < head

        def attend(i, carry):
            def cols_of(part):
                return pl.ds(pl.multiple_of(part * width + i * 2 * head, 2 * head), 2 * head)

            q, k, v = qkv_ref[:, cols_of(0)], qkv_ref[:, cols_of(1)], qkv_ref[:, cols_of(2)]
            parts = []
            for h in range(2):
                q_h = jnp.where(lower == (h == 0), q, jnp.zeros_like(q))
                s = dot_t(q_h, k) + bias_v[...]
                e = jnp.exp(s - jnp.max(s, axis=-1, keepdims=True))
                p = (e * (1.0 / jnp.sum(e, axis=-1, keepdims=True))).astype(BF)
                p_v[2 * i + h] = p
                pltpu.make_async_copy(p_v.at[2 * i + h], p_ref.at[2 * i + h], sems.at[0]).start()
                parts.append(dot(p, v))
            c_ref[:, pl.ds(pl.multiple_of(i * 2 * head, 2 * head), 2 * head)] = jnp.where(
                lower, parts[0], parts[1]).astype(BF)
            return carry

        lax.fori_loop(0, pairs, attend, 0)

        def output(j, carry):
            cols = pl.ds(pl.multiple_of(j * cols_step, cols_step), cols_step)
            acc[:, cols] = dot(c_ref[...], wts.slab[:, pl.ds(
                pl.multiple_of(3 * width + j * cols_step, cols_step), cols_step)])
            return carry

        lax.fori_loop(0, width // cols_step, output, 0)
        post_forward(wts, x_ref, acc, y_ref, saved, adapt)
        send_out(y_ref, ins[0][GROUP], stack_refs, sems.at[1])()
        pltpu.make_async_copy(p_v, p_ref, sems.at[0]).wait()

    outs = [(like((rows, width)), VMEM), (like((rows, 3 * width)), VMEM),
            (like((HEADS, rows, rows)), ANY), (like((rows, width)), VMEM)]
    outs += saved_outs(rows, width)
    scratch = weight_scratch(weights) + [
        pltpu.VMEM((rows, width), F32), pltpu.VMEM((rows, rows), F32),
        pltpu.VMEM((HEADS, rows, rows), BF), pltpu.SemaphoreType.DMA((2,))]
    res, stacks = run(
        body, weight_ins(weights) + [(x, VMEM), (seg[:, None], VMEM), (seg[None, :], VMEM)],
        outs, stacks, scratch, "attn_forward", 20)
    return res[0], res[1:], stacks


def attn_backward(dy, saved, block, weights, adapt, stacks):
    rows, width = dy.shape
    head = width // HEADS
    pairs = HEADS // 2
    cols_step = 256
    n_w = len(weight_ins(weights))
    qkv, probs, ctx = saved[:3]
    saved = saved[3:]

    def body(ins, outs, stack_refs, scratch):
        dy_ref, p_ref, qkv_ref, c_ref, *saved_ref = ins[n_w:]
        p_v, dz, db, dpt, dc_v, dqkv, dx_v, grads, sems = scratch[3:]
        wts = Weights(ins[:n_w], scratch[:3])
        wts.start()
        copy_p = pltpu.make_async_copy(p_ref, p_v, sems.at[0])
        copy_p.start()
        post_backward(wts, dy_ref, saved_ref, dz, db, grads, dpt, adapt)
        copy_grads = pltpu.make_async_copy(grads, stack_refs[-1].at[block], sems.at[1])
        copy_grads.start()
        wts.wait_slab()

        def context(j, carry):
            cols = pl.ds(pl.multiple_of(j * cols_step, cols_step), cols_step)
            dc_v[:, cols] = dot_t(db[...], wts.slab[cols, 3 * width :]).astype(BF)
            return carry

        lax.fori_loop(0, width // cols_step, context, 0)
        copy_p.wait()
        lower = lax.broadcasted_iota(jnp.int32, (rows, 2 * head), 1) < head

        def attend(i, carry):
            def cols_of(part):
                return pl.ds(pl.multiple_of(part * width + i * 2 * head, 2 * head), 2 * head)

            q, k, v = qkv_ref[:, cols_of(0)], qkv_ref[:, cols_of(1)], qkv_ref[:, cols_of(2)]
            dc = dc_v[:, cols_of(0)]
            dc_wide = dc.astype(F32)
            prod = dc_wide * c_ref[:, cols_of(0)].astype(F32)
            q_t = q.astype(F32).T.astype(BF)
            dc_t = dc_wide.T.astype(BF)
            dq, dk, dv = [], [], []
            for h in range(2):
                mine = lower == (h == 0)
                p = p_v[2 * i + h]
                delta = jnp.sum(jnp.where(mine, prod, 0.0), axis=-1, keepdims=True)
                dp = dot_t(jnp.where(mine, dc, jnp.zeros_like(dc)), v)
                ds = (p.astype(F32) * (dp - delta)).astype(BF)
                dq.append(dot(ds, k))
                dk.append(dot(q_t[h * head : (h + 1) * head], ds))
                dv.append(dot(dc_t[h * head : (h + 1) * head], p))
            dqkv[:, cols_of(0)] = (jnp.where(lower, dq[0], dq[1]) * head ** -0.5).astype(BF)
            dqkv[:, cols_of(1)] = jnp.concatenate(dk, axis=0).T.astype(BF)
            dqkv[:, cols_of(2)] = jnp.concatenate(dv, axis=0).T.astype(BF)
            return carry

        lax.fori_loop(0, pairs, attend, 0)

        def output(j, carry):
            cols = pl.ds(pl.multiple_of(j * cols_step, cols_step), cols_step)
            dx_v[:, cols] = (dz[:, cols] + dot_t(dqkv[...], wts.slab[cols, : 3 * width])).astype(BF)
            return carry

        lax.fori_loop(0, width // cols_step, output, 0)
        if outs:
            outs[0][...] = dx_v[...]
        send_out(dx_v, ins[0][GROUP], stack_refs[:-1], sems.at[2])()
        copy_grads.wait()

    outs = [] if block == 0 else [(like((rows, width)), VMEM)]
    scratch = weight_scratch(weights) + [
        pltpu.VMEM((HEADS, rows, rows), BF), pltpu.VMEM((rows, width), F32),
        pltpu.VMEM((rows, width), BF), pltpu.VMEM((128, rows), BF), pltpu.VMEM((rows, width), BF),
        pltpu.VMEM((rows, 3 * width), BF), pltpu.VMEM((rows, width), BF),
        pltpu.VMEM((2 * adapt + EXTRA, width), BF), pltpu.SemaphoreType.DMA((3,))]
    res, stacks = run(
        body, weight_ins(weights) + [(dy, VMEM), (probs, ANY), (qkv, VMEM), (ctx, VMEM)]
        + [(x, VMEM) for x in saved],
        outs, stacks, scratch, "attn_backward", 20)
    return (res[0] if outs else None), stacks


def place_rows(place, pieces):
    count = len(pieces)

    def body(ins, outs, stack_refs, scratch):
        place_ref, pieces_ref = ins[0], ins[1:]
        buf, sems = scratch
        for i, piece in enumerate(pieces_ref):
            pltpu.make_async_copy(piece, buf.at[i], sems.at[i]).start()
        stores = []
        for i, piece in enumerate(pieces_ref):
            pltpu.make_async_copy(piece, buf.at[i], sems.at[i]).wait()
            stores.append(pltpu.make_async_copy(buf.at[i], outs[0].at[place_ref[i]], sems.at[i]))
            stores[-1].start()
        for copy in stores:
            copy.wait()

    res, _ = run(body, [(place, SMEM)] + [(x, ANY) for x in pieces],
                 [(like((count,) + pieces[0].shape), ANY)], [],
                 [pltpu.VMEM((count,) + pieces[0].shape, BF), pltpu.SemaphoreType.DMA((count,))],
                 "place_rows", 3)
    return res[0]


def split_rows(v):
    high = v.astype(BF)
    return high, (v - high.astype(F32)).astype(BF)


def pack_adapters(ad_down, down_bias, ad_up, up_bias, gain, bias):
    width, adapt = ad_down.shape
    rows = []
    for v in (jnp.pad(down_bias, (0, width - adapt)), up_bias, gain, bias):
        rows += list(split_rows(v))
    mats = jnp.concatenate([ad_down.T, ad_up], axis=0).astype(BF)
    mats = jnp.concatenate([mats[i : i + EXTRA] for i in range(0, 2 * adapt, EXTRA)], axis=1)
    rows = jnp.pad(jnp.stack(rows), ((0, 16 - len(rows)), (0, mats.shape[1] - width)))
    return jnp.concatenate([mats, rows], axis=0)


def per_device(tokens, cotangent, segment_ids, slabs, ffn_down,
               ad_down, ad_down_bias, ad_up, ad_up_bias, ln_gain, ln_bias):
    n_section = lax.axis_size("section")
    n_rows = lax.axis_size("rows")
    s = lax.axis_index("section")
    r = lax.axis_index("rows")
    core = r % GROUP
    n_micro, rows_dev, width = tokens.shape
    adapt = ad_down.shape[2]

    def sect(x, apart, to=None):
        pairs = [(i, i ^ apart) for i in range(n_section)]
        return lax.ppermute(x, "section", [p for p in pairs if to is None or p[1] in to])

    def peer(x, apart=1):
        return lax.ppermute(x, "rows", [(i, i ^ apart) for i in range(n_rows)])

    def cross(x, moves):
        pairs = []
        for (s0, c0), (s1, c1) in moves:
            for g in range(n_rows // GROUP):
                pairs.append((s0 * n_rows + g * GROUP + c0, s1 * n_rows + g * GROUP + c1))
        return lax.ppermute(x, ("section", "rows"), pairs)

    own_micro = s * GROUP + core
    peer_micro = s * GROUP + 1 - core

    slab = slabs[0]
    piece = slab.shape[0] // (GROUP * PIECES)
    adapters = (ad_down[0], ad_down_bias[0], ad_up[0], ad_up_bias[0], ln_gain[0], ln_bias[0])
    near, far, passed = [], [], []
    for k in range(PIECES):
        given = lax.dynamic_slice_in_dim(slab, (core * PIECES + k) * piece, piece, 0)
        if k == PIECES - 1:
            own_pack = pack_adapters(*adapters)
            given = jnp.concatenate([given, own_pack], axis=0)
        near.append(sect(given, 1))
        far.append(sect(given, 2))

    def gather_item(x):
        mine = lax.dynamic_index_in_dim(x, own_micro, 0, keepdims=False)
        given = lax.dynamic_index_in_dim(x, peer_micro, 0, keepdims=False)
        return jnp.concatenate([mine, peer(given)], axis=0)

    hidden = gather_item(tokens)
    cot = gather_item(cotangent)
    seg_a = lax.dynamic_slice(segment_ids, (own_micro, r * rows_dev), (1, rows_dev))[0]
    seg_b = lax.dynamic_slice(segment_ids, (own_micro, (r ^ 1) * rows_dev), (1, rows_dev))[0]
    seg = jnp.concatenate([seg_a, seg_b])

    diag, near_x, far_x, diag_x = [], [], [], []
    sections = range(n_section)
    moves = [((t ^ 1, 0), (t, 0)) for t in sections] + [((t ^ 2, 1), (t, 1)) for t in sections]
    for k in range(PIECES):
        near_x.append(peer(near[k]))
        far_x.append(peer(far[k]))
        diag.append(cross(jnp.where(core == 0, far[k], near[k]), moves))
        diag_x.append(peer(diag[k]))

    def weights_of(b):
        d = s ^ b
        src = [jnp.where(d == 0, 0, jnp.where(core == h, d, d + n_section - 1))
               for h in range(GROUP)] + [d]
        return (jnp.stack(src).astype(jnp.int32), slab, own_pack,
                near + far + diag + near_x + far_x + diag_x)

    weights = [weights_of(b) for b in range(n_section)]
    place = jnp.stack([(s ^ d) * GROUP + (core if i == 0 else 1 - core)
                       for d in sections for i in range(GROUP)]).astype(jnp.int32)

    def deliver(pieces, d):
        moves = [((t ^ d, c), (t, 1 - c)) for t in sections for c in range(GROUP)]
        own = pieces[GROUP * d]
        return [own if d == 0 else sect(own, d), cross(pieces[GROUP * d + 1], moves)]

    pieces = tuple([like((rows_dev, width))] * (GROUP * n_section))
    sent, saves = pieces, []
    for b in range(n_section):
        if b % 2 == 0:
            hidden, saved, sent = attn_forward(hidden, seg, b, weights[b], adapt, sent)
        else:
            hidden, saved, sent = ffn_forward(hidden, b, weights[b], ffn_down, adapt, sent)
        saves.append(saved)

    arrived = {3: deliver(sent, 3), 0: deliver(sent, 0)}
    grad = cot
    stacks = pieces + (like((n_section, 2 * adapt + EXTRA, width)),)
    for b in reversed(range(n_section)):
        if b == 2:
            grad, *late = lax.optimization_barrier((grad, *arrived[3], arrived[0][1], *sent))
            arrived[3], arrived[0], sent = late[:2], [arrived[0][0], late[2]], late[3:]
            arrived[1], arrived[2] = deliver(sent, 1), deliver(sent, 2)
        if b == 1:
            grad, *late = lax.optimization_barrier((grad, *arrived[1], *arrived[2]))
            arrived[1], arrived[2] = late[:2], late[2:]
        if b % 2 == 0:
            grad, stacks = attn_backward(grad, saves[b], b, weights[b], adapt, stacks)
        else:
            grad, stacks = ffn_backward(grad, saves[b], b, weights[b], ffn_down, adapt, stacks)

    block_outputs = place_rows(place, [x for d in sections for x in arrived[d]])
    arrived = [deliver(stacks, d) for d in sections]
    total, arrived[0][1] = lax.optimization_barrier((stacks[-1], arrived[0][1]))
    input_grads = place_rows(place, [x for pair in arrived for x in pair])

    part = total.shape[1] // GROUP
    keep = lax.dynamic_slice_in_dim(total, core * part, part, 1)
    give = lax.dynamic_slice_in_dim(total, (1 - core) * part, part, 1)

    def added(left, right):
        return (left.astype(F32) + right.astype(F32)).astype(BF)

    total = added(keep, peer(give))
    apart = n_section // 2
    while apart >= 1:
        high = (s // apart) % 2
        keep = lax.dynamic_slice_in_dim(total, high * apart, apart, 0)
        give = lax.dynamic_slice_in_dim(total, (1 - high) * apart, apart, 0)
        total = added(keep, sect(give, apart))
        apart //= 2
    total = total[0]
    apart = GROUP
    while apart < n_rows:
        total = added(total, peer(total, apart))
        apart *= 2
    other = peer(total)
    total = jnp.where(core == 0, jnp.concatenate([total, other], axis=0),
                      jnp.concatenate([other, total], axis=0)).astype(F32)
    return (block_outputs[None], input_grads[None], total[:adapt].T[None],
            total[2 * adapt + 3, :adapt][None], total[adapt : 2 * adapt][None],
            total[2 * adapt][None], total[2 * adapt + 1][None], total[2 * adapt + 2][None])


def solution(mesh):
    in_specs = (
        P(None, "rows", None), P(None, "rows", None), P(), P("section", None, None), P(),
        P("section", None, None), P("section", None), P("section", None, None),
        P("section", None), P("section", None), P("section", None),
    )
    out_specs = (
        P("section", None, "rows", None), P("section", None, "rows", None),
        P("section", None, None), P("section", None), P("section", None, None),
        P("section", None), P("section", None), P("section", None),
    )
    return jax.shard_map(
        per_device, mesh=mesh, in_specs=in_specs, out_specs=out_specs, check_vma=False
    )
```

```python
import jax
import jax.numpy as jnp
from jax import lax
from jax.experimental import pallas as pl
from jax.experimental.pallas import tpu as pltpu
from jax.sharding import Mesh, PartitionSpec as P

HEADS = 12
GROUP = 2
PIECES = 1
EXTRA = 32
COST = 1e8
BF = jnp.bfloat16
F32 = jnp.float32
VMEM = pl.BlockSpec(memory_space=pltpu.VMEM)
ANY = pl.BlockSpec(memory_space=pl.ANY)
SMEM = pl.BlockSpec(memory_space=pltpu.SMEM)
LIMIT = 56 * 1024 * 1024


def dot(left, right):
    return jnp.dot(left, right, preferred_element_type=F32)


def dot_t(left, right):
    return lax.dot_general(left, right, (((1,), (1,)), ((), ())), preferred_element_type=F32)


def gelu_pair(x):
    t = 1.0 / (1.0 + 0.23164188 * jnp.abs(x))
    poly = t * (0.127414796 + t * (-0.142248368 + t * (0.710706871 + t * (
        -0.726576014 + t * 0.530702715))))
    bell = jnp.exp(-0.5 * (x * x))
    tail = poly * bell
    phi = jnp.where(x < 0, tail, 1.0 - tail)
    return x * phi, phi + x * (0.3989422804014327 * bell)


def like(shape, dtype=BF):
    return jax.ShapeDtypeStruct(shape, dtype)


def run(body, ins, outs, stacks, scratch, name, micros, nbytes=0):
    ins, outs = list(ins), list(outs)
    made = [isinstance(x, jax.ShapeDtypeStruct) for x in stacks]
    aliases = {}
    kept = 0
    for i, stack in enumerate(stacks):
        if not made[i]:
            aliases[len(ins) + kept] = len(outs) + i
            kept += 1
    arrays = [a for a, _ in ins] + [x for x, m in zip(stacks, made) if not m]
    specs = [sp for _, sp in ins] + [ANY] * kept
    n_in, n_out, n_stack = len(ins), len(outs), len(stacks)

    def wrapped(*refs):
        got_in = refs[:n_in]
        rest = refs[n_in + kept :]
        body(got_in, rest[:n_out], rest[n_out : n_out + n_stack], rest[n_out + n_stack :])

    res = pl.pallas_call(
        wrapped,
        out_shape=[sh for sh, _ in outs] + [like(x.shape, x.dtype) for x in stacks],
        in_specs=specs,
        out_specs=[sp for _, sp in outs] + [ANY] * n_stack,
        scratch_shapes=scratch,
        name=name,
        input_output_aliases=aliases,
        cost_estimate=pl.CostEstimate(flops=int(micros * COST), bytes_accessed=nbytes,
                                      transcendentals=0),
        compiler_params=pltpu.CompilerParams(vmem_limit_bytes=LIMIT),
    )(*arrays)
    return tuple(res[:n_out]), tuple(res[n_out:])


class Copies:
    def __init__(self, sems):
        self.sems, self.used, self.waits = sems, 0, {}

    def sem(self):
        self.used += 1
        return self.sems.at[self.used - 1]

    def start(self, name, *pairs):
        for source, target in pairs:
            copy = pltpu.make_async_copy(source, target, self.sem())
            copy.start()
            self.waits.setdefault(name, []).append(copy.wait)

    def later(self, name, source, target, sem):
        self.waits.setdefault(name, []).append(pltpu.make_async_copy(source, target, sem).wait)

    def wait(self, *names):
        for name in names:
            for wait in self.waits.pop(name, []):
                wait()

    def wait_all(self):
        self.wait(*list(self.waits))


def load_slab(copies, name, src, block, weights, slab_v):
    own, own_pack, bufs = weights
    rows = own.shape[0] // (GROUP * PIECES)
    sem = copies.sem()
    for h in range(GROUP):
        for k in range(PIECES):
            at = pl.ds((h * PIECES + k) * rows, rows)

            @pl.when(src[block, h] == 0)
            def _():
                pltpu.make_async_copy(own.at[at], slab_v.at[at], sem).start()

            for i in range(len(bufs) // PIECES):
                @pl.when(src[block, h] == i + 1)
                def _():
                    pltpu.make_async_copy(bufs[i * PIECES + k].at[pl.ds(0, rows)], slab_v.at[at],
                                          sem).start()
    copies.later(name, own, slab_v, sem)


def load_pack(copies, name, src, block, weights, pack_v):
    own, own_pack, bufs = weights
    rows = own.shape[0] // (GROUP * PIECES)
    size = own_pack.shape[0] // GROUP
    sem = copies.sem()
    for h in range(GROUP):
        at = pl.ds(h * size, size)

        @pl.when(src[block, h] == 0)
        def _():
            pltpu.make_async_copy(own_pack.at[at], pack_v.at[at], sem).start()

        for i in range(len(bufs) // PIECES):
            @pl.when(src[block, h] == i + 1)
            def _():
                pltpu.make_async_copy(bufs[i * PIECES + PIECES - 1].at[pl.ds(rows, size)],
                                      pack_v.at[at], sem).start()
    copies.later(name, own_pack, pack_v, sem)


def send_grads(copies, name, value_ref, apart, outs):
    sem = copies.sem()
    for d, out in enumerate(outs):
        @pl.when(apart == d)
        def _():
            pltpu.make_async_copy(value_ref, out, sem).start()
    copies.later(name, value_ref, outs[0], sem)


def send_rows(copies, name, value_ref, block, core, out):
    half = value_ref.shape[0] // GROUP
    for i in range(GROUP):
        to = GROUP * block + (core if i == 0 else GROUP - 1 - core)
        copies.start(name, (value_ref.at[pl.ds(i * half, half)], out.at[to]))


def adapters(pack, width, adapt):
    rows = [pack[:, i * width : (i + 1) * width] for i in range(2 * adapt // EXTRA)]
    zeros = jnp.zeros((128 - adapt, width), BF)
    per = adapt // EXTRA
    down_t = jnp.concatenate(rows[:per] + [zeros], axis=0)
    up = jnp.concatenate(rows[per:] + [zeros], axis=0)
    return down_t, up


def post_forward(pack, small, x_ref, b_ref, y_ref, saved, adapt):
    low_ref, ut_ref, slope_ref, zhat_ref, rstd_ref = saved
    rows, width = x_ref.shape
    down_t, up = adapters(pack, width, adapt)
    down_bias, up_bias, gain, bias = [small[i : i + 1, :] for i in range(4)]
    step = 128

    def body(i, carry):
        at = pl.ds(pl.multiple_of(i * step, step), step)
        branch = b_ref[at, :]
        low = branch.astype(BF)
        low_ref[at, :] = low
        pre = dot_t(low, down_t) + down_bias[:, :128]
        inner, slope = gelu_pair(pre)
        slope_ref[at, :] = slope
        ut_ref[:, at] = inner.T.astype(BF)
        mixed = x_ref[at, :].astype(F32) + branch + dot(inner.astype(BF), up) + up_bias
        center = mixed - jnp.mean(mixed, axis=-1, keepdims=True)
        rstd = lax.rsqrt(jnp.mean(center * center, axis=-1, keepdims=True) + 1e-05)
        zhat = center * rstd
        y_ref[at, :] = (zhat * gain + bias).astype(BF)
        zhat_ref[at, :] = zhat.astype(BF)
        rstd_ref[at, :] = jnp.broadcast_to(rstd, (step, 128))
        return carry

    lax.fori_loop(0, rows // step, body, 0)


def post_backward(pack, small, dy_ref, saved, dz_ref, db_ref, grads_ref, dpt_ref, adapt):
    low_ref, ut_ref, slope_ref, zhat_ref, rstd_ref = saved
    rows, width = dy_ref.shape
    down_t, up = adapters(pack, width, adapt)
    gain = small[2:3, :]
    step = 128

    def fold(v):
        return jnp.sum(v.reshape(v.shape[0] // 8, 8, v.shape[1]), axis=0)

    def body(i, carry):
        s_bias, s_gain, s_upb, s_downb = carry
        at = pl.ds(pl.multiple_of(i * step, step), step)
        d_out = dy_ref[at, :].astype(F32)
        zhat = zhat_ref[at, :].astype(F32)
        s_bias = s_bias + fold(d_out)
        s_gain = s_gain + fold(d_out * zhat)
        dz = d_out * gain
        dz = rstd_ref[at, :1] * (dz - jnp.mean(dz, axis=-1, keepdims=True)
                                 - zhat * jnp.mean(dz * zhat, axis=-1, keepdims=True))
        s_upb = s_upb + fold(dz)
        low = dz.astype(BF)
        db_ref[at, :] = low
        d_pre = dot_t(low, up) * slope_ref[at, :]
        s_downb = s_downb + fold(d_pre)
        dpt_ref[:, at] = d_pre.T.astype(BF)
        dz_ref[at, :] = dz
        return s_bias, s_gain, s_upb, s_downb

    zero = jnp.zeros((8, width), F32)
    s_bias, s_gain, s_upb, s_downb = lax.fori_loop(
        0, rows // step, body, (zero, zero, zero, jnp.zeros((8, 128), F32)))
    g_down = dot(dpt_ref[...], low_ref[...])
    g_up = dot(ut_ref[...], db_ref[...])
    grads_ref[0:adapt, :] = g_down[:adapt].astype(BF)
    grads_ref[adapt : 2 * adapt, :] = g_up[:adapt].astype(BF)
    tail = jnp.concatenate(
        [jnp.sum(v, axis=0, keepdims=True) for v in (s_upb, s_gain, s_bias)]
        + [jnp.concatenate([jnp.sum(s_downb, axis=0, keepdims=True),
                            jnp.zeros((1, width - 128), F32)], axis=1),
           jnp.zeros((EXTRA - 4, width), F32)], axis=0)
    grads_ref[2 * adapt :, :] = tail.astype(BF)

    def body2(i, carry):
        at = pl.ds(pl.multiple_of(i * step, step), step)
        d_pre = dpt_ref[:, at].astype(F32).T.astype(BF)
        db_ref[at, :] = (dz_ref[at, :] + dot(d_pre, down_t)).astype(BF)
        return carry

    lax.fori_loop(0, rows // step, body2, 0)


def tile(i, size):
    return pl.ds(pl.multiple_of(i * size, size), size)


def ffn_branch(x_ref, slab, down, slope_ref, acc, chunk=512):
    def step(j, carry):
        cols = tile(j, chunk)
        act, slope = gelu_pair(dot(x_ref[...], slab[:, cols]))
        slope_ref[:, cols] = slope.astype(BF)
        part = dot(act.astype(BF), down[cols, :])

        @pl.when(j == 0)
        def _():
            acc[...] = part

        @pl.when(j > 0)
        def _():
            acc[...] += part
        return carry

    lax.fori_loop(0, slab.shape[1] // chunk, step, 0)


def ffn_branch_back(db, slab, down, slope_ref, acc, chunk=512):
    def step(j, carry):
        cols = tile(j, chunk)
        dg = dot_t(db[...], down[cols, :])
        df = (dg * slope_ref[:, cols].astype(F32)).astype(BF)
        acc[...] += dot_t(df, slab[:, cols])
        return carry

    lax.fori_loop(0, slab.shape[1] // chunk, step, 0)


def project(x_ref, slab, qkv_ref, step=256):
    width = x_ref.shape[1]
    scale_q = (width // HEADS) ** -0.5

    def body(j, carry):
        cols = tile(j, step)
        scale = jnp.where(j < width // step, scale_q, 1.0)
        qkv_ref[:, cols] = (dot(x_ref[...], slab[:, cols]) * scale).astype(BF)
        return carry

    lax.fori_loop(0, 3 * width // step, body, 0)


def attend(qkv_ref, bias_v, p_v, c_ref, p_out, p_sem):
    rows, width = c_ref.shape
    head = width // HEADS
    lower = lax.broadcasted_iota(jnp.int32, (rows, 2 * head), 1) < head

    def body(i, carry):
        def part(n):
            return qkv_ref[:, pl.ds(pl.multiple_of(n * width + i * 2 * head, 2 * head), 2 * head)]

        q, k, v = part(0), part(1), part(2)
        parts = []
        for h in range(2):
            q_h = jnp.where(lower == (h == 0), q, jnp.zeros_like(q))
            s = dot_t(q_h, k) + bias_v[...]
            e = jnp.exp(s - jnp.max(s, axis=-1, keepdims=True))
            p = (e * (1.0 / jnp.sum(e, axis=-1, keepdims=True))).astype(BF)
            p_v[2 * i + h] = p
            pltpu.make_async_copy(p_v.at[2 * i + h], p_out.at[2 * i + h], p_sem).start()
            parts.append(dot(p, v))
        c_ref[:, tile(i, 2 * head)] = jnp.where(lower, parts[0], parts[1]).astype(BF)
        return carry

    lax.fori_loop(0, HEADS // 2, body, 0)


def attend_back(qkv_ref, c_ref, dc_ref, p_v, dqkv):
    rows, width = c_ref.shape
    head = width // HEADS
    lower = lax.broadcasted_iota(jnp.int32, (rows, 2 * head), 1) < head

    def body(i, carry):
        def cols(n):
            return pl.ds(pl.multiple_of(n * width + i * 2 * head, 2 * head), 2 * head)

        q, k, v = qkv_ref[:, cols(0)], qkv_ref[:, cols(1)], qkv_ref[:, cols(2)]
        dc = dc_ref[:, cols(0)]
        dc_wide = dc.astype(F32)
        prod = dc_wide * c_ref[:, cols(0)].astype(F32)
        q_t = q.astype(F32).T.astype(BF)
        dc_t = dc_wide.T.astype(BF)
        dq, dk, dv = [], [], []
        for h in range(2):
            mine = lower == (h == 0)
            p = p_v[2 * i + h]
            delta = jnp.sum(jnp.where(mine, prod, 0.0), axis=-1, keepdims=True)
            dp = dot_t(jnp.where(mine, dc, jnp.zeros_like(dc)), v)
            ds = (p.astype(F32) * (dp - delta)).astype(BF)
            dq.append(dot(ds, k))
            dk.append(dot(q_t[h * head : (h + 1) * head], ds))
            dv.append(dot(dc_t[h * head : (h + 1) * head], p))
        dqkv[:, cols(0)] = (jnp.where(lower, dq[0], dq[1]) * head ** -0.5).astype(BF)
        dqkv[:, cols(1)] = jnp.concatenate(dk, axis=0).T.astype(BF)
        dqkv[:, cols(2)] = jnp.concatenate(dv, axis=0).T.astype(BF)
        return carry

    lax.fori_loop(0, HEADS // 2, body, 0)


def by_columns(target, count, value, step=256):
    def body(j, carry):
        cols = tile(j, step)
        target[:, cols] = value(cols, j).astype(target.dtype)
        return carry

    lax.fori_loop(0, count // step, body, 0)


def post_saved(rows, width):
    return [((rows, width), BF), ((128, rows), BF), ((rows, 128), F32), ((rows, width), BF),
            ((rows, 128), F32)]


def block_saved(block, rows, width, ff):
    if block % 2 == 0:
        first = [((rows, 3 * width), BF), ((rows, width), BF), ((HEADS, rows, rows), BF)]
    else:
        first = [((rows, ff), BF)]
    return first + post_saved(rows, width)


def weight_ins(weights):
    own, own_pack, bufs = weights
    return [(own, ANY), (own_pack, ANY)] + [(x, ANY) for x in bufs]


def forward(x, seg, src, weights, small, down, adapt, pieces):
    rows, width = x.shape
    ff = weights[0].shape[1]
    blocks = range(2 * down.shape[0])
    n_w = len(weight_ins(weights))
    shapes = [block_saved(b, rows, width, ff) for b in blocks]

    def body(ins, outs, sent, scratch):
        src_ref, x_ref, segc_ref, segr_ref, small_ref, down_ref = ins[:6]
        wts = (ins[6], ins[7], ins[8 : 6 + n_w])
        saved_out, rest = [], outs
        for b in blocks:
            saved_out.append(rest[: len(shapes[b])])
            rest = rest[len(shapes[b]) :]
        slabs, packs, down_v, y_v, acc, bias_v, sems = scratch[:7]
        kept = [scratch[7:15], scratch[15:21]]
        copies = Copies(sems)
        load_slab(copies, "slab0", src_ref, 0, wts, slabs.at[0])
        for b in blocks:
            load_pack(copies, "pack", src_ref, b, wts, packs.at[b])
        load_slab(copies, "slab1", src_ref, 1, wts, slabs.at[1])
        copies.start("down", (down_ref.at[0], down_v))
        bias_v[...] = jnp.where(segc_ref[...] == segr_ref[...], 0.0, -1e30)
        hidden = x_ref
        for b in blocks:
            slab = slabs.at[b % 2]
            copies.wait("slab%d" % b, "saved%d" % (b - 2))
            mine = kept[b % 2]
            y = y_v.at[b % 2]
            if b % 2 == 0:
                qkv, ctx, probs = mine[:3]
                project(hidden, slab, qkv)
                copies.start("saved%d" % b, (qkv, saved_out[b][0]))
                p_sem = copies.sem()
                attend(qkv, bias_v, probs, ctx, saved_out[b][2], p_sem)
                copies.later("saved%d" % b, probs, saved_out[b][2], p_sem)
                copies.start("saved%d" % b, (ctx, saved_out[b][1]))
                by_columns(acc, width, lambda cols, j: dot(ctx[...], slab[:, pl.ds(
                    pl.multiple_of(3 * width + j * 256, 256), 256)]))
                post = mine[3:]
                n_first = 3
            else:
                copies.wait("down")
                ffn_branch(hidden, slab, down_v, mine[0], acc)
                copies.start("saved%d" % b, (mine[0], saved_out[b][0]))
                if b + 2 in blocks:
                    copies.start("down", (down_ref.at[b // 2 + 1], down_v))
                post = mine[1:]
                n_first = 1
            if b + 2 in blocks:
                load_slab(copies, "slab%d" % (b + 2), src_ref, b + 2, wts, slab)
            copies.wait("pack", "rows%d" % (b - 2))
            post_forward(packs.at[b], small_ref.at[src_ref[b, GROUP]], hidden, acc, y, post, adapt)
            send_rows(copies, "rows%d" % b, y, b, src_ref[b, GROUP + 1], sent[0])
            copies.start("saved%d" % b, *zip(post, saved_out[b][n_first:]))
            hidden = y
        copies.wait_all()

    outs = [(like(sh, dt), ANY) for b in blocks for sh, dt in shapes[b]]
    scratch = [
        pltpu.VMEM((2,) + weights[0].shape, BF),
        pltpu.VMEM((len(blocks),) + weights[1].shape, BF),
        pltpu.VMEM((ff, width), BF), pltpu.VMEM((2, rows, width), BF),
        pltpu.VMEM((rows, width), F32), pltpu.VMEM((rows, rows), F32),
        pltpu.SemaphoreType.DMA((64,))]
    for b in range(2):
        scratch += [pltpu.VMEM(sh, dt) for sh, dt in shapes[b]]
    res, sent = run(
        body, [(src, SMEM), (x, VMEM), (seg[:, None], VMEM), (seg[None, :], VMEM), (small, VMEM),
               (down, ANY)]
        + weight_ins(weights), outs, pieces, scratch, "forward", 60)
    saved = []
    for b in blocks:
        saved.append(res[: len(shapes[b])])
        res = res[len(shapes[b]) :]
    return saved, sent


def backward(dy, saved, layer, src, weights, small, down, adapt, stacks, through=None):
    rows, width = dy.shape
    ff = weights[0].shape[1]
    n_w = len(weight_ins(weights))
    blocks = (2 * layer + 1, 2 * layer)
    head = width // HEADS

    def body(ins, outs, stack_refs, scratch):
        src_ref, dy_ref, small_ref, down_ref = ins[:4]
        wts = (ins[4], ins[5], ins[6 : 4 + n_w])
        rest = ins[4 + n_w :]
        n_f = len(saved[blocks[0]])
        if through is not None:
            *rest, through_ref = rest
            *scratch, through_v = scratch
        in_f, in_a = rest[:n_f], rest[n_f:]
        slabs, packs, down_v, acc, db, dpt, grads, dx_v, dc_v, dqkv, dy_v, sems = scratch[:12]
        buf_f, buf_a = scratch[12 : 12 + n_f], scratch[12 + n_f :]
        sent, grads_out = stack_refs[0], stack_refs[1:]
        copies = Copies(sems)
        b = blocks[0]
        copies.start("dy", (dy_ref, dy_v))
        copies.start("post", *zip(in_f[1:], buf_f[1:]))
        load_pack(copies, "post", src_ref, b, wts, packs.at[0])
        copies.start("main", (down_ref.at[layer], down_v), (in_f[0], buf_f[0]))
        load_slab(copies, "main", src_ref, b, wts, slabs.at[0])
        load_pack(copies, "post_a", src_ref, b - 1, wts, packs.at[1])
        copies.start("post_a", *zip(in_a[3:], buf_a[3:]))
        load_slab(copies, "slab_a", src_ref, b - 1, wts, slabs.at[1])
        copies.start("main_a", *zip(in_a[:3], buf_a[:3]))

        if through is not None:
            copies.start("through", (through_ref, through_v))
        copies.wait("dy", "post")
        post_backward(packs.at[0], small_ref.at[src_ref[b, GROUP]], dy_v, buf_f[1:], acc, db, grads.at[0], dpt, adapt)
        send_grads(copies, "grads", grads.at[0], src_ref[b, GROUP], grads_out)
        copies.wait("main")
        ffn_branch_back(db, slabs.at[0], down_v, buf_f[0], acc)
        dx_v[...] = acc[...].astype(BF)
        send_rows(copies, "rows", dx_v, b, src_ref[b, GROUP + 1], sent)

        if through is not None:
            copies.wait("through")
            copies.start("through", (through_v, outs[-1]))
        b = blocks[1]
        copies.wait("post_a")
        qkv, ctx, probs = buf_a[:3]
        post_backward(packs.at[1], small_ref.at[src_ref[b, GROUP]], dx_v, buf_a[3:], acc, db, grads.at[1], dpt, adapt)
        send_grads(copies, "grads", grads.at[1], src_ref[b, GROUP], grads_out)
        copies.wait("slab_a")
        slab = slabs.at[1]
        by_columns(dc_v, width, lambda cols, j: dot_t(db[...], slab[cols, 3 * width :]))
        copies.wait("main_a")
        attend_back(qkv, ctx, dc_v, probs, dqkv)
        by_columns(dy_v, width,
                   lambda cols, j: acc[:, cols] + dot_t(dqkv[...], slab[cols, : 3 * width]))
        send_rows(copies, "rows", dy_v, b, src_ref[b, GROUP + 1], sent)
        if layer > 0:
            copies.start("dx", (dy_v, outs[0]))
        copies.wait_all()

    outs = [] if layer == 0 else [(like((rows, width)), ANY)]
    scratch = [
        pltpu.VMEM((2,) + weights[0].shape, BF), pltpu.VMEM((2,) + weights[1].shape, BF),
        pltpu.VMEM((ff, width), BF), pltpu.VMEM((rows, width), F32), pltpu.VMEM((rows, width), BF),
        pltpu.VMEM((128, rows), BF), pltpu.VMEM((2, 2 * adapt + EXTRA, width), BF),
        pltpu.VMEM((rows, width), BF), pltpu.VMEM((rows, width), BF),
        pltpu.VMEM((rows, 3 * width), BF), pltpu.VMEM((rows, width), BF),
        pltpu.SemaphoreType.DMA((48,))]
    for b in blocks:
        scratch += [pltpu.VMEM(x.shape, x.dtype) for x in saved[b]]
    passed = []
    if through is not None:
        passed = [(through, ANY)]
        outs.append((like(through.shape), ANY))
        scratch.append(pltpu.VMEM(through.shape, BF))
    res, stacks = run(
        body, [(src, SMEM), (dy, ANY), (small, VMEM), (down, ANY)] + weight_ins(weights)
        + [(x, ANY) for b in blocks for x in saved[b]] + passed,
        outs, stacks, scratch, "backward", 30)
    return res[0], stacks


def per_device(tokens, cotangent, segment_ids, slabs, ffn_down,
               ad_down, ad_down_bias, ad_up, ad_up_bias, ln_gain, ln_bias):
    n_section, n_group = lax.axis_size("section"), lax.axis_size("group")
    s, group, core = (lax.axis_index(name) for name in ("section", "group", "core"))
    n_micro, rows_dev, width = tokens.shape
    adapt = ad_down.shape[2]
    sections = range(n_section)

    def sect(x, apart):
        return lax.ppermute(x, "section", [(i, i ^ apart) for i in sections])

    def peer(x):
        return lax.ppermute(x, "core", [(0, 1), (1, 0)])

    def by_core(x, apart):
        pairs = [(i * GROUP + c, (i ^ apart[c]) * GROUP + c) for i in sections for c in range(GROUP)]
        return lax.ppermute(x, ("section", "core"), pairs)

    slab = slabs[0]
    half = slab.shape[0] // GROUP
    mats = jnp.concatenate([ad_down[0].T, ad_up[0]], axis=0).astype(BF)
    own_pack = jnp.concatenate([mats[i : i + EXTRA] for i in range(0, 2 * adapt, EXTRA)], axis=1)
    own_small = jnp.concatenate([jnp.pad(ad_down_bias, ((0, 0), (0, width - adapt))), ad_up_bias,
                                 ln_gain, ln_bias, jnp.zeros((4, width), F32)], axis=0)
    small = [own_small] + [sect(own_small, d) for d in range(1, n_section)]
    size = own_pack.shape[0] // GROUP
    given = jnp.concatenate([lax.dynamic_slice_in_dim(slab, core * half, half, 0),
                             lax.dynamic_slice_in_dim(own_pack, core * size, size, 0)], axis=0)
    second = by_core(given, (2, 1))
    first = by_core(given, (1, 2))
    second, *small = lax.optimization_barrier((second, *small))
    third = by_core(second, (1, 2))
    bufs = [first, second, third, peer(first), peer(second), peer(third)]
    small = jnp.stack(small)

    own_micro = s * GROUP + core
    peer_micro = s * GROUP + 1 - core

    def gather_item(x):
        mine = lax.dynamic_index_in_dim(x, own_micro, 0, keepdims=False)
        given = lax.dynamic_index_in_dim(x, peer_micro, 0, keepdims=False)
        return jnp.concatenate([mine, peer(given)], axis=0)

    hidden = gather_item(tokens)
    cot = gather_item(cotangent)
    item_start = group * GROUP * rows_dev
    seg = jnp.concatenate([
        lax.dynamic_slice(segment_ids, (own_micro, item_start + c * rows_dev), (1, rows_dev))[0]
        for c in (core, 1 - core)])

    def source(b):
        d = s ^ b
        at = []
        for h in range(GROUP):
            i = jnp.where(d == 3, 3, jnp.where((d == 1) == (h == 0), 1, 2))
            at.append(jnp.where(d == 0, 0, jnp.where(core == h, i, i + 3)))
        return jnp.stack(at + [d, core]).astype(jnp.int32)

    src = jnp.stack([source(b) for b in sections])
    weights = (slab, own_pack, bufs)

    def to_owners(x):
        return lax.all_to_all(x, ("section", "core"), 0, 0, tiled=True)

    rows = (like((n_section * GROUP, rows_dev, width)),)
    saved, sent = forward(hidden, seg, src, weights, small, ffn_down, adapt, rows)
    block_outputs = to_owners(sent[0])
    stacks = rows + tuple([like((2 * adapt + EXTRA, width))] * n_section)
    grad, stacks = backward(cot, saved, 1, src, weights, small, ffn_down, adapt, stacks)
    block_outputs, stacks = backward(grad, saved, 0, src, weights, small, ffn_down, adapt, stacks,
                                     block_outputs)
    total = stacks[1].astype(F32)
    for d in range(1, n_section):
        total = total + sect(stacks[1 + d], d).astype(F32)
    total, leaving = lax.optimization_barrier((total.astype(BF), stacks[0]))
    input_grads = to_owners(leaving)
    total = (total.astype(F32) + peer(total).astype(F32)).astype(BF)
    apart = 1
    while apart < n_group:
        other = lax.ppermute(total, "group", [(i, i ^ apart) for i in range(n_group)])
        total = (total.astype(F32) + other.astype(F32)).astype(BF)
        apart *= 2
    total = total.astype(F32)
    return (block_outputs[None], input_grads[None], total[:adapt].T[None],
            total[2 * adapt + 3, :adapt][None], total[adapt : 2 * adapt][None],
            total[2 * adapt][None], total[2 * adapt + 1][None], total[2 * adapt + 2][None])


def solution(mesh):
    n_section, n_rows = mesh.devices.shape
    cores = Mesh(mesh.devices.reshape(n_section, n_rows // GROUP, GROUP),
                 ("section", "group", "core"))
    rows = ("group", "core")
    in_specs = (
        P(None, rows, None), P(None, rows, None), P(), P("section", None, None), P(),
        P("section", None, None), P("section", None), P("section", None, None),
        P("section", None), P("section", None), P("section", None),
    )
    out_specs = (
        P("section", None, rows, None), P("section", None, rows, None),
        P("section", None, None), P("section", None), P("section", None, None),
        P("section", None), P("section", None), P("section", None),
    )
    return jax.shard_map(
        per_device, mesh=cores, in_specs=in_specs, out_specs=out_specs, check_vma=False
    )
```

```python
import jax
import jax.numpy as jnp
from jax import lax
from jax.experimental import pallas as pl
from jax.experimental.pallas import tpu as pltpu
from jax.sharding import Mesh, PartitionSpec as P

HEADS = 12
GROUP = 2
PARTS = 4
EXTRA = 32
COST = 1e8
BF = jnp.bfloat16
F32 = jnp.float32
VMEM = pl.BlockSpec(memory_space=pltpu.VMEM)
ANY = pl.BlockSpec(memory_space=pl.ANY)
SMEM = pl.BlockSpec(memory_space=pltpu.SMEM)
LIMIT = 56 * 1024 * 1024


def dot(left, right):
    return jnp.dot(left, right, preferred_element_type=F32)


def dot_t(left, right):
    return lax.dot_general(left, right, (((1,), (1,)), ((), ())), preferred_element_type=F32)


def gelu_pair(x):
    size = jnp.abs(x)
    base = 1.0 + 0.23164188 * size
    t = 1.0 / base
    poly = 0.127414796 + t * (-0.142248368 + t * (0.710706871 + t * (
        -0.726576014 + t * 0.530702715)))
    bell = jnp.exp2(-0.7213475204444817 * (x * x))
    tail = (t * poly) * bell
    phi = jnp.where(x < 0, tail, 1.0 - tail)
    return x * phi, phi + x * (0.3989422804014327 * bell)


def like(shape, dtype=BF):
    return jax.ShapeDtypeStruct(shape, dtype)


def run(body, ins, outs, stacks, scratch, name, micros, nbytes=0):
    ins, outs = list(ins), list(outs)
    made = [isinstance(x, jax.ShapeDtypeStruct) for x in stacks]
    aliases = {}
    kept = 0
    for i, stack in enumerate(stacks):
        if not made[i]:
            aliases[len(ins) + kept] = len(outs) + i
            kept += 1
    arrays = [a for a, _ in ins] + [x for x, m in zip(stacks, made) if not m]
    specs = [sp for _, sp in ins] + [ANY] * kept
    n_in, n_out, n_stack = len(ins), len(outs), len(stacks)

    def wrapped(*refs):
        got_in = refs[:n_in]
        rest = refs[n_in + kept :]
        body(got_in, rest[:n_out], rest[n_out : n_out + n_stack], rest[n_out + n_stack :])

    res = pl.pallas_call(
        wrapped,
        out_shape=[sh for sh, _ in outs] + [like(x.shape, x.dtype) for x in stacks],
        in_specs=specs,
        out_specs=[sp for _, sp in outs] + [ANY] * n_stack,
        scratch_shapes=scratch,
        name=name,
        input_output_aliases=aliases,
        cost_estimate=pl.CostEstimate(flops=int(micros * COST), bytes_accessed=nbytes,
                                      transcendentals=0),
        compiler_params=pltpu.CompilerParams(vmem_limit_bytes=LIMIT),
    )(*arrays)
    return tuple(res[:n_out]), tuple(res[n_out:])


class Copies:
    def __init__(self, sems):
        self.sems, self.used, self.waits = sems, 0, {}

    def sem(self):
        self.used += 1
        return self.sems.at[self.used - 1]

    def start(self, name, *pairs):
        for source, target in pairs:
            copy = pltpu.make_async_copy(source, target, self.sem())
            copy.start()
            self.waits.setdefault(name, []).append(copy.wait)

    def later(self, name, source, target, sem):
        self.waits.setdefault(name, []).append(pltpu.make_async_copy(source, target, sem).wait)

    def wait(self, *names):
        for name in names:
            for wait in self.waits.pop(name, []):
                wait()

    def wait_all(self):
        self.wait(*list(self.waits))


def load_slab(copies, name, src, block, weights, slab_v, columns):
    own, own_pack, bufs = weights
    rows = own.shape[0] // GROUP
    sem = copies.sem()
    for h in range(GROUP):
        at = pl.ds(h * rows, rows)

        @pl.when(src[block, h] == 0)
        def _():
            pltpu.make_async_copy(own.at[at, columns], slab_v.at[at, columns], sem).start()

        for i, buf in enumerate(bufs):
            @pl.when(src[block, h] == i + 1)
            def _():
                pltpu.make_async_copy(buf.at[pl.ds(0, rows), columns], slab_v.at[at, columns],
                                      sem).start()
    copies.later(name, own.at[:, columns], slab_v.at[:, columns], sem)


def load_pack(copies, name, src, block, weights, pack_v):
    own, own_pack, bufs = weights
    rows = own.shape[0] // GROUP
    size = own_pack.shape[0] // GROUP
    sem = copies.sem()
    for h in range(GROUP):
        at = pl.ds(h * size, size)

        @pl.when(src[block, h] == 0)
        def _():
            pltpu.make_async_copy(own_pack.at[at], pack_v.at[at], sem).start()

        for i, buf in enumerate(bufs):
            @pl.when(src[block, h] == i + 1)
            def _():
                pltpu.make_async_copy(buf.at[pl.ds(rows, size)], pack_v.at[at], sem).start()
    copies.later(name, own_pack, pack_v, sem)


def send_grads(copies, name, value_ref, apart, outs):
    sem = copies.sem()
    for d, out in enumerate(outs):
        @pl.when(apart == d)
        def _():
            pltpu.make_async_copy(value_ref, out, sem).start()
    copies.later(name, value_ref, outs[0], sem)


def send_rows(copies, name, value_ref, block, core, out):
    half = value_ref.shape[0] // GROUP
    for i in range(GROUP):
        to = GROUP * block + (core if i == 0 else GROUP - 1 - core)
        copies.start(name, (value_ref.at[pl.ds(i * half, half)], out.at[to]))


def adapters(pack, width, adapt):
    rows = [pack[:, i * width : (i + 1) * width] for i in range(2 * adapt // EXTRA)]
    zeros = jnp.zeros((128 - adapt, width), BF)
    per = adapt // EXTRA
    down_t = jnp.concatenate(rows[:per] + [zeros], axis=0)
    up = jnp.concatenate(rows[per:] + [zeros], axis=0)
    return down_t, up


def post_forward(pack, small, x_ref, b_ref, y_ref, saved, adapt):
    low_ref, ut_ref, slope_ref, zhat_ref, rstd_ref = saved
    rows, width = x_ref.shape
    down_t, up = adapters(pack, width, adapt)
    down_bias, up_bias, gain, bias = [small[i : i + 1, :] for i in range(4)]
    step = 512

    def body(i, carry):
        at = pl.ds(pl.multiple_of(i * step, step), step)
        branch = b_ref[at, :]
        low = branch.astype(BF)
        low_ref[at, :] = low
        pre = dot_t(low, down_t) + down_bias[:, :128]
        inner, slope = gelu_pair(pre)
        slope_ref[at, :] = slope
        ut_ref[:, at] = inner.T.astype(BF)
        mixed = x_ref[at, :].astype(F32) + branch + dot(inner.astype(BF), up) + up_bias
        center = mixed - jnp.mean(mixed, axis=-1, keepdims=True)
        rstd = lax.rsqrt(jnp.mean(center * center, axis=-1, keepdims=True) + 1e-05)
        zhat = center * rstd
        y_ref[at, :] = (zhat * gain + bias).astype(BF)
        zhat_ref[at, :] = zhat.astype(BF)
        rstd_ref[at, :] = jnp.broadcast_to(rstd, (step, 128))
        return carry

    lax.fori_loop(0, rows // step, body, 0)


def post_backward(pack, small, dy_ref, saved, dz_ref, db_ref, grads_ref, dpt_ref, adapt):
    low_ref, ut_ref, slope_ref, zhat_ref, rstd_ref = saved
    rows, width = dy_ref.shape
    down_t, up = adapters(pack, width, adapt)
    gain = small[2:3, :]
    step = 512

    def fold(v):
        return jnp.sum(v.reshape(v.shape[0] // 8, 8, v.shape[1]), axis=0)

    def body(i, carry):
        s_bias, s_gain, s_upb, s_downb = carry
        at = pl.ds(pl.multiple_of(i * step, step), step)
        d_out = dy_ref[at, :].astype(F32)
        zhat = zhat_ref[at, :].astype(F32)
        s_bias = s_bias + fold(d_out)
        s_gain = s_gain + fold(d_out * zhat)
        dz = d_out * gain
        dz = rstd_ref[at, :1] * (dz - jnp.mean(dz, axis=-1, keepdims=True)
                                 - zhat * jnp.mean(dz * zhat, axis=-1, keepdims=True))
        s_upb = s_upb + fold(dz)
        low = dz.astype(BF)
        db_ref[at, :] = low
        d_pre = dot_t(low, up) * slope_ref[at, :]
        s_downb = s_downb + fold(d_pre)
        dpt_ref[:, at] = d_pre.T.astype(BF)
        dz_ref[at, :] = dz
        return s_bias, s_gain, s_upb, s_downb

    zero = jnp.zeros((8, width), F32)
    s_bias, s_gain, s_upb, s_downb = lax.fori_loop(
        0, rows // step, body, (zero, zero, zero, jnp.zeros((8, 128), F32)))
    g_down = dot(dpt_ref[...], low_ref[...])
    g_up = dot(ut_ref[...], db_ref[...])
    grads_ref[0:adapt, :] = g_down[:adapt].astype(BF)
    grads_ref[adapt : 2 * adapt, :] = g_up[:adapt].astype(BF)
    tail = jnp.concatenate(
        [jnp.sum(v, axis=0, keepdims=True) for v in (s_upb, s_gain, s_bias)]
        + [jnp.concatenate([jnp.sum(s_downb, axis=0, keepdims=True),
                            jnp.zeros((1, width - 128), F32)], axis=1),
           jnp.zeros((EXTRA - 4, width), F32)], axis=0)
    grads_ref[2 * adapt :, :] = tail.astype(BF)

    def body2(i, carry):
        at = pl.ds(pl.multiple_of(i * step, step), step)
        d_pre = dpt_ref[:, at].astype(F32).T.astype(BF)
        db_ref[at, :] = (dz_ref[at, :] + dot(d_pre, down_t)).astype(BF)
        return carry

    lax.fori_loop(0, rows // step, body2, 0)


def tile(i, size):
    return pl.ds(pl.multiple_of(i * size, size), size)


def part_of(size, i):
    return pl.ds(i * (size // PARTS), size // PARTS)


def tiles(size, step, ready):
    for j in range(size // step):
        if j * step % (size // PARTS) == 0:
            ready(j * step // (size // PARTS))
        yield slice(j * step, (j + 1) * step)


def ffn_branch(x_ref, slab, down, slope_ref, acc, ready, step=256):
    acc[...] = jnp.zeros_like(acc)
    act, before = None, None
    for cols in tiles(slab.shape[1], step, ready):
        values, slope = gelu_pair(dot(x_ref[...], slab[:, cols]))
        slope_ref[:, cols] = slope.astype(BF)
        if act is not None:
            acc[...] += dot(act, down[before, :])
        act, before = values.astype(BF), cols
    acc[...] += dot(act, down[before, :])


def ffn_branch_back(db, slab, down, slope_ref, acc, ready, step=256):
    df, before = None, None
    for cols in tiles(slab.shape[1], step, ready):
        dg = dot_t(db[...], down[cols, :])
        if df is not None:
            acc[...] += dot_t(df, slab[:, before])
        df, before = (dg * slope_ref[:, cols].astype(F32)).astype(BF), cols
    acc[...] += dot_t(df, slab[:, before])


def project(x_ref, slab, qkv_ref, ready, step=256):
    width = x_ref.shape[1]
    for cols in tiles(slab.shape[1], step, ready):
        if cols.start < 3 * width:
            value = dot(x_ref[...], slab[:, cols])
            if cols.start < width:
                value = value * (width // HEADS) ** -0.5
            qkv_ref[:, cols] = value.astype(BF)


def attend(qkv_ref, bias_v, p_v, c_ref, p_out, p_sem):
    rows, width = c_ref.shape
    head = width // HEADS
    lower = lax.broadcasted_iota(jnp.int32, (rows, 2 * head), 1) < head

    def body(i, carry):
        def part(n):
            return qkv_ref[:, pl.ds(pl.multiple_of(n * width + i * 2 * head, 2 * head), 2 * head)]

        q, k, v = part(0), part(1), part(2)
        parts = []
        for h in range(2):
            q_h = jnp.where(lower == (h == 0), q, jnp.zeros_like(q))
            s = dot_t(q_h, k) + bias_v[...]
            e = jnp.exp(s - jnp.max(s, axis=-1, keepdims=True))
            p = (e * (1.0 / jnp.sum(e, axis=-1, keepdims=True))).astype(BF)
            p_v[2 * i + h] = p
            pltpu.make_async_copy(p_v.at[2 * i + h], p_out.at[2 * i + h], p_sem).start()
            parts.append(dot(p, v))
        c_ref[:, tile(i, 2 * head)] = jnp.where(lower, parts[0], parts[1]).astype(BF)
        return carry

    lax.fori_loop(0, HEADS // 2, body, 0, unroll=6)


def attend_back(qkv_ref, c_ref, dc_ref, p_v, dqkv):
    rows, width = c_ref.shape
    head = width // HEADS
    lower = lax.broadcasted_iota(jnp.int32, (rows, 2 * head), 1) < head

    def body(i, carry):
        def cols(n):
            return pl.ds(pl.multiple_of(n * width + i * 2 * head, 2 * head), 2 * head)

        q, k, v = qkv_ref[:, cols(0)], qkv_ref[:, cols(1)], qkv_ref[:, cols(2)]
        dc = dc_ref[:, cols(0)]
        dc_wide = dc.astype(F32)
        prod = dc_wide * c_ref[:, cols(0)].astype(F32)
        q_t = q.astype(F32).T.astype(BF)
        dc_t = dc_wide.T.astype(BF)
        dq, dk, dv = [], [], []
        for h in range(2):
            mine = lower == (h == 0)
            p = p_v[2 * i + h]
            delta = jnp.sum(jnp.where(mine, prod, 0.0), axis=-1, keepdims=True)
            dp = dot_t(jnp.where(mine, dc, jnp.zeros_like(dc)), v)
            ds = (p.astype(F32) * (dp - delta)).astype(BF)
            dq.append(dot(ds, k))
            dk.append(dot(q_t[h * head : (h + 1) * head], ds))
            dv.append(dot(dc_t[h * head : (h + 1) * head], p))
        dqkv[:, cols(0)] = (jnp.where(lower, dq[0], dq[1]) * head ** -0.5).astype(BF)
        dqkv[:, cols(1)] = jnp.concatenate(dk, axis=0).T.astype(BF)
        dqkv[:, cols(2)] = jnp.concatenate(dv, axis=0).T.astype(BF)
        return carry

    lax.fori_loop(0, HEADS // 2, body, 0, unroll=3)


def by_columns(target, value, step=256):
    for j in range(target.shape[1] // step):
        cols = slice(j * step, (j + 1) * step)
        target[:, cols] = value(cols).astype(target.dtype)


def post_saved(rows, width):
    return [((rows, width), BF), ((128, rows), BF), ((rows, 128), F32), ((rows, width), BF),
            ((rows, 128), F32)]


def block_saved(block, rows, width, ff):
    if block % 2 == 0:
        first = [((rows, 3 * width), BF), ((rows, width), BF), ((HEADS, rows, rows), BF)]
    else:
        first = [((rows, ff), BF)]
    return first + post_saved(rows, width)


def weight_ins(weights):
    own, own_pack, bufs = weights
    return [(own, ANY), (own_pack, ANY)] + [(x, ANY) for x in bufs]


def forward(x, seg, src, weights, small, down, adapt, pieces):
    rows, width = x.shape
    ff = weights[0].shape[1]
    blocks = range(2 * down.shape[0])
    n_w = len(weight_ins(weights))
    shapes = [block_saved(b, rows, width, ff) for b in blocks]

    def body(ins, outs, sent, scratch):
        src_ref, x_ref, segc_ref, segr_ref, small_ref, down_ref = ins[:6]
        wts = (ins[6], ins[7], ins[8 : 6 + n_w])
        saved_out, rest = [], outs
        for b in blocks:
            saved_out.append(rest[: len(shapes[b])])
            rest = rest[len(shapes[b]) :]
        slabs, packs, down_v, y_v, acc, bias_v, sems = scratch[:7]
        kept = [scratch[7:15], scratch[15:21]]
        copies = Copies(sems)

        def slab_parts(b):
            for i in range(PARTS):
                load_slab(copies, "slab%d%d" % (b, i), src_ref, b, wts, slabs.at[b % 2],
                          part_of(ff, i))

        def down_parts(layer):
            for i in range(PARTS):
                rows_at = part_of(ff, i)
                copies.start("down%d%d" % (layer, i),
                             (down_ref.at[layer, rows_at], down_v.at[rows_at]))

        slab_parts(0)
        for b in blocks:
            load_pack(copies, "pack", src_ref, b, wts, packs.at[b])
        bias_v[...] = jnp.where(segc_ref[...] == segr_ref[...], 0.0, -1e30)
        hidden = x_ref
        for b in blocks:
            slab = slabs.at[b % 2]
            copies.wait("saved%d" % (b - 2))
            mine = kept[b % 2]
            y = y_v.at[b % 2]
            if b % 2 == 0:
                qkv, ctx, probs = mine[:3]
                project(hidden, slab, qkv, lambda i: copies.wait("slab%d%d" % (b, i)))
                copies.start("saved%d" % b, (qkv, saved_out[b][0]))
                if b == 0:
                    slab_parts(1)
                    down_parts(0)
                p_sem = copies.sem()
                attend(qkv, bias_v, probs, ctx, saved_out[b][2], p_sem)
                copies.later("saved%d" % b, probs, saved_out[b][2], p_sem)
                copies.start("saved%d" % b, (ctx, saved_out[b][1]))
                by_columns(acc, lambda cols: dot(
                    ctx[...], slab[:, 3 * width + cols.start : 3 * width + cols.stop]))
                post = mine[3:]
            else:
                ffn_branch(hidden, slab, down_v, mine[0], acc, lambda i: copies.wait(
                    "slab%d%d" % (b, i), "down%d%d" % (b // 2, i)))
                copies.start("saved%d" % b, (mine[0], saved_out[b][0]))
                if b + 2 in blocks:
                    down_parts(b // 2 + 1)
                post = mine[1:]
            if b + 2 in blocks:
                slab_parts(b + 2)
            copies.wait("pack", "rows%d" % (b - 2))
            post_forward(packs.at[b], small_ref.at[src_ref[b, GROUP]], hidden, acc, y, post, adapt)
            send_rows(copies, "rows%d" % b, y, b, src_ref[b, GROUP + 1], sent[0])
            copies.start("saved%d" % b, *zip(post, saved_out[b][-len(post) :]))
            hidden = y
        copies.wait_all()

    outs = [(like(sh, dt), ANY) for b in blocks for sh, dt in shapes[b]]
    scratch = [
        pltpu.VMEM((2,) + weights[0].shape, BF),
        pltpu.VMEM((len(blocks),) + weights[1].shape, BF),
        pltpu.VMEM((ff, width), BF), pltpu.VMEM((2, rows, width), BF),
        pltpu.VMEM((rows, width), F32), pltpu.VMEM((rows, rows), F32),
        pltpu.SemaphoreType.DMA((96,))]
    for b in range(2):
        scratch += [pltpu.VMEM(sh, dt) for sh, dt in shapes[b]]
    res, sent = run(
        body, [(src, SMEM), (x, VMEM), (seg[:, None], VMEM), (seg[None, :], VMEM), (small, VMEM),
               (down, ANY)]
        + weight_ins(weights), outs, pieces, scratch, "forward", 60)
    saved = []
    for b in blocks:
        saved.append(res[: len(shapes[b])])
        res = res[len(shapes[b]) :]
    return saved, sent


def backward(dy, saved, layer, src, weights, small, down, adapt, stacks):
    rows, width = dy.shape
    ff = weights[0].shape[1]
    n_w = len(weight_ins(weights))
    blocks = (2 * layer + 1, 2 * layer)
    head = width // HEADS

    def body(ins, outs, stack_refs, scratch):
        src_ref, dy_ref, small_ref, down_ref = ins[:4]
        wts = (ins[4], ins[5], ins[6 : 4 + n_w])
        rest = ins[4 + n_w :]
        n_f = len(saved[blocks[0]])
        in_f, in_a = rest[:n_f], rest[n_f:]
        slabs, packs, down_v, acc, db, dpt, grads, dx_v, dc_v, dqkv, dy_v, sems = scratch[:12]
        buf_f, buf_a = scratch[12 : 12 + n_f], scratch[12 + n_f :]
        sent, grads_out = stack_refs[0], stack_refs[1:]
        copies = Copies(sems)
        b = blocks[0]
        copies.start("dy", (dy_ref, dy_v))
        copies.start("post", *zip(in_f[1:], buf_f[1:]))
        load_pack(copies, "post", src_ref, b, wts, packs.at[0])
        for i in range(PARTS):
            at, name = part_of(ff, i), "ffn%d" % i
            copies.start(name, (down_ref.at[layer, at], down_v.at[at]),
                         (in_f[0].at[:, at], buf_f[0].at[:, at]))
            load_slab(copies, name, src_ref, b, wts, slabs.at[0], at)
        copies.wait("dy", "post")
        post_backward(packs.at[0], small_ref.at[src_ref[b, GROUP]], dy_v, buf_f[1:], acc, db,
                      grads.at[0], dpt, adapt)
        send_grads(copies, "grads", grads.at[0], src_ref[b, GROUP], grads_out)
        load_pack(copies, "post_a", src_ref, b - 1, wts, packs.at[1])
        copies.start("post_a", *zip(in_a[3:], buf_a[3:]))
        for i in reversed(range(PARTS)):
            load_slab(copies, "slab_a", src_ref, b - 1, wts, slabs.at[1], part_of(ff, i))
        copies.start("main_a", *zip(in_a[:3], buf_a[:3]))
        ffn_branch_back(db, slabs.at[0], down_v, buf_f[0], acc,
                        lambda i: copies.wait("ffn%d" % i))
        dx_v[...] = acc[...].astype(BF)
        send_rows(copies, "rows", dx_v, b, src_ref[b, GROUP + 1], sent)

        b = blocks[1]
        copies.wait("post_a")
        qkv, ctx, probs = buf_a[:3]
        post_backward(packs.at[1], small_ref.at[src_ref[b, GROUP]], dx_v, buf_a[3:], acc, db,
                      grads.at[1], dpt, adapt)
        send_grads(copies, "grads", grads.at[1], src_ref[b, GROUP], grads_out)
        copies.wait("slab_a")
        slab = slabs.at[1]
        by_columns(dc_v, lambda cols: dot_t(db[...], slab[cols, 3 * width :]))
        copies.wait("main_a")
        attend_back(qkv, ctx, dc_v, probs, dqkv)
        by_columns(dy_v, lambda cols: acc[:, cols] + dot_t(dqkv[...], slab[cols, : 3 * width]))
        send_rows(copies, "rows", dy_v, b, src_ref[b, GROUP + 1], sent)
        if layer > 0:
            copies.start("dx", (dy_v, outs[0]))
        copies.wait_all()

    outs = [] if layer == 0 else [(like((rows, width)), ANY)]
    scratch = [
        pltpu.VMEM((2,) + weights[0].shape, BF), pltpu.VMEM((2,) + weights[1].shape, BF),
        pltpu.VMEM((ff, width), BF), pltpu.VMEM((rows, width), F32), pltpu.VMEM((rows, width), BF),
        pltpu.VMEM((128, rows), BF), pltpu.VMEM((2, 2 * adapt + EXTRA, width), BF),
        pltpu.VMEM((rows, width), BF), pltpu.VMEM((rows, width), BF),
        pltpu.VMEM((rows, 3 * width), BF), pltpu.VMEM((rows, width), BF),
        pltpu.SemaphoreType.DMA((64,))]
    for b in blocks:
        scratch += [pltpu.VMEM(x.shape, x.dtype) for x in saved[b]]
    res, stacks = run(
        body, [(src, SMEM), (dy, ANY), (small, VMEM), (down, ANY)] + weight_ins(weights)
        + [(x, ANY) for b in blocks for x in saved[b]],
        outs, stacks, scratch, "backward", 30)
    return (res[0] if res else None), stacks


def settle(x):
    def body(ins, outs, stack_refs, scratch):
        buf, sems = scratch
        loads = [pltpu.make_async_copy(ins[0].at[i], buf.at[i], sems.at[i])
                 for i in range(x.shape[0])]
        stores = [pltpu.make_async_copy(buf.at[i], outs[0].at[i], sems.at[i])
                  for i in range(x.shape[0])]
        for load in loads:
            load.start()
        for load, store in zip(loads, stores):
            load.wait()
            store.start()
        for store in stores:
            store.wait()

    res, _ = run(body, [(x, ANY)], [(like(x.shape), ANY)], [],
                 [pltpu.VMEM(x.shape, BF), pltpu.SemaphoreType.DMA((x.shape[0],))], "settle", 3)
    return res[0]


def per_device(tokens, cotangent, segment_ids, slabs, ffn_down,
               ad_down, ad_down_bias, ad_up, ad_up_bias, ln_gain, ln_bias):
    n_section, n_group = lax.axis_size("section"), lax.axis_size("group")
    s, group, core = (lax.axis_index(name) for name in ("section", "group", "core"))
    n_micro, rows_dev, width = tokens.shape
    adapt = ad_down.shape[2]
    sections = range(n_section)

    def sect(x, apart):
        return lax.ppermute(x, "section", [(i, i ^ apart) for i in sections])

    def peer(x):
        return lax.ppermute(x, "core", [(0, 1), (1, 0)])

    def by_core(x, apart):
        pairs = [(i * GROUP + c, (i ^ apart[c]) * GROUP + c) for i in sections for c in range(GROUP)]
        return lax.ppermute(x, ("section", "core"), pairs)

    slab = slabs[0]
    half = slab.shape[0] // GROUP
    mats = jnp.concatenate([ad_down[0].T, ad_up[0]], axis=0).astype(BF)
    own_pack = jnp.concatenate([mats[i : i + EXTRA] for i in range(0, 2 * adapt, EXTRA)], axis=1)
    own_small = jnp.concatenate([jnp.pad(ad_down_bias, ((0, 0), (0, width - adapt))), ad_up_bias,
                                 ln_gain, ln_bias, jnp.zeros((4, width), F32)], axis=0)
    small = [own_small] + [sect(own_small, d) for d in range(1, n_section)]
    size = own_pack.shape[0] // GROUP
    given = jnp.concatenate([lax.dynamic_slice_in_dim(slab, core * half, half, 0),
                             lax.dynamic_slice_in_dim(own_pack, core * size, size, 0)], axis=0)
    second = by_core(given, (2, 1))
    first = by_core(given, (1, 2))
    second, *small = lax.optimization_barrier((second, *small))
    third = by_core(second, (1, 2))
    bufs = [first, second, third, peer(first), peer(second), peer(third)]
    small = jnp.stack(small)

    own_micro = s * GROUP + core
    peer_micro = s * GROUP + 1 - core

    def gather_item(x):
        mine = lax.dynamic_index_in_dim(x, own_micro, 0, keepdims=False)
        given = lax.dynamic_index_in_dim(x, peer_micro, 0, keepdims=False)
        return jnp.concatenate([mine, peer(given)], axis=0)

    hidden = gather_item(tokens)
    cot = gather_item(cotangent)
    item_start = group * GROUP * rows_dev
    seg = jnp.concatenate([
        lax.dynamic_slice(segment_ids, (own_micro, item_start + c * rows_dev), (1, rows_dev))[0]
        for c in (core, 1 - core)])

    def source(b):
        d = s ^ b
        at = []
        for h in range(GROUP):
            i = jnp.where(d == 3, 3, jnp.where((d == 1) == (h == 0), 1, 2))
            at.append(jnp.where(d == 0, 0, jnp.where(core == h, i, i + 3)))
        return jnp.stack(at + [d, core]).astype(jnp.int32)

    src = jnp.stack([source(b) for b in sections])
    weights = (slab, own_pack, bufs)

    def to_owners(x):
        return lax.all_to_all(x, ("section", "core"), 0, 0, tiled=True)

    rows = (like((n_section * GROUP, rows_dev, width)),)
    saved, sent = forward(hidden, seg, src, weights, small, ffn_down, adapt, rows)
    block_outputs = to_owners(sent[0])
    stacks = rows + tuple([like((2 * adapt + EXTRA, width))] * n_section)
    grad, stacks = backward(cot, saved, 1, src, weights, small, ffn_down, adapt, stacks)
    _, stacks = backward(grad, saved, 0, src, weights, small, ffn_down, adapt, stacks)
    block_outputs, *stacks = lax.optimization_barrier((block_outputs, *stacks))
    block_outputs = settle(block_outputs)
    total = stacks[1].astype(F32)
    for d in range(1, n_section):
        total = total + sect(stacks[1 + d], d).astype(F32)
    total, leaving = lax.optimization_barrier((total.astype(BF), stacks[0]))
    input_grads = to_owners(leaving)
    total = (total.astype(F32) + peer(total).astype(F32)).astype(BF)
    apart = 1
    while apart < n_group:
        other = lax.ppermute(total, "group", [(i, i ^ apart) for i in range(n_group)])
        total = (total.astype(F32) + other.astype(F32)).astype(BF)
        apart *= 2
    total = total.astype(F32)
    return (block_outputs[None], input_grads[None], total[:adapt].T[None],
            total[2 * adapt + 3, :adapt][None], total[adapt : 2 * adapt][None],
            total[2 * adapt][None], total[2 * adapt + 1][None], total[2 * adapt + 2][None])


def solution(mesh):
    n_section, n_rows = mesh.devices.shape
    cores = Mesh(mesh.devices.reshape(n_section, n_rows // GROUP, GROUP),
                 ("section", "group", "core"))
    rows = ("group", "core")
    in_specs = (
        P(None, rows, None), P(None, rows, None), P(), P("section", None, None), P(),
        P("section", None, None), P("section", None), P("section", None, None),
        P("section", None), P("section", None), P("section", None),
    )
    out_specs = (
        P("section", None, rows, None), P("section", None, rows, None),
        P("section", None, None), P("section", None), P("section", None, None),
        P("section", None), P("section", None), P("section", None),
    )
    return jax.shard_map(
        per_device, mesh=cores, in_specs=in_specs, out_specs=out_specs, check_vma=False
    )
```

```python
import jax
import jax.numpy as jnp
from jax import lax
from jax.experimental import pallas as pl
from jax.experimental.pallas import tpu as pltpu
from jax.sharding import Mesh, PartitionSpec as P

HEADS = 12
GROUP = 2
PARTS = 4
EXTRA = 32
COST = 1e8
BF = jnp.bfloat16
F32 = jnp.float32
VMEM = pl.BlockSpec(memory_space=pltpu.VMEM)
ANY = pl.BlockSpec(memory_space=pl.ANY)
SMEM = pl.BlockSpec(memory_space=pltpu.SMEM)
LIMIT = 56 * 1024 * 1024


def dot(left, right):
    return jnp.dot(left, right, preferred_element_type=F32)


def dot_t(left, right):
    return lax.dot_general(left, right, (((1,), (1,)), ((), ())), preferred_element_type=F32)


def gelu_pair(x):
    size = jnp.abs(x)
    base = 1.0 + 0.23164188 * size
    t = 1.0 / base
    poly = 0.127414796 + t * (-0.142248368 + t * (0.710706871 + t * (
        -0.726576014 + t * 0.530702715)))
    bell = jnp.exp2(-0.7213475204444817 * (x * x))
    tail = (t * poly) * bell
    phi = jnp.where(x < 0, tail, 1.0 - tail)
    return x * phi, phi + x * (0.3989422804014327 * bell)


def like(shape, dtype=BF):
    return jax.ShapeDtypeStruct(shape, dtype)


def run(body, ins, outs, scratch, name, micros):
    n_in, n_out = len(ins), len(outs)

    def wrapped(*refs):
        body(refs[:n_in], refs[n_in : n_in + n_out], refs[n_in + n_out :])

    return pl.pallas_call(
        wrapped,
        out_shape=[shape for shape, _ in outs],
        in_specs=[spec for _, spec in ins],
        out_specs=[spec for _, spec in outs],
        scratch_shapes=scratch,
        name=name,
        cost_estimate=pl.CostEstimate(flops=int(micros * COST), bytes_accessed=0, transcendentals=0),
        compiler_params=pltpu.CompilerParams(vmem_limit_bytes=LIMIT),
    )(*[array for array, _ in ins])


class Group:
    def __init__(self, sems, count):
        self.sems, self.first, self.pairs = sems, sems.used, []
        sems.used += count

    def start(self, *pairs):
        for i, (source, target) in enumerate(pairs):
            pltpu.make_async_copy(source, target, self.sems.ref.at[self.first + i]).start()

    def wait(self, *pairs):
        for i, (source, target) in enumerate(pairs):
            pltpu.make_async_copy(source, target, self.sems.ref.at[self.first + i]).wait()


class Sems:
    def __init__(self, ref):
        self.ref, self.used = ref, 0

    def run(self, count):
        self.used += count
        return self.ref.at[pl.ds(self.used - count, count)]


def load_slab(sems, src, block, weights, slab_v):
    own, own_pack, bufs = weights
    rows = own.shape[0] // GROUP
    plane = src[block, GROUP + 2]
    for h in range(GROUP):
        for i, parts in enumerate([(own,)] + list(bufs)):
            size = rows // len(parts)

            @pl.when(src[block, h] == i)
            def _():
                for p in range(PARTS):
                    columns = pl.ds(p * (own.shape[1] // PARTS), own.shape[1] // PARTS)
                    for n, buf in enumerate(parts):
                        first = h * rows if i == 0 else 0
                        to = h * rows
                        if len(parts) > 1:
                            to += size * (plane if n == 0 else 1 - plane)
                        pltpu.make_async_copy(
                            buf.at[pl.ds(first, size), columns],
                            slab_v.at[pl.ds(pl.multiple_of(to, 64), size), columns],
                            sems.at[p]).start()


def slab_part(sems, weights, slab_v, p):
    own = weights[0]
    columns = part_of(own.shape[1], p)
    pltpu.make_async_copy(own.at[:, columns], slab_v.at[:, columns], sems.at[p]).wait()


def load_down(sems, down, layer, down_v):
    for p in range(PARTS):
        rows = pl.ds(p * (down_v.shape[0] // PARTS), down_v.shape[0] // PARTS)
        pltpu.make_async_copy(down.at[layer, rows], down_v.at[rows], sems.at[p]).start()


def down_part(sems, down, down_v, p):
    rows = part_of(down_v.shape[0], p)
    pltpu.make_async_copy(down.at[0, rows], down_v.at[rows], sems.at[p]).wait()


def load_pack(sem, src, block, weights, pack_v):
    own, own_pack, bufs = weights
    rows = own.shape[0] // GROUP
    size = own_pack.shape[0] // GROUP
    for h in range(GROUP):
        at = pl.ds(h * size, size)
        for i, parts in enumerate([(own_pack,)] + list(bufs)):
            buf = parts[0]
            first = h * size if i == 0 else rows // len(parts)

            @pl.when(src[block, h] == i)
            def _():
                pltpu.make_async_copy(buf.at[pl.ds(first, size)], pack_v.at[at], sem).start()


def send_grads(sem, value_ref, apart, outs):
    for d, out in enumerate(outs):
        @pl.when(apart == d)
        def _():
            pltpu.make_async_copy(value_ref, out, sem).start()


def row_copies(value_ref, block, core, out, sem):
    half = value_ref.shape[0] // GROUP
    return [pltpu.make_async_copy(
        value_ref.at[pl.ds(i * half, half)],
        out.at[GROUP * block + (core if i == 0 else GROUP - 1 - core)], sem) for i in range(GROUP)]


def adapters(pack, width, adapt):
    rows = [pack[:, i * width : (i + 1) * width] for i in range(2 * adapt // EXTRA)]
    zeros = jnp.zeros((128 - adapt, width), BF)
    per = adapt // EXTRA
    down_t = jnp.concatenate(rows[:per] + [zeros], axis=0)
    up = jnp.concatenate(rows[per:] + [zeros], axis=0)
    return down_t, up


def post_forward(pack, small, x_ref, b_ref, y_ref, saved, adapt):
    low_ref, ut_ref, slope_ref, zhat_ref, rstd_ref = saved
    rows, width = x_ref.shape
    down_t, up = adapters(pack, width, adapt)
    down_bias, up_bias, gain, bias = [small[i : i + 1, :] for i in range(4)]
    step = 512

    def body(i, carry):
        at = pl.ds(pl.multiple_of(i * step, step), step)
        branch = b_ref[at, :]
        low = branch.astype(BF)
        low_ref[at, :] = low
        pre = dot_t(low, down_t) + down_bias[:, :128]
        inner, slope = gelu_pair(pre)
        slope_ref[at, :] = slope
        ut_ref[:, at] = inner.T.astype(BF)
        mixed = x_ref[at, :].astype(F32) + branch + dot(inner.astype(BF), up) + up_bias
        center = mixed - jnp.mean(mixed, axis=-1, keepdims=True)
        rstd = lax.rsqrt(jnp.mean(center * center, axis=-1, keepdims=True) + 1e-05)
        zhat = center * rstd
        y_ref[at, :] = (zhat * gain + bias).astype(BF)
        zhat_ref[at, :] = zhat.astype(BF)
        rstd_ref[at, :] = jnp.broadcast_to(rstd, (step, 128))
        return carry

    lax.fori_loop(0, rows // step, body, 0)


def post_backward(pack, small, dy_ref, saved, dz_ref, db_ref, grads_ref, dpt_ref, adapt):
    low_ref, ut_ref, slope_ref, zhat_ref, rstd_ref = saved
    rows, width = dy_ref.shape
    down_t, up = adapters(pack, width, adapt)
    gain = small[2:3, :]
    step = 512

    def fold(v):
        return jnp.sum(v.reshape(v.shape[0] // 8, 8, v.shape[1]), axis=0)

    def body(i, carry):
        s_bias, s_gain, s_upb, s_downb = carry
        at = pl.ds(pl.multiple_of(i * step, step), step)
        d_out = dy_ref[at, :].astype(F32)
        zhat = zhat_ref[at, :].astype(F32)
        s_bias = s_bias + fold(d_out)
        s_gain = s_gain + fold(d_out * zhat)
        dz = d_out * gain
        dz = rstd_ref[at, :1] * (dz - jnp.mean(dz, axis=-1, keepdims=True)
                                 - zhat * jnp.mean(dz * zhat, axis=-1, keepdims=True))
        s_upb = s_upb + fold(dz)
        low = dz.astype(BF)
        db_ref[at, :] = low
        d_pre = dot_t(low, up) * slope_ref[at, :]
        s_downb = s_downb + fold(d_pre)
        dpt_ref[:, at] = d_pre.T.astype(BF)
        dz_ref[at, :] = dz
        return s_bias, s_gain, s_upb, s_downb

    zero = jnp.zeros((8, width), F32)
    s_bias, s_gain, s_upb, s_downb = lax.fori_loop(
        0, rows // step, body, (zero, zero, zero, jnp.zeros((8, 128), F32)))
    g_down = dot(dpt_ref[...], low_ref[...])
    g_up = dot(ut_ref[...], db_ref[...])
    grads_ref[0:adapt, :] = g_down[:adapt].astype(BF)
    grads_ref[adapt : 2 * adapt, :] = g_up[:adapt].astype(BF)
    tail = jnp.concatenate(
        [jnp.sum(v, axis=0, keepdims=True) for v in (s_upb, s_gain, s_bias)]
        + [jnp.concatenate([jnp.sum(s_downb, axis=0, keepdims=True),
                            jnp.zeros((1, width - 128), F32)], axis=1),
           jnp.zeros((EXTRA - 4, width), F32)], axis=0)
    grads_ref[2 * adapt :, :] = tail.astype(BF)

    def body2(i, carry):
        at = pl.ds(pl.multiple_of(i * step, step), step)
        d_pre = dpt_ref[:, at].astype(F32).T.astype(BF)
        db_ref[at, :] = (dz_ref[at, :] + dot(d_pre, down_t)).astype(BF)
        return carry

    lax.fori_loop(0, rows // step, body2, 0)


def tile(i, size):
    return pl.ds(pl.multiple_of(i * size, size), size)


def part_of(size, i):
    return tile(i, size // PARTS)


def ffn_branch(x_ref, slab, down, slope_ref, acc, ready, step=256):
    acc[...] = jnp.zeros_like(acc)
    size = slab.shape[1] // PARTS

    def part(i, carry):
        ready(i)
        act, before = None, None
        for j in range(size // step):
            cols = pl.ds(pl.multiple_of(i * size + j * step, step), step)
            values, slope = gelu_pair(dot(x_ref[...], slab[:, cols]))
            slope_ref[:, cols] = slope.astype(BF)
            if act is not None:
                acc[...] += dot(act, down[before, :])
            act, before = values.astype(BF), cols
        acc[...] += dot(act, down[before, :])
        return carry

    lax.fori_loop(0, PARTS, part, 0, unroll=2)


def ffn_branch_back(db, slab, down, slope_ref, acc, ready, step=256):
    size = slab.shape[1] // PARTS

    def part(i, carry):
        ready(i)
        df, before = None, None
        for j in range(size // step):
            cols = pl.ds(pl.multiple_of(i * size + j * step, step), step)
            dg = dot_t(db[...], down[cols, :])
            if df is not None:
                acc[...] += dot_t(df, slab[:, before])
            df, before = (dg * slope_ref[:, cols].astype(F32)).astype(BF), cols
        acc[...] += dot_t(df, slab[:, before])
        return carry

    lax.fori_loop(0, PARTS, part, 0, unroll=2)


def project(x_ref, slab, qkv_ref, ready, step=256):
    width = x_ref.shape[1]

    def part(i, carry):
        ready(i)
        scale = jnp.where(i == 0, (width // HEADS) ** -0.5, 1.0)
        for j in range(width // step):
            cols = pl.ds(pl.multiple_of(i * width + j * step, step), step)
            qkv_ref[:, cols] = (dot(x_ref[...], slab[:, cols]) * scale).astype(BF)
        return carry

    lax.fori_loop(0, 3, part, 0)


def attend(qkv_ref, bias_v, p_v, c_ref):
    rows, width = c_ref.shape
    head = width // HEADS
    lower = lax.broadcasted_iota(jnp.int32, (rows, 2 * head), 1) < head

    def body(i, carry):
        def part(n):
            return qkv_ref[:, pl.ds(pl.multiple_of(n * width + i * 2 * head, 2 * head), 2 * head)]

        q, k, v = part(0), part(1), part(2)
        parts = []
        for h in range(2):
            q_h = jnp.where(lower == (h == 0), q, jnp.zeros_like(q))
            s = dot_t(q_h, k) + bias_v[...]
            e = jnp.exp(s - jnp.max(s, axis=-1, keepdims=True))
            p = (e * (1.0 / jnp.sum(e, axis=-1, keepdims=True))).astype(BF)
            p_v[2 * i + h] = p
            parts.append(dot(p, v))
        c_ref[:, tile(i, 2 * head)] = jnp.where(lower, parts[0], parts[1]).astype(BF)
        return carry

    lax.fori_loop(0, HEADS // 2, body, 0, unroll=6)


def attend_back(qkv_ref, c_ref, dc_ref, p_v, dqkv):
    rows, width = c_ref.shape
    head = width // HEADS
    lower = lax.broadcasted_iota(jnp.int32, (rows, 2 * head), 1) < head

    def body(i, carry):
        def cols(n):
            return pl.ds(pl.multiple_of(n * width + i * 2 * head, 2 * head), 2 * head)

        q, k, v = qkv_ref[:, cols(0)], qkv_ref[:, cols(1)], qkv_ref[:, cols(2)]
        dc = dc_ref[:, cols(0)]
        dc_wide = dc.astype(F32)
        prod = dc_wide * c_ref[:, cols(0)].astype(F32)
        q_t = q.astype(F32).T.astype(BF)
        dc_t = dc_wide.T.astype(BF)
        dq, dk, dv = [], [], []
        for h in range(2):
            mine = lower == (h == 0)
            p = p_v[2 * i + h]
            delta = jnp.sum(jnp.where(mine, prod, 0.0), axis=-1, keepdims=True)
            dp = dot_t(jnp.where(mine, dc, jnp.zeros_like(dc)), v)
            ds = (p.astype(F32) * (dp - delta)).astype(BF)
            dq.append(dot(ds, k))
            dk.append(dot(q_t[h * head : (h + 1) * head], ds))
            dv.append(dot(dc_t[h * head : (h + 1) * head], p))
        dqkv[:, cols(0)] = (jnp.where(lower, dq[0], dq[1]) * head ** -0.5).astype(BF)
        dqkv[:, cols(1)] = jnp.concatenate(dk, axis=0).T.astype(BF)
        dqkv[:, cols(2)] = jnp.concatenate(dv, axis=0).T.astype(BF)
        return carry

    lax.fori_loop(0, HEADS // 2, body, 0, unroll=6)


def by_columns(target, value, step=256):
    for j in range(target.shape[1] // step):
        cols = slice(j * step, (j + 1) * step)
        target[:, cols] = value(cols).astype(target.dtype)


def post_saved(rows, width):
    return [((rows, width), BF), ((128, rows), BF), ((rows, 128), F32), ((rows, width), BF),
            ((rows, 128), F32)]


def block_saved(block, rows, width, ff):
    if block % 2 == 0:
        first = [((rows, 3 * width), BF), ((rows, width), BF), ((HEADS, rows, rows), BF)]
    else:
        first = [((rows, ff), BF)]
    return first + post_saved(rows, width)


def weight_ins(weights):
    own, own_pack, bufs = weights
    return [(own, ANY), (own_pack, ANY)] + [(x, ANY) for parts in bufs for x in parts]


def weight_refs(refs, weights):
    refs, parts = list(refs), []
    for group in weights[2]:
        parts.append(tuple(refs[2 + sum(map(len, parts)) :][: len(group)]))
    return refs[0], refs[1], parts


def forward(x, seg, src, weights, small, down, adapt):
    rows, width = x.shape
    ff = weights[0].shape[1]
    layers = down.shape[0]
    n_w = len(weight_ins(weights))
    shapes = [block_saved(b, rows, width, ff) for b in range(2)]
    n_a = len(shapes[0])

    def body(ins, outs, scratch):
        src_ref, x_ref, segc_ref, segr_ref, small_ref, down_ref = ins[:6]
        wts = weight_refs(ins[6 : 6 + n_w], weights)
        out_a, out_f, sent = outs[:n_a], outs[n_a:-1], outs[-1]
        slabs, packs, down_v, y_v, acc, bias_v, sem_ref = scratch[:7]
        buf_a, buf_f = scratch[7 : 7 + n_a], scratch[7 + n_a :]
        sems = Sems(sem_ref)
        slab_sems = [sems.run(PARTS) for b in range(2)]
        down_sems, pack_sem = sems.run(PARTS), sems.run(1).at[0]
        group_a, group_f = Group(sems, n_a), Group(sems, len(buf_f))
        rows_sems = sems.run(2)
        core = src_ref[0, GROUP + 1]

        load_slab(slab_sems[0], src_ref, 0, wts, slabs.at[0])
        for b in range(2 * layers):
            load_pack(pack_sem, src_ref, b, wts, packs.at[b])
        bias_v[...] = jnp.where(segc_ref[...] == segr_ref[...], 0.0, -1e30)
        y_v[1] = x_ref[...]
        for b in range(2 * layers):
            pltpu.make_async_copy(wts[1], packs.at[b], pack_sem).wait()

        def save_a(layer):
            return [(buf, out.at[layer]) for buf, out in zip(buf_a, out_a)]

        def save_f(layer):
            return [(buf, out.at[layer]) for buf, out in zip(buf_f, out_f)]

        def wait_rows(i):
            for copy in row_copies(y_v.at[i], 0, 0, sent, rows_sems.at[i]):
                copy.wait()

        def layer_step(layer, carry):
            b = 2 * layer
            slab = slabs.at[0]

            @pl.when(layer > 0)
            def _():
                group_a.wait(*save_a(0))
                wait_rows(0)

            qkv, ctx, probs = buf_a[:3]
            project(y_v.at[1], slab, qkv, lambda i: slab_part(slab_sems[0], wts, slab, i))
            slab_part(slab_sems[0], wts, slab, PARTS - 1)
            load_slab(slab_sems[1], src_ref, b + 1, wts, slabs.at[1])
            load_down(down_sems, down_ref, layer, down_v)
            attend(qkv, bias_v, probs, ctx)
            by_columns(acc, lambda cols: dot(
                ctx[...], slab[:, 3 * width + cols.start : 3 * width + cols.stop]))

            @pl.when(layer + 1 < layers)
            def _():
                load_slab(slab_sems[0], src_ref, b + 2, wts, slab)

            post_forward(packs.at[b], small_ref.at[src_ref[b, GROUP]], y_v.at[1], acc, y_v.at[0],
                         buf_a[3:], adapt)
            for copy in row_copies(y_v.at[0], b, core, sent, rows_sems.at[0]):
                copy.start()
            group_a.start(*save_a(layer))

            @pl.when(layer > 0)
            def _():
                group_f.wait(*save_f(0))
                wait_rows(1)

            def ready(i):
                slab_part(slab_sems[1], wts, slabs.at[1], i)
                down_part(down_sems, down_ref, down_v, i)

            ffn_branch(y_v.at[0], slabs.at[1], down_v, buf_f[0], acc, ready)
            post_forward(packs.at[b + 1], small_ref.at[src_ref[b + 1, GROUP]], y_v.at[0], acc,
                         y_v.at[1], buf_f[1:], adapt)
            for copy in row_copies(y_v.at[1], b + 1, core, sent, rows_sems.at[1]):
                copy.start()
            group_f.start(*save_f(layer))
            return carry

        lax.fori_loop(0, layers, layer_step, 0)
        group_a.wait(*save_a(0))
        group_f.wait(*save_f(0))
        for i in range(2):
            wait_rows(i)

    outs = [(like((layers,) + sh, dt), ANY) for b in range(2) for sh, dt in shapes[b]]
    outs.append((like((2 * layers * GROUP, rows // GROUP, width)), ANY))
    scratch = [
        pltpu.VMEM((2,) + weights[0].shape, BF),
        pltpu.VMEM((2 * layers,) + weights[1].shape, BF),
        pltpu.VMEM((ff, width), BF), pltpu.VMEM((2, rows, width), BF),
        pltpu.VMEM((rows, width), F32), pltpu.VMEM((rows, rows), F32),
        pltpu.SemaphoreType.DMA((48,))]
    for b in range(2):
        scratch += [pltpu.VMEM(sh, dt) for sh, dt in shapes[b]]
    res = run(
        body, [(src, SMEM), (x, VMEM), (seg[:, None], VMEM), (seg[None, :], VMEM), (small, VMEM),
               (down, ANY)] + weight_ins(weights), outs, scratch, "forward", 60)
    return (res[:n_a], res[n_a:-1]), res[-1]


def backward(dy, saved, src, weights, small, down, adapt):
    rows, width = dy.shape
    ff = weights[0].shape[1]
    layers = down.shape[0]
    n_w = len(weight_ins(weights))
    saved_a, saved_f = saved
    n_a, n_f = len(saved_a), len(saved_f)

    def body(ins, outs, scratch):
        src_ref, dy_ref, small_ref, down_ref = ins[:4]
        wts = weight_refs(ins[4 : 4 + n_w], weights)
        in_a, in_f = ins[4 + n_w : 4 + n_w + n_a], ins[4 + n_w + n_a :]
        sent, grads_out = outs[0], outs[1:]
        slabs, packs, down_v, acc, db, dpt, grads, dx_v, dc_v, dqkv, dy_v, sem_ref = scratch[:12]
        buf_a, buf_f = scratch[12 : 12 + n_a], scratch[12 + n_a :]
        sems = Sems(sem_ref)
        slab_sems = [sems.run(PARTS) for i in range(2)]
        down_sems, pack_sems = sems.run(PARTS), sems.run(2)
        group_a, group_f, group_dy = Group(sems, n_a), Group(sems, n_f), Group(sems, 1)
        rows_sems, grads_sems = sems.run(2), sems.run(2)
        core = src_ref[0, GROUP + 1]

        def load_a(layer):
            return [(x.at[layer], buf) for x, buf in zip(in_a[3:] + in_a[:3], buf_a[3:] + buf_a[:3])]

        def load_f(layer):
            return [(x.at[layer], buf) for x, buf in zip(in_f[1:] + in_f[:1], buf_f[1:] + buf_f[:1])]

        def fetch_f(layer):
            b = 2 * layer + 1
            group_f.start(*load_f(layer))
            load_pack(pack_sems.at[0], src_ref, b, wts, packs.at[0])
            load_down(down_sems, down_ref, layer, down_v)
            load_slab(slab_sems[0], src_ref, b, wts, slabs.at[0])

        def wait_pack(i):
            pltpu.make_async_copy(wts[1], packs.at[i], pack_sems.at[i]).wait()

        def wait_sent(i, value_ref):
            for copy in row_copies(value_ref, 0, 0, sent, rows_sems.at[i]):
                copy.wait()
            pltpu.make_async_copy(grads.at[i], grads_out[0], grads_sems.at[i]).wait()

        group_dy.start((dy_ref, dy_v))
        fetch_f(layers - 1)
        group_dy.wait((dy_ref, dy_v))

        def layer_step(count, carry):
            layer = layers - 1 - count
            b = 2 * layer + 1

            @pl.when(count > 0)
            def _():
                wait_sent(0, dx_v)

            group_f.wait(*load_f(0))
            wait_pack(0)
            post_backward(packs.at[0], small_ref.at[src_ref[b, GROUP]], dy_v, buf_f[1:], acc, db,
                          grads.at[0], dpt, adapt)
            send_grads(grads_sems.at[0], grads.at[0], src_ref[b, GROUP], grads_out)
            load_pack(pack_sems.at[1], src_ref, b - 1, wts, packs.at[1])
            group_a.start(*load_a(layer))
            load_slab(slab_sems[1], src_ref, b - 1, wts, slabs.at[1])

            def ready(i):
                slab_part(slab_sems[0], wts, slabs.at[0], i)
                down_part(down_sems, down_ref, down_v, i)

            ffn_branch_back(db, slabs.at[0], down_v, buf_f[0], acc, ready)
            dx_v[...] = acc[...].astype(BF)
            for copy in row_copies(dx_v, b, core, sent, rows_sems.at[0]):
                copy.start()

            @pl.when(count > 0)
            def _():
                wait_sent(1, dy_v)

            group_a.wait(*load_a(0))
            wait_pack(1)

            @pl.when(layer > 0)
            def _():
                fetch_f(layer - 1)

            post_backward(packs.at[1], small_ref.at[src_ref[b - 1, GROUP]], dx_v, buf_a[3:], acc,
                          db, grads.at[1], dpt, adapt)
            send_grads(grads_sems.at[1], grads.at[1], src_ref[b - 1, GROUP], grads_out)
            slab = slabs.at[1]
            for i in range(PARTS):
                slab_part(slab_sems[1], wts, slab, i)
            by_columns(dc_v, lambda cols: dot_t(db[...], slab[cols, 3 * width :]))
            attend_back(buf_a[0], buf_a[1], dc_v, buf_a[2], dqkv)
            by_columns(dy_v, lambda cols: acc[:, cols] + dot_t(dqkv[...], slab[cols, : 3 * width]))
            for copy in row_copies(dy_v, b - 1, core, sent, rows_sems.at[1]):
                copy.start()
            return carry

        lax.fori_loop(0, layers, layer_step, 0)
        wait_sent(0, dx_v)
        wait_sent(1, dy_v)

    grad_shape = (2 * adapt + EXTRA, width)
    outs = [(like((2 * layers * GROUP, rows // GROUP, width)), ANY)]
    outs += [(like(grad_shape), ANY)] * (2 * layers)
    scratch = [
        pltpu.VMEM((2,) + weights[0].shape, BF), pltpu.VMEM((2,) + weights[1].shape, BF),
        pltpu.VMEM((ff, width), BF), pltpu.VMEM((rows, width), F32), pltpu.VMEM((rows, width), BF),
        pltpu.VMEM((128, rows), BF), pltpu.VMEM((2,) + grad_shape, BF),
        pltpu.VMEM((rows, width), BF), pltpu.VMEM((rows, width), BF),
        pltpu.VMEM((rows, 3 * width), BF), pltpu.VMEM((rows, width), BF),
        pltpu.SemaphoreType.DMA((48,))]
    scratch += [pltpu.VMEM(x.shape[1:], x.dtype) for x in tuple(saved_a) + tuple(saved_f)]
    res = run(
        body, [(src, SMEM), (dy, ANY), (small, VMEM), (down, ANY)] + weight_ins(weights)
        + [(x, ANY) for x in tuple(saved_a) + tuple(saved_f)], outs, scratch, "backward", 60)
    return res[0], res[1:]


def settle(x):
    def body(ins, outs, scratch):
        buf, sems = scratch
        loads = [pltpu.make_async_copy(ins[0].at[i], buf.at[i], sems.at[i])
                 for i in range(x.shape[0])]
        stores = [pltpu.make_async_copy(buf.at[i], outs[0].at[i], sems.at[i])
                  for i in range(x.shape[0])]
        for load in loads:
            load.start()
        for load, store in zip(loads, stores):
            load.wait()
            store.start()
        for store in stores:
            store.wait()

    return run(body, [(x, ANY)], [(like(x.shape), ANY)],
               [pltpu.VMEM(x.shape, BF), pltpu.SemaphoreType.DMA((x.shape[0],))], "settle", 3)[0]


def per_device(tokens, cotangent, segment_ids, slabs, ffn_down,
               ad_down, ad_down_bias, ad_up, ad_up_bias, ln_gain, ln_bias):
    n_section, n_group = lax.axis_size("section"), lax.axis_size("group")
    s, group, core = (lax.axis_index(name) for name in ("section", "group", "core"))
    n_micro, rows_dev, width = tokens.shape
    adapt = ad_down.shape[2]
    sections = range(n_section)

    def sect(x, apart):
        return lax.ppermute(x, "section", [(i, i ^ apart) for i in sections])

    def peer(x):
        return lax.ppermute(x, "core", [(0, 1), (1, 0)])

    def by_core(x, apart):
        pairs = [(i * GROUP + c, (i ^ apart[c]) * GROUP + c) for i in sections for c in range(GROUP)]
        return lax.ppermute(x, ("section", "core"), pairs)

    slab = slabs[0]
    half = slab.shape[0] // GROUP
    mats = jnp.concatenate([ad_down[0].T, ad_up[0]], axis=0).astype(BF)
    own_pack = jnp.concatenate([mats[i : i + EXTRA] for i in range(0, 2 * adapt, EXTRA)], axis=1)
    own_small = jnp.concatenate([jnp.pad(ad_down_bias, ((0, 0), (0, width - adapt))), ad_up_bias,
                                 ln_gain, ln_bias, jnp.zeros((4, width), F32)], axis=0)
    small = [own_small] + [sect(own_small, d) for d in range(1, n_section)]
    size = own_pack.shape[0] // GROUP
    plane = group % 2
    pack_half = lax.dynamic_slice_in_dim(own_pack, core * size, size, 0)
    quarter = lax.dynamic_slice_in_dim(slab, core * half + plane * (half // 2), half // 2, 0)
    given = jnp.concatenate([lax.dynamic_slice_in_dim(slab, core * half, half, 0), pack_half],
                            axis=0)
    own_micro = s * GROUP + core
    peer_micro = s * GROUP + 1 - core

    def gather_item(x):
        mine = lax.dynamic_index_in_dim(x, own_micro, 0, keepdims=False)
        given = lax.dynamic_index_in_dim(x, peer_micro, 0, keepdims=False)
        return jnp.concatenate([mine, peer(given)], axis=0)

    hidden = gather_item(tokens)
    cot = gather_item(cotangent)
    second = by_core(given, (2, 1))
    first = by_core(jnp.concatenate([quarter, pack_half], axis=0), (1, 2))
    second, first, hidden, cot, *small = lax.optimization_barrier(
        (second, first, hidden, cot, *small))
    first_z = lax.ppermute(first, "group", [(i, i ^ 1) for i in range(n_group)])
    third = by_core(second, (1, 2))
    bufs = [(first, first_z), (second,), (third,)]
    bufs += [tuple(peer(x) for x in parts) for parts in bufs]
    small = jnp.stack(small)

    item_start = group * GROUP * rows_dev
    seg = jnp.concatenate([
        lax.dynamic_slice(segment_ids, (own_micro, item_start + c * rows_dev), (1, rows_dev))[0]
        for c in (core, 1 - core)])

    def source(b):
        d = s ^ b
        at = []
        for h in range(GROUP):
            i = jnp.where(d == 3, 3, jnp.where((d == 1) == (h == 0), 1, 2))
            at.append(jnp.where(d == 0, 0, jnp.where(core == h, i, i + 3)))
        return jnp.stack(at + [d, core, plane]).astype(jnp.int32)

    src = jnp.stack([source(b) for b in sections])
    weights = (slab, own_pack, bufs)

    def to_owners(x):
        return lax.all_to_all(x, ("section", "core"), 0, 0, tiled=True)

    saved, sent = forward(hidden, seg, src, weights, small, ffn_down, adapt)
    block_outputs = to_owners(sent)
    leaving, grads = backward(cot, saved, src, weights, small, ffn_down, adapt)
    block_outputs, leaving, *grads = lax.optimization_barrier((block_outputs, leaving, *grads))
    block_outputs = settle(block_outputs)

    coming = [sect(grads[d], d) for d in range(1, n_section)]
    *coming, leaving = lax.optimization_barrier((*coming, leaving))
    total = grads[0].astype(F32)
    for part in coming:
        total = total + part.astype(F32)
    total = total.astype(BF)
    input_grads = to_owners(leaving)
    total = (total.astype(F32) + peer(total).astype(F32)).astype(BF)
    apart = 1
    while apart < n_group:
        other = lax.ppermute(total, "group", [(i, i ^ apart) for i in range(n_group)])
        total = (total.astype(F32) + other.astype(F32)).astype(BF)
        apart *= 2
    total = total.astype(F32)
    return (block_outputs[None], input_grads[None], total[:adapt].T[None],
            total[2 * adapt + 3, :adapt][None], total[adapt : 2 * adapt][None],
            total[2 * adapt][None], total[2 * adapt + 1][None], total[2 * adapt + 2][None])


def solution(mesh):
    n_section, n_rows = mesh.devices.shape
    cores = Mesh(mesh.devices.reshape(n_section, n_rows // GROUP, GROUP),
                 ("section", "group", "core"))
    rows = ("group", "core")
    in_specs = (
        P(None, rows, None), P(None, rows, None), P(), P("section", None, None), P(),
        P("section", None, None), P("section", None), P("section", None, None),
        P("section", None), P("section", None), P("section", None),
    )
    out_specs = (
        P("section", None, rows, None), P("section", None, rows, None),
        P("section", None, None), P("section", None), P("section", None, None),
        P("section", None), P("section", None), P("section", None),
    )
    return jax.shard_map(
        per_device, mesh=cores, in_specs=in_specs, out_specs=out_specs, check_vma=False
    )
```

```python
import jax
import jax.numpy as jnp
from jax import lax
from jax.experimental import pallas as pl
from jax.experimental.pallas import tpu as pltpu
from jax.sharding import Mesh, PartitionSpec as P

HEADS = 12
GROUP = 2
PARTS = 4
EXTRA = 32
SUMS = 16
COST = 1e8
BF = jnp.bfloat16
F32 = jnp.float32
VMEM = pl.BlockSpec(memory_space=pltpu.VMEM)
ANY = pl.BlockSpec(memory_space=pl.ANY)
SMEM = pl.BlockSpec(memory_space=pltpu.SMEM)
LIMIT = 56 * 1024 * 1024


def dot(left, right):
    return jnp.dot(left, right, preferred_element_type=F32)


def dot_t(left, right):
    return lax.dot_general(left, right, (((1,), (1,)), ((), ())), preferred_element_type=F32)


def gelu_pair(x):
    size = jnp.abs(x)
    base = 1.0 + 0.23164188 * size
    t = 1.0 / base
    poly = 0.127414796 + t * (-0.142248368 + t * (0.710706871 + t * (
        -0.726576014 + t * 0.530702715)))
    bell = jnp.exp2(-0.7213475204444817 * (x * x))
    tail = (t * poly) * bell
    phi = jnp.where(x < 0, tail, 1.0 - tail)
    return x * phi, phi + x * (0.3989422804014327 * bell)


def like(shape, dtype=BF):
    return jax.ShapeDtypeStruct(shape, dtype)


def run(body, ins, outs, scratch, name, micros):
    n_in, n_out = len(ins), len(outs)

    def wrapped(*refs):
        body(refs[:n_in], refs[n_in : n_in + n_out], refs[n_in + n_out :])

    return pl.pallas_call(
        wrapped,
        out_shape=[shape for shape, _ in outs],
        in_specs=[spec for _, spec in ins],
        out_specs=[spec for _, spec in outs],
        scratch_shapes=scratch,
        name=name,
        cost_estimate=pl.CostEstimate(flops=int(micros * COST), bytes_accessed=0, transcendentals=0),
        compiler_params=pltpu.CompilerParams(vmem_limit_bytes=LIMIT),
    )(*[array for array, _ in ins])


class Group:
    def __init__(self, sems, count):
        self.sems, self.first, self.pairs = sems, sems.used, []
        sems.used += count

    def start(self, *pairs):
        for i, (source, target) in enumerate(pairs):
            pltpu.make_async_copy(source, target, self.sems.ref.at[self.first + i]).start()

    def wait(self, *pairs):
        for i, (source, target) in enumerate(pairs):
            pltpu.make_async_copy(source, target, self.sems.ref.at[self.first + i]).wait()


class Sems:
    def __init__(self, ref):
        self.ref, self.used = ref, 0

    def run(self, count):
        self.used += count
        return self.ref.at[pl.ds(self.used - count, count)]


def load_slab(sems, src, block, weights, slab_v, order=range(PARTS)):
    own, own_pack, bufs = weights
    rows = own.shape[0] // GROUP
    plane = src[block, GROUP + 2]
    for h in range(GROUP):
        for i, parts in enumerate([(own,)] + list(bufs)):
            size = rows // len(parts)

            @pl.when(src[block, h] == i)
            def _():
                for p in order:
                    columns = pl.ds(p * (own.shape[1] // PARTS), own.shape[1] // PARTS)
                    for n, buf in enumerate(parts):
                        first = h * rows if i == 0 else 0
                        to = h * rows
                        if len(parts) > 1:
                            to += size * (plane if n == 0 else 1 - plane)
                        pltpu.make_async_copy(
                            buf.at[pl.ds(first, size), columns],
                            slab_v.at[pl.ds(pl.multiple_of(to, 64), size), columns],
                            sems.at[p]).start()


def slab_part(sems, weights, slab_v, p):
    own = weights[0]
    columns = part_of(own.shape[1], p)
    pltpu.make_async_copy(own.at[:, columns], slab_v.at[:, columns], sems.at[p]).wait()


def load_down(sems, down, layer, down_v, p):
    rows = pl.ds(p * (down_v.shape[0] // PARTS), down_v.shape[0] // PARTS)
    pltpu.make_async_copy(down.at[layer, rows], down_v.at[rows], sems.at[p]).start()


def down_part(sems, down, down_v, p):
    rows = part_of(down_v.shape[0], p)
    pltpu.make_async_copy(down.at[0, rows], down_v.at[rows], sems.at[p]).wait()


def load_pack(sem, src, block, weights, pack_v):
    own, own_pack, bufs = weights
    rows = own.shape[0] // GROUP
    size = own_pack.shape[0] // GROUP
    for h in range(GROUP):
        at = pl.ds(h * size, size)
        for i, parts in enumerate([(own_pack,)] + list(bufs)):
            buf = parts[0]
            first = h * size if i == 0 else rows // len(parts)

            @pl.when(src[block, h] == i)
            def _():
                pltpu.make_async_copy(buf.at[pl.ds(first, size)], pack_v.at[at], sem).start()


def send_grads(sem, value_ref, apart, outs):
    for d, out in enumerate(outs):
        @pl.when(apart == d)
        def _():
            pltpu.make_async_copy(value_ref, out, sem).start()


def row_copies(value_ref, block, core, out, sem):
    half = value_ref.shape[0] // GROUP
    return [pltpu.make_async_copy(
        value_ref.at[pl.ds(i * half, half)],
        out.at[GROUP * block + (core if i == 0 else GROUP - 1 - core)], sem) for i in range(GROUP)]


def adapters(pack, width, adapt):
    rows = [pack[:, i * width : (i + 1) * width] for i in range(2 * adapt // EXTRA)]
    zeros = jnp.zeros((128 - adapt, width), BF)
    per = adapt // EXTRA
    down_t = jnp.concatenate(rows[:per] + [zeros], axis=0)
    up = jnp.concatenate(rows[per:] + [zeros], axis=0)
    return down_t, up


def post_forward(pack, small, x_ref, b_ref, y_ref, saved, adapt):
    low_ref, ut_ref, slope_ref, zhat_ref, rstd_ref = saved
    rows, width = x_ref.shape
    down_t, up = adapters(pack, width, adapt)
    down_bias, up_bias, gain, bias = [small[i : i + 1, :] for i in range(4)]
    step = 512

    def body(i, carry):
        at = pl.ds(pl.multiple_of(i * step, step), step)
        branch = b_ref[at, :]
        low = branch.astype(BF)
        low_ref[at, :] = low
        pre = dot_t(low, down_t) + down_bias[:, :128]
        inner, slope = gelu_pair(pre)
        slope_ref[at, :] = slope
        ut_ref[:, at] = inner.T.astype(BF)
        mixed = x_ref[at, :].astype(F32) + branch + dot(inner.astype(BF), up) + up_bias
        center = mixed - jnp.mean(mixed, axis=-1, keepdims=True)
        rstd = lax.rsqrt(jnp.mean(center * center, axis=-1, keepdims=True) + 1e-05)
        zhat = center * rstd
        y_ref[at, :] = (zhat * gain + bias).astype(BF)
        zhat_ref[at, :] = zhat.astype(BF)
        rstd_ref[at, :] = jnp.broadcast_to(rstd, (step, 128))
        return carry

    lax.fori_loop(0, rows // step, body, 0)


def post_backward(pack, small, dy_ref, saved, dz_ref, db_ref, grads_ref, dpt_ref, adapt):
    low_ref, ut_ref, slope_ref, zhat_ref, rstd_ref = saved
    rows, width = dy_ref.shape
    down_t, up = adapters(pack, width, adapt)
    gain = small[2:3, :]
    step = 512

    def fold(v):
        return jnp.sum(v.reshape(v.shape[0] // 8, 8, v.shape[1]), axis=0)

    def body(i, carry):
        s_bias, s_gain, s_upb, s_downb = carry
        at = pl.ds(pl.multiple_of(i * step, step), step)
        d_out = dy_ref[at, :].astype(F32)
        zhat = zhat_ref[at, :].astype(F32)
        s_bias = s_bias + fold(d_out)
        s_gain = s_gain + fold(d_out * zhat)
        dz = d_out * gain
        dz = rstd_ref[at, :1] * (dz - jnp.mean(dz, axis=-1, keepdims=True)
                                 - zhat * jnp.mean(dz * zhat, axis=-1, keepdims=True))
        s_upb = s_upb + fold(dz)
        low = dz.astype(BF)
        db_ref[at, :] = low
        d_pre = dot_t(low, up) * slope_ref[at, :]
        s_downb = s_downb + fold(d_pre)
        dpt_ref[:, at] = d_pre.T.astype(BF)
        dz_ref[at, :] = dz
        return s_bias, s_gain, s_upb, s_downb

    zero = jnp.zeros((8, width), F32)
    s_bias, s_gain, s_upb, s_downb = lax.fori_loop(
        0, rows // step, body, (zero, zero, zero, jnp.zeros((8, 128), F32)))
    g_down = dot(dpt_ref[...], low_ref[...])
    g_up = dot(ut_ref[...], db_ref[...])
    grads_ref[0:adapt, :] = g_down[:adapt].astype(BF)
    grads_ref[adapt : 2 * adapt, :] = g_up[:adapt].astype(BF)
    tail = jnp.concatenate(
        [jnp.sum(v, axis=0, keepdims=True) for v in (s_upb, s_gain, s_bias)]
        + [jnp.concatenate([jnp.sum(s_downb, axis=0, keepdims=True),
                            jnp.zeros((1, width - 128), F32)], axis=1),
           jnp.zeros((SUMS - 4, width), F32)], axis=0)
    grads_ref[2 * adapt :, :] = tail.astype(BF)

    def body2(i, carry):
        at = pl.ds(pl.multiple_of(i * step, step), step)
        d_pre = dpt_ref[:, at].astype(F32).T.astype(BF)
        db_ref[at, :] = (dz_ref[at, :] + dot(d_pre, down_t)).astype(BF)
        return carry

    lax.fori_loop(0, rows // step, body2, 0)


def tile(i, size):
    return pl.ds(pl.multiple_of(i * size, size), size)


def part_of(size, i):
    return tile(i, size // PARTS)


def ffn_branch(x_ref, slab, down, slope_ref, acc, ready, step=256):
    acc[...] = jnp.zeros_like(acc)
    size = slab.shape[1] // PARTS

    def part(i, carry):
        ready(i)
        act, before = None, None
        for j in range(size // step):
            cols = pl.ds(pl.multiple_of(i * size + j * step, step), step)
            values, slope = gelu_pair(dot(x_ref[...], slab[:, cols]))
            slope_ref[:, cols] = slope.astype(BF)
            if act is not None:
                acc[...] += dot(act, down[before, :])
            act, before = values.astype(BF), cols
        acc[...] += dot(act, down[before, :])
        return carry

    lax.fori_loop(0, PARTS, part, 0, unroll=2)


def ffn_branch_back(db, slab, down, slope_ref, acc, ready, step=256):
    size = slab.shape[1] // PARTS

    def part(i, carry):
        ready(i)
        df, before = None, None
        for j in range(size // step):
            cols = pl.ds(pl.multiple_of(i * size + j * step, step), step)
            dg = dot_t(db[...], down[cols, :])
            if df is not None:
                acc[...] += dot_t(df, slab[:, before])
            df, before = (dg * slope_ref[:, cols].astype(F32)).astype(BF), cols
        acc[...] += dot_t(df, slab[:, before])
        return carry

    lax.fori_loop(0, PARTS, part, 0, unroll=2)


def project(x_ref, slab, qkv_ref, ready, step=256):
    width = x_ref.shape[1]

    def part(i, carry):
        ready(i)
        scale = jnp.where(i == 0, (width // HEADS) ** -0.5, 1.0)
        for j in range(width // step):
            cols = pl.ds(pl.multiple_of(i * width + j * step, step), step)
            qkv_ref[:, cols] = (dot(x_ref[...], slab[:, cols]) * scale).astype(BF)
        return carry

    lax.fori_loop(0, 3, part, 0)


def attend(qkv_ref, bias_v, p_v, c_ref):
    rows, width = c_ref.shape
    head = width // HEADS
    lower = lax.broadcasted_iota(jnp.int32, (rows, 2 * head), 1) < head

    def body(i, carry):
        def part(n):
            return qkv_ref[:, pl.ds(pl.multiple_of(n * width + i * 2 * head, 2 * head), 2 * head)]

        q, k, v = part(0), part(1), part(2)
        parts = []
        for h in range(2):
            q_h = jnp.where(lower == (h == 0), q, jnp.zeros_like(q))
            s = dot_t(q_h, k) + bias_v[...]
            e = jnp.exp(s - jnp.max(s, axis=-1, keepdims=True))
            p = (e * (1.0 / jnp.sum(e, axis=-1, keepdims=True))).astype(BF)
            p_v[2 * i + h] = p
            parts.append(dot(p, v))
        c_ref[:, tile(i, 2 * head)] = jnp.where(lower, parts[0], parts[1]).astype(BF)
        return carry

    lax.fori_loop(0, HEADS // 2, body, 0, unroll=6)


def attend_back(qkv_ref, c_ref, dc_ref, p_v, dqkv):
    rows, width = c_ref.shape
    head = width // HEADS
    lower = lax.broadcasted_iota(jnp.int32, (rows, 2 * head), 1) < head

    def body(i, carry):
        def cols(n):
            return pl.ds(pl.multiple_of(n * width + i * 2 * head, 2 * head), 2 * head)

        q, k, v = qkv_ref[:, cols(0)], qkv_ref[:, cols(1)], qkv_ref[:, cols(2)]
        dc = dc_ref[:, cols(0)]
        dc_wide = dc.astype(F32)
        prod = dc_wide * c_ref[:, cols(0)].astype(F32)
        q_t = q.astype(F32).T.astype(BF)
        dc_t = dc_wide.T.astype(BF)
        dq, dk, dv = [], [], []
        for h in range(2):
            mine = lower == (h == 0)
            p = p_v[2 * i + h]
            delta = jnp.sum(jnp.where(mine, prod, 0.0), axis=-1, keepdims=True)
            dp = dot_t(jnp.where(mine, dc, jnp.zeros_like(dc)), v)
            ds = (p.astype(F32) * (dp - delta)).astype(BF)
            dq.append(dot(ds, k))
            dk.append(dot(q_t[h * head : (h + 1) * head], ds))
            dv.append(dot(dc_t[h * head : (h + 1) * head], p))
        dqkv[:, cols(0)] = (jnp.where(lower, dq[0], dq[1]) * head ** -0.5).astype(BF)
        dqkv[:, cols(1)] = jnp.concatenate(dk, axis=0).T.astype(BF)
        dqkv[:, cols(2)] = jnp.concatenate(dv, axis=0).T.astype(BF)
        return carry

    lax.fori_loop(0, HEADS // 2, body, 0, unroll=6)


def by_columns(target, value, step=256):
    for j in range(target.shape[1] // step):
        cols = slice(j * step, (j + 1) * step)
        target[:, cols] = value(cols).astype(target.dtype)


def post_saved(rows, width):
    return [((rows, width), BF), ((128, rows), BF), ((rows, 128), F32), ((rows, width), BF),
            ((rows, 128), F32)]


def block_saved(block, rows, width, ff):
    if block % 2 == 0:
        first = [((rows, 3 * width), BF), ((rows, width), BF), ((HEADS, rows, rows), BF)]
    else:
        first = [((rows, ff), BF)]
    return first + post_saved(rows, width)


def weight_ins(weights):
    own, own_pack, bufs = weights
    return [(own, ANY), (own_pack, ANY)] + [(x, ANY) for parts in bufs for x in parts]


def weight_refs(refs, weights):
    refs, parts = list(refs), []
    for group in weights[2]:
        parts.append(tuple(refs[2 + sum(map(len, parts)) :][: len(group)]))
    return refs[0], refs[1], parts


def forward(x, seg, src, weights, small, down, adapt):
    rows, width = x.shape
    ff = weights[0].shape[1]
    layers = down.shape[0]
    n_w = len(weight_ins(weights))
    shapes = [block_saved(b, rows, width, ff) for b in range(2)]
    n_a = len(shapes[0])

    def body(ins, outs, scratch):
        src_ref, x_ref, segc_ref, segr_ref, small_ref, down_ref = ins[:6]
        wts = weight_refs(ins[6 : 6 + n_w], weights)
        out_a, out_f, sent = outs[:n_a], outs[n_a:-1], outs[-1]
        slabs, packs, down_v, y_v, acc, bias_v, sem_ref = scratch[:7]
        buf_a, buf_f = scratch[7 : 7 + n_a], scratch[7 + n_a :]
        sems = Sems(sem_ref)
        slab_sems = [sems.run(PARTS) for b in range(2)]
        down_sems, pack_sem = sems.run(PARTS), sems.run(1).at[0]
        group_a, group_f = Group(sems, n_a), Group(sems, len(buf_f))
        rows_sems = sems.run(2)
        core = src_ref[0, GROUP + 1]

        load_slab(slab_sems[0], src_ref, 0, wts, slabs.at[0])
        for b in range(2 * layers):
            load_pack(pack_sem, src_ref, b, wts, packs.at[b])
        bias_v[...] = jnp.where(segc_ref[...] == segr_ref[...], 0.0, -1e30)
        y_v[1] = x_ref[...]
        for b in range(2 * layers):
            pltpu.make_async_copy(wts[1], packs.at[b], pack_sem).wait()

        def save_a(layer):
            return [(buf, out.at[layer]) for buf, out in zip(buf_a, out_a)]

        def save_f(layer):
            return [(buf, out.at[layer]) for buf, out in zip(buf_f, out_f)]

        def wait_rows(i):
            for copy in row_copies(y_v.at[i], 0, 0, sent, rows_sems.at[i]):
                copy.wait()

        def layer_step(layer, carry):
            b = 2 * layer
            slab = slabs.at[0]

            @pl.when(layer > 0)
            def _():
                group_a.wait(*save_a(0))
                wait_rows(0)

            qkv, ctx, probs = buf_a[:3]
            project(y_v.at[1], slab, qkv, lambda i: slab_part(slab_sems[0], wts, slab, i))
            slab_part(slab_sems[0], wts, slab, PARTS - 1)
            for p in range(PARTS):
                load_slab(slab_sems[1], src_ref, b + 1, wts, slabs.at[1], [p])
                load_down(down_sems, down_ref, layer, down_v, p)
            attend(qkv, bias_v, probs, ctx)
            by_columns(acc, lambda cols: dot(
                ctx[...], slab[:, 3 * width + cols.start : 3 * width + cols.stop]))

            @pl.when(layer + 1 < layers)
            def _():
                load_slab(slab_sems[0], src_ref, b + 2, wts, slab)

            post_forward(packs.at[b], small_ref.at[src_ref[b, GROUP]], y_v.at[1], acc, y_v.at[0],
                         buf_a[3:], adapt)
            for copy in row_copies(y_v.at[0], b, core, sent, rows_sems.at[0]):
                copy.start()
            group_a.start(*save_a(layer))

            @pl.when(layer > 0)
            def _():
                group_f.wait(*save_f(0))
                wait_rows(1)

            def ready(i):
                slab_part(slab_sems[1], wts, slabs.at[1], i)
                down_part(down_sems, down_ref, down_v, i)

            ffn_branch(y_v.at[0], slabs.at[1], down_v, buf_f[0], acc, ready)
            post_forward(packs.at[b + 1], small_ref.at[src_ref[b + 1, GROUP]], y_v.at[0], acc,
                         y_v.at[1], buf_f[1:], adapt)
            for copy in row_copies(y_v.at[1], b + 1, core, sent, rows_sems.at[1]):
                copy.start()
            group_f.start(*save_f(layer))
            return carry

        lax.fori_loop(0, layers, layer_step, 0)
        group_a.wait(*save_a(0))
        group_f.wait(*save_f(0))
        for i in range(2):
            wait_rows(i)

    outs = [(like((layers,) + sh, dt), ANY) for b in range(2) for sh, dt in shapes[b]]
    outs.append((like((2 * layers * GROUP, rows // GROUP, width)), ANY))
    scratch = [
        pltpu.VMEM((2,) + weights[0].shape, BF),
        pltpu.VMEM((2 * layers,) + weights[1].shape, BF),
        pltpu.VMEM((ff, width), BF), pltpu.VMEM((2, rows, width), BF),
        pltpu.VMEM((rows, width), F32), pltpu.VMEM((rows, rows), F32),
        pltpu.SemaphoreType.DMA((48,))]
    for b in range(2):
        scratch += [pltpu.VMEM(sh, dt) for sh, dt in shapes[b]]
    res = run(
        body, [(src, SMEM), (x, VMEM), (seg[:, None], VMEM), (seg[None, :], VMEM), (small, VMEM),
               (down, ANY)] + weight_ins(weights), outs, scratch, "forward", 60)
    return (res[:n_a], res[n_a:-1]), res[-1]


def backward(dy, saved, src, weights, small, down, adapt):
    rows, width = dy.shape
    ff = weights[0].shape[1]
    layers = down.shape[0]
    n_w = len(weight_ins(weights))
    saved_a, saved_f = saved
    n_a, n_f = len(saved_a), len(saved_f)

    def body(ins, outs, scratch):
        src_ref, dy_ref, small_ref, down_ref = ins[:4]
        wts = weight_refs(ins[4 : 4 + n_w], weights)
        in_a, in_f = ins[4 + n_w : 4 + n_w + n_a], ins[4 + n_w + n_a :]
        sent, grads_out = outs[0], outs[1:]
        slabs, packs, down_v, acc, db, dpt, grads, dx_v, dc_v, dqkv, dy_v, sem_ref = scratch[:12]
        buf_a, buf_f = scratch[12 : 12 + n_a], scratch[12 + n_a :]
        sems = Sems(sem_ref)
        slab_sems = [sems.run(PARTS) for i in range(2)]
        down_sems, slope_sems, pack_sems = sems.run(PARTS), sems.run(PARTS), sems.run(2)
        group_a, post_a = Group(sems, 3), Group(sems, n_a - 3)
        post_f, group_dy = Group(sems, n_f - 1), Group(sems, 1)
        rows_sems, grads_sems = sems.run(2), sems.run(2)
        core = src_ref[0, GROUP + 1]

        def pairs(refs, bufs, layer):
            return [(x.at[layer], buf) for x, buf in zip(refs, bufs)]

        def slope_part(layer, p):
            columns = part_of(ff, p)
            return pltpu.make_async_copy(in_f[0].at[layer, :, columns], buf_f[0].at[:, columns],
                                         slope_sems.at[p])

        def fetch_f(layer):
            b = 2 * layer + 1
            post_f.start(*pairs(in_f[1:], buf_f[1:], layer))
            load_pack(pack_sems.at[0], src_ref, b, wts, packs.at[0])
            for p in range(PARTS):
                load_down(down_sems, down_ref, layer, down_v, p)
                slope_part(layer, p).start()
                load_slab(slab_sems[0], src_ref, b, wts, slabs.at[0], [p])

        def wait_pack(i):
            pltpu.make_async_copy(wts[1], packs.at[i], pack_sems.at[i]).wait()

        def wait_sent(i, value_ref):
            for copy in row_copies(value_ref, 0, 0, sent, rows_sems.at[i]):
                copy.wait()
            pltpu.make_async_copy(grads.at[i], grads_out[0], grads_sems.at[i]).wait()

        group_dy.start((dy_ref, dy_v))
        fetch_f(layers - 1)
        group_dy.wait((dy_ref, dy_v))

        def layer_step(count, carry):
            layer = layers - 1 - count
            b = 2 * layer + 1

            @pl.when(count > 0)
            def _():
                wait_sent(0, dx_v)

            post_f.wait(*pairs(in_f[1:], buf_f[1:], 0))
            wait_pack(0)
            post_backward(packs.at[0], small_ref.at[src_ref[b, GROUP]], dy_v, buf_f[1:], acc, db,
                          grads.at[0], dpt, adapt)
            send_grads(grads_sems.at[0], grads.at[0], src_ref[b, GROUP], grads_out)
            load_pack(pack_sems.at[1], src_ref, b - 1, wts, packs.at[1])
            post_a.start(*pairs(in_a[3:], buf_a[3:], layer))
            load_slab(slab_sems[1], src_ref, b - 1, wts, slabs.at[1], [PARTS - 1])
            group_a.start(*pairs(in_a[:3], buf_a[:3], layer))
            load_slab(slab_sems[1], src_ref, b - 1, wts, slabs.at[1], range(PARTS - 1))

            def ready(i):
                slab_part(slab_sems[0], wts, slabs.at[0], i)
                down_part(down_sems, down_ref, down_v, i)
                slope_part(0, i).wait()

            ffn_branch_back(db, slabs.at[0], down_v, buf_f[0], acc, ready)
            dx_v[...] = acc[...].astype(BF)
            for copy in row_copies(dx_v, b, core, sent, rows_sems.at[0]):
                copy.start()

            @pl.when(count > 0)
            def _():
                wait_sent(1, dy_v)

            post_a.wait(*pairs(in_a[3:], buf_a[3:], 0))
            wait_pack(1)

            @pl.when(layer > 0)
            def _():
                fetch_f(layer - 1)

            post_backward(packs.at[1], small_ref.at[src_ref[b - 1, GROUP]], dx_v, buf_a[3:], acc,
                          db, grads.at[1], dpt, adapt)
            send_grads(grads_sems.at[1], grads.at[1], src_ref[b - 1, GROUP], grads_out)
            slab = slabs.at[1]
            slab_part(slab_sems[1], wts, slab, PARTS - 1)
            by_columns(dc_v, lambda cols: dot_t(db[...], slab[cols, 3 * width :]))
            group_a.wait(*pairs(in_a[:3], buf_a[:3], 0))
            attend_back(buf_a[0], buf_a[1], dc_v, buf_a[2], dqkv)
            for i in range(PARTS - 1):
                slab_part(slab_sems[1], wts, slab, i)
            by_columns(dy_v, lambda cols: acc[:, cols] + dot_t(dqkv[...], slab[cols, : 3 * width]))
            for copy in row_copies(dy_v, b - 1, core, sent, rows_sems.at[1]):
                copy.start()
            return carry

        lax.fori_loop(0, layers, layer_step, 0)
        wait_sent(0, dx_v)
        wait_sent(1, dy_v)

    grad_shape = (2 * adapt + SUMS, width)
    outs = [(like((2 * layers * GROUP, rows // GROUP, width)), ANY)]
    outs += [(like(grad_shape), ANY)] * (2 * layers)
    scratch = [
        pltpu.VMEM((2,) + weights[0].shape, BF), pltpu.VMEM((2,) + weights[1].shape, BF),
        pltpu.VMEM((ff, width), BF), pltpu.VMEM((rows, width), F32), pltpu.VMEM((rows, width), BF),
        pltpu.VMEM((128, rows), BF), pltpu.VMEM((2,) + grad_shape, BF),
        pltpu.VMEM((rows, width), BF), pltpu.VMEM((rows, width), BF),
        pltpu.VMEM((rows, 3 * width), BF), pltpu.VMEM((rows, width), BF),
        pltpu.SemaphoreType.DMA((48,))]
    scratch += [pltpu.VMEM(x.shape[1:], x.dtype) for x in tuple(saved_a) + tuple(saved_f)]
    res = run(
        body, [(src, SMEM), (dy, ANY), (small, VMEM), (down, ANY)] + weight_ins(weights)
        + [(x, ANY) for x in tuple(saved_a) + tuple(saved_f)], outs, scratch, "backward", 60)
    return res[0], res[1:]


def settle(x):
    def body(ins, outs, scratch):
        buf, sems = scratch
        loads = [pltpu.make_async_copy(ins[0].at[i], buf.at[i], sems.at[i])
                 for i in range(x.shape[0])]
        stores = [pltpu.make_async_copy(buf.at[i], outs[0].at[i], sems.at[i])
                  for i in range(x.shape[0])]
        for load in loads:
            load.start()
        for load, store in zip(loads, stores):
            load.wait()
            store.start()
        for store in stores:
            store.wait()

    return run(body, [(x, ANY)], [(like(x.shape), ANY)],
               [pltpu.VMEM(x.shape, BF), pltpu.SemaphoreType.DMA((x.shape[0],))], "settle", 3)[0]


def per_device(tokens, cotangent, segment_ids, slabs, ffn_down,
               ad_down, ad_down_bias, ad_up, ad_up_bias, ln_gain, ln_bias):
    n_section, n_group = lax.axis_size("section"), lax.axis_size("group")
    s, group, core = (lax.axis_index(name) for name in ("section", "group", "core"))
    n_micro, rows_dev, width = tokens.shape
    adapt = ad_down.shape[2]
    sections = range(n_section)

    def sect(x, apart):
        return lax.ppermute(x, "section", [(i, i ^ apart) for i in sections])

    def peer(x):
        return lax.ppermute(x, "core", [(0, 1), (1, 0)])

    def by_core(x, apart):
        pairs = [(i * GROUP + c, (i ^ apart[c]) * GROUP + c) for i in sections for c in range(GROUP)]
        return lax.ppermute(x, ("section", "core"), pairs)

    slab = slabs[0]
    half = slab.shape[0] // GROUP
    mats = jnp.concatenate([ad_down[0].T, ad_up[0]], axis=0).astype(BF)
    own_pack = jnp.concatenate([mats[i : i + EXTRA] for i in range(0, 2 * adapt, EXTRA)], axis=1)
    own_small = jnp.concatenate([jnp.pad(ad_down_bias, ((0, 0), (0, width - adapt))), ad_up_bias,
                                 ln_gain, ln_bias, jnp.zeros((4, width), F32)], axis=0)
    small = [own_small] + [sect(own_small, d) for d in range(1, n_section)]
    size = own_pack.shape[0] // GROUP
    plane = group % 2
    pack_half = lax.dynamic_slice_in_dim(own_pack, core * size, size, 0)
    quarter = lax.dynamic_slice_in_dim(slab, core * half + plane * (half // 2), half // 2, 0)
    given = jnp.concatenate([lax.dynamic_slice_in_dim(slab, core * half, half, 0), pack_half],
                            axis=0)
    own_micro = s * GROUP + core
    peer_micro = s * GROUP + 1 - core

    def gather_item(x):
        mine = lax.dynamic_index_in_dim(x, own_micro, 0, keepdims=False)
        given = lax.dynamic_index_in_dim(x, peer_micro, 0, keepdims=False)
        return jnp.concatenate([mine, peer(given)], axis=0)

    hidden = gather_item(tokens)
    cot = gather_item(cotangent)
    second = by_core(given, (2, 1))
    first = by_core(jnp.concatenate([quarter, pack_half], axis=0), (1, 2))
    second, first, hidden, cot, *small = lax.optimization_barrier(
        (second, first, hidden, cot, *small))
    first_z = lax.ppermute(first, "group", [(i, i ^ 1) for i in range(n_group)])
    third = by_core(second, (1, 2))
    bufs = [(first, first_z), (second,), (third,)]
    bufs += [tuple(peer(x) for x in parts) for parts in bufs]
    small = jnp.stack(small)

    item_start = group * GROUP * rows_dev
    seg = jnp.concatenate([
        lax.dynamic_slice(segment_ids, (own_micro, item_start + c * rows_dev), (1, rows_dev))[0]
        for c in (core, 1 - core)])

    def source(b):
        d = s ^ b
        at = []
        for h in range(GROUP):
            i = jnp.where(d == 3, 3, jnp.where((d == 1) == (h == 0), 1, 2))
            at.append(jnp.where(d == 0, 0, jnp.where(core == h, i, i + 3)))
        return jnp.stack(at + [d, core, plane]).astype(jnp.int32)

    src = jnp.stack([source(b) for b in sections])
    weights = (slab, own_pack, bufs)

    def to_owners(x):
        return lax.all_to_all(x, ("section", "core"), 0, 0, tiled=True)

    saved, sent = forward(hidden, seg, src, weights, small, ffn_down, adapt)
    block_outputs = to_owners(sent)
    leaving, grads = backward(cot, saved, src, weights, small, ffn_down, adapt)
    block_outputs, leaving, *grads = lax.optimization_barrier((block_outputs, leaving, *grads))
    block_outputs = settle(block_outputs)

    coming = [sect(grads[d], d) for d in range(1, n_section)]
    *coming, leaving = lax.optimization_barrier((*coming, leaving))
    total = grads[0].astype(F32)
    for part in coming:
        total = total + part.astype(F32)
    total = total.astype(BF)
    input_grads = settle(to_owners(leaving))
    total = (total.astype(F32) + peer(total).astype(F32)).astype(BF)
    apart = 1
    while apart < n_group:
        other = lax.ppermute(total, "group", [(i, i ^ apart) for i in range(n_group)])
        total = (total.astype(F32) + other.astype(F32)).astype(BF)
        apart *= 2
    total = total.astype(F32)
    return (block_outputs[None], input_grads[None], total[:adapt].T[None],
            total[2 * adapt + 3, :adapt][None], total[adapt : 2 * adapt][None],
            total[2 * adapt][None], total[2 * adapt + 1][None], total[2 * adapt + 2][None])


def solution(mesh):
    n_section, n_rows = mesh.devices.shape
    cores = Mesh(mesh.devices.reshape(n_section, n_rows // GROUP, GROUP),
                 ("section", "group", "core"))
    rows = ("group", "core")
    in_specs = (
        P(None, rows, None), P(None, rows, None), P(), P("section", None, None), P(),
        P("section", None, None), P("section", None), P("section", None, None),
        P("section", None), P("section", None), P("section", None),
    )
    out_specs = (
        P("section", None, rows, None), P("section", None, rows, None),
        P("section", None, None), P("section", None), P("section", None, None),
        P("section", None), P("section", None), P("section", None),
    )
    return jax.shard_map(
        per_device, mesh=cores, in_specs=in_specs, out_specs=out_specs, check_vma=False
    )
```

```python
import jax
import jax.numpy as jnp
from jax import lax
from jax.experimental import pallas as pl
from jax.experimental.pallas import tpu as pltpu
from jax.sharding import Mesh, PartitionSpec as P

HEADS = 12
GROUP = 2
PARTS = 4
EXTRA = 32
SUMS = 16
COST = 1e8
BF = jnp.bfloat16
F32 = jnp.float32
VMEM = pl.BlockSpec(memory_space=pltpu.VMEM)
ANY = pl.BlockSpec(memory_space=pl.ANY)
SMEM = pl.BlockSpec(memory_space=pltpu.SMEM)
LIMIT = 56 * 1024 * 1024


def dot(left, right):
    return jnp.dot(left, right, preferred_element_type=F32)


def dot_t(left, right):
    return lax.dot_general(left, right, (((1,), (1,)), ((), ())), preferred_element_type=F32)


def gelu_pair(x):
    size = jnp.abs(x)
    base = 1.0 + 0.23164188 * size
    t = 1.0 / base
    poly = 0.127414796 + t * (-0.142248368 + t * (0.710706871 + t * (
        -0.726576014 + t * 0.530702715)))
    bell = jnp.exp2(-0.7213475204444817 * (x * x))
    tail = (t * poly) * bell
    phi = jnp.where(x < 0, tail, 1.0 - tail)
    return x * phi, phi + x * (0.3989422804014327 * bell)


def like(shape, dtype=BF):
    return jax.ShapeDtypeStruct(shape, dtype)


def run(body, ins, outs, scratch, name, micros):
    n_in, n_out = len(ins), len(outs)

    def wrapped(*refs):
        body(refs[:n_in], refs[n_in : n_in + n_out], refs[n_in + n_out :])

    return pl.pallas_call(
        wrapped,
        out_shape=[shape for shape, _ in outs],
        in_specs=[spec for _, spec in ins],
        out_specs=[spec for _, spec in outs],
        scratch_shapes=scratch,
        name=name,
        cost_estimate=pl.CostEstimate(flops=int(micros * COST), bytes_accessed=0, transcendentals=0),
        compiler_params=pltpu.CompilerParams(vmem_limit_bytes=LIMIT),
    )(*[array for array, _ in ins])


class Group:
    def __init__(self, sems, count):
        self.sems, self.first, self.pairs = sems, sems.used, []
        sems.used += count

    def start(self, *pairs):
        for i, (source, target) in enumerate(pairs):
            pltpu.make_async_copy(source, target, self.sems.ref.at[self.first + i]).start()

    def wait(self, *pairs):
        for i, (source, target) in enumerate(pairs):
            pltpu.make_async_copy(source, target, self.sems.ref.at[self.first + i]).wait()


class Sems:
    def __init__(self, ref):
        self.ref, self.used = ref, 0

    def run(self, count):
        self.used += count
        return self.ref.at[pl.ds(self.used - count, count)]


def load_slab(sems, src, block, weights, slab_v, order=range(PARTS)):
    own, own_pack, bufs = weights
    rows = own.shape[0] // GROUP
    plane = src[block, GROUP + 2]
    for h in range(GROUP):
        for i, parts in enumerate([(own,)] + list(bufs)):
            size = rows // len(parts)

            @pl.when(src[block, h] == i)
            def _():
                for p in order:
                    columns = pl.ds(p * (own.shape[1] // PARTS), own.shape[1] // PARTS)
                    for n, buf in enumerate(parts):
                        first = h * rows if i == 0 else 0
                        to = h * rows
                        if len(parts) > 1:
                            to += size * (plane if n == 0 else 1 - plane)
                        pltpu.make_async_copy(
                            buf.at[pl.ds(first, size), columns],
                            slab_v.at[pl.ds(pl.multiple_of(to, 64), size), columns],
                            sems.at[p]).start()


def slab_part(sems, weights, slab_v, p):
    own = weights[0]
    columns = part_of(own.shape[1], p)
    pltpu.make_async_copy(own.at[:, columns], slab_v.at[:, columns], sems.at[p]).wait()


def load_down(sems, down, layer, down_v, p):
    rows = pl.ds(p * (down_v.shape[0] // PARTS), down_v.shape[0] // PARTS)
    pltpu.make_async_copy(down.at[layer, rows], down_v.at[rows], sems.at[p]).start()


def down_part(sems, down, down_v, p):
    rows = part_of(down_v.shape[0], p)
    pltpu.make_async_copy(down.at[0, rows], down_v.at[rows], sems.at[p]).wait()


def load_pack(sem, src, block, weights, pack_v):
    own, own_pack, bufs = weights
    rows = own.shape[0] // GROUP
    size = own_pack.shape[0] // GROUP
    for h in range(GROUP):
        at = pl.ds(h * size, size)
        for i, parts in enumerate([(own_pack,)] + list(bufs)):
            buf = parts[0]
            first = h * size if i == 0 else rows // len(parts)

            @pl.when(src[block, h] == i)
            def _():
                pltpu.make_async_copy(buf.at[pl.ds(first, size)], pack_v.at[at], sem).start()


def send_grads(sem, value_ref, apart, outs):
    for d, out in enumerate(outs):
        @pl.when(apart == d)
        def _():
            pltpu.make_async_copy(value_ref, out, sem).start()


def row_copies(value_ref, block, core, out, sem):
    half = value_ref.shape[0] // GROUP
    return [pltpu.make_async_copy(
        value_ref.at[pl.ds(i * half, half)],
        out.at[GROUP * block + (core if i == 0 else GROUP - 1 - core)], sem) for i in range(GROUP)]


def adapters(pack, width, adapt):
    rows = [pack[:, i * width : (i + 1) * width] for i in range(2 * adapt // EXTRA)]
    zeros = jnp.zeros((128 - adapt, width), BF)
    per = adapt // EXTRA
    down_t = jnp.concatenate(rows[:per] + [zeros], axis=0)
    up = jnp.concatenate(rows[per:] + [zeros], axis=0)
    return down_t, up


def post_forward(pack, small, x_ref, b_ref, y_ref, saved, adapt):
    low_ref, ut_ref, slope_ref, zhat_ref, rstd_ref = saved
    rows, width = x_ref.shape
    down_t, up = adapters(pack, width, adapt)
    down_bias, up_bias, gain, bias = [small[i : i + 1, :] for i in range(4)]
    step = 512

    def body(i, carry):
        at = pl.ds(pl.multiple_of(i * step, step), step)
        branch = b_ref[at, :]
        low = branch.astype(BF)
        low_ref[at, :] = low
        pre = dot_t(low, down_t) + down_bias[:, :128]
        inner, slope = gelu_pair(pre)
        slope_ref[at, :] = slope
        ut_ref[:, at] = inner.T.astype(BF)
        mixed = x_ref[at, :].astype(F32) + branch + dot(inner.astype(BF), up) + up_bias
        center = mixed - jnp.mean(mixed, axis=-1, keepdims=True)
        rstd = lax.rsqrt(jnp.mean(center * center, axis=-1, keepdims=True) + 1e-05)
        zhat = center * rstd
        y_ref[at, :] = (zhat * gain + bias).astype(BF)
        zhat_ref[at, :] = zhat.astype(BF)
        rstd_ref[at, :] = jnp.broadcast_to(rstd, (step, 128))
        return carry

    lax.fori_loop(0, rows // step, body, 0)


def post_backward(pack, small, dy_ref, saved, dz_ref, db_ref, grads_ref, dpt_ref, adapt):
    low_ref, ut_ref, slope_ref, zhat_ref, rstd_ref = saved
    rows, width = dy_ref.shape
    down_t, up = adapters(pack, width, adapt)
    gain = small[2:3, :]
    step = 512

    def fold(v):
        return jnp.sum(v.reshape(v.shape[0] // 8, 8, v.shape[1]), axis=0)

    def body(i, carry):
        s_bias, s_gain, s_upb, s_downb = carry
        at = pl.ds(pl.multiple_of(i * step, step), step)
        d_out = dy_ref[at, :].astype(F32)
        zhat = zhat_ref[at, :].astype(F32)
        s_bias = s_bias + fold(d_out)
        s_gain = s_gain + fold(d_out * zhat)
        dz = d_out * gain
        dz = rstd_ref[at, :1] * (dz - jnp.mean(dz, axis=-1, keepdims=True)
                                 - zhat * jnp.mean(dz * zhat, axis=-1, keepdims=True))
        s_upb = s_upb + fold(dz)
        low = dz.astype(BF)
        db_ref[at, :] = low
        d_pre = dot_t(low, up) * slope_ref[at, :]
        s_downb = s_downb + fold(d_pre)
        dpt_ref[:, at] = d_pre.T.astype(BF)
        dz_ref[at, :] = dz
        return s_bias, s_gain, s_upb, s_downb

    zero = jnp.zeros((8, width), F32)
    s_bias, s_gain, s_upb, s_downb = lax.fori_loop(
        0, rows // step, body, (zero, zero, zero, jnp.zeros((8, 128), F32)))
    g_down = dot(dpt_ref[...], low_ref[...])
    g_up = dot(ut_ref[...], db_ref[...])
    grads_ref[0:adapt, :] = g_down[:adapt].astype(BF)
    grads_ref[adapt : 2 * adapt, :] = g_up[:adapt].astype(BF)
    tail = jnp.concatenate(
        [jnp.sum(v, axis=0, keepdims=True) for v in (s_upb, s_gain, s_bias)]
        + [jnp.concatenate([jnp.sum(s_downb, axis=0, keepdims=True),
                            jnp.zeros((1, width - 128), F32)], axis=1),
           jnp.zeros((SUMS - 4, width), F32)], axis=0)
    grads_ref[2 * adapt :, :] = tail.astype(BF)

    def body2(i, carry):
        at = pl.ds(pl.multiple_of(i * step, step), step)
        d_pre = dpt_ref[:, at].astype(F32).T.astype(BF)
        db_ref[at, :] = (dz_ref[at, :] + dot(d_pre, down_t)).astype(BF)
        return carry

    lax.fori_loop(0, rows // step, body2, 0)


def tile(i, size):
    return pl.ds(pl.multiple_of(i * size, size), size)


def part_of(size, i):
    return tile(i, size // PARTS)


def ffn_branch(x_ref, slab, down, slope_ref, acc, ready, step=256):
    size = slab.shape[1] // PARTS
    before = None
    for i in range(PARTS + 1):
        if i < PARTS:
            ready(i)
            acts = []
            for j in range(size // step):
                cols = slice(i * size + j * step, i * size + (j + 1) * step)
                values, slope = gelu_pair(dot(x_ref[...], slab[:, cols]))
                slope_ref[:, cols] = slope.astype(BF)
                acts.append(values.astype(BF))
        if i == 1:
            acc[...] = dot(before, down[:size, :])
        elif i > 1:
            acc[...] += dot(before, down[(i - 1) * size : i * size, :])
        before = jnp.concatenate(acts, axis=1)


def ffn_branch_back(db, slab, down, slope_ref, acc, ready, step=256):
    size = slab.shape[1] // PARTS

    def part(i, carry):
        ready(i)
        df, before = None, None
        for j in range(size // step):
            cols = pl.ds(pl.multiple_of(i * size + j * step, step), step)
            dg = dot_t(db[...], down[cols, :])
            if df is not None:
                acc[...] += dot_t(df, slab[:, before])
            df, before = (dg * slope_ref[:, cols].astype(F32)).astype(BF), cols
        acc[...] += dot_t(df, slab[:, before])
        return carry

    lax.fori_loop(0, PARTS, part, 0, unroll=2)


def project(x_ref, slab, qkv_ref, ready, step=256):
    width = x_ref.shape[1]

    def part(i, carry):
        ready(i)
        scale = jnp.where(i == 0, (width // HEADS) ** -0.5, 1.0)
        for j in range(width // step):
            cols = pl.ds(pl.multiple_of(i * width + j * step, step), step)
            qkv_ref[:, cols] = (dot(x_ref[...], slab[:, cols]) * scale).astype(BF)
        return carry

    lax.fori_loop(0, 3, part, 0)


def attend(qkv_ref, bias_v, p_v, c_ref):
    rows, width = c_ref.shape
    head = width // HEADS
    lower = lax.broadcasted_iota(jnp.int32, (rows, 2 * head), 1) < head

    def body(i, carry):
        def part(n):
            return qkv_ref[:, pl.ds(pl.multiple_of(n * width + i * 2 * head, 2 * head), 2 * head)]

        q, k, v = part(0), part(1), part(2)
        parts = []
        for h in range(2):
            q_h = jnp.where(lower == (h == 0), q, jnp.zeros_like(q))
            s = dot_t(q_h, k) + bias_v[...]
            e = jnp.exp(s - jnp.max(s, axis=-1, keepdims=True))
            p = (e * (1.0 / jnp.sum(e, axis=-1, keepdims=True))).astype(BF)
            p_v[2 * i + h] = p
            parts.append(dot(p, v))
        c_ref[:, tile(i, 2 * head)] = jnp.where(lower, parts[0], parts[1]).astype(BF)
        return carry

    lax.fori_loop(0, HEADS // 2, body, 0, unroll=6)


def attend_back(qkv_ref, c_ref, dc_ref, p_v, dqkv):
    rows, width = c_ref.shape
    head = width // HEADS
    lower = lax.broadcasted_iota(jnp.int32, (rows, 2 * head), 1) < head

    def body(i, carry):
        def cols(n):
            return pl.ds(pl.multiple_of(n * width + i * 2 * head, 2 * head), 2 * head)

        q, k, v = qkv_ref[:, cols(0)], qkv_ref[:, cols(1)], qkv_ref[:, cols(2)]
        dc = dc_ref[:, cols(0)]
        dc_wide = dc.astype(F32)
        prod = dc_wide * c_ref[:, cols(0)].astype(F32)
        q_t = q.astype(F32).T.astype(BF)
        dc_t = dc_wide.T.astype(BF)
        dq, dk, dv = [], [], []
        for h in range(2):
            mine = lower == (h == 0)
            p = p_v[2 * i + h]
            delta = jnp.sum(jnp.where(mine, prod, 0.0), axis=-1, keepdims=True)
            dp = dot_t(jnp.where(mine, dc, jnp.zeros_like(dc)), v)
            ds = (p.astype(F32) * (dp - delta)).astype(BF)
            dq.append(dot(ds, k))
            dk.append(dot(q_t[h * head : (h + 1) * head], ds))
            dv.append(dot(dc_t[h * head : (h + 1) * head], p))
        dqkv[:, cols(0)] = (jnp.where(lower, dq[0], dq[1]) * head ** -0.5).astype(BF)
        dqkv[:, cols(1)] = jnp.concatenate(dk, axis=0).T.astype(BF)
        dqkv[:, cols(2)] = jnp.concatenate(dv, axis=0).T.astype(BF)
        return carry

    lax.fori_loop(0, HEADS // 2, body, 0, unroll=6)


def by_columns(target, value, step=256):
    for j in range(target.shape[1] // step):
        cols = slice(j * step, (j + 1) * step)
        target[:, cols] = value(cols).astype(target.dtype)


def post_saved(rows, width):
    return [((rows, width), BF), ((128, rows), BF), ((rows, 128), F32), ((rows, width), BF),
            ((rows, 128), F32)]


def block_saved(block, rows, width, ff):
    if block % 2 == 0:
        first = [((rows, 3 * width), BF), ((rows, width), BF), ((HEADS, rows, rows), BF)]
    else:
        first = [((rows, ff), BF)]
    return first + post_saved(rows, width)


def weight_ins(weights):
    own, own_pack, bufs = weights
    return [(own, ANY), (own_pack, ANY)] + [(x, ANY) for parts in bufs for x in parts]


def weight_refs(refs, weights):
    refs, parts = list(refs), []
    for group in weights[2]:
        parts.append(tuple(refs[2 + sum(map(len, parts)) :][: len(group)]))
    return refs[0], refs[1], parts


def forward(x, seg, src, weights, small, down, adapt):
    rows, width = x.shape
    ff = weights[0].shape[1]
    layers = down.shape[0]
    n_w = len(weight_ins(weights))
    shapes = [block_saved(b, rows, width, ff) for b in range(2)]
    n_a = len(shapes[0])

    def body(ins, outs, scratch):
        src_ref, x_ref, segc_ref, segr_ref, small_ref, down_ref = ins[:6]
        wts = weight_refs(ins[6 : 6 + n_w], weights)
        out_a, out_f, sent = outs[:n_a], outs[n_a:-1], outs[-1]
        slabs, packs, down_v, y_v, acc, bias_v, sem_ref = scratch[:7]
        buf_a, buf_f = scratch[7 : 7 + n_a], scratch[7 + n_a :]
        sems = Sems(sem_ref)
        slab_sems = [sems.run(PARTS) for b in range(2)]
        down_sems, pack_sem = sems.run(PARTS), sems.run(1).at[0]
        group_a, group_f = Group(sems, n_a), Group(sems, len(buf_f) - 1)
        group_slope = Group(sems, 1)
        rows_sems = sems.run(2)
        core = src_ref[0, GROUP + 1]

        load_slab(slab_sems[0], src_ref, 0, wts, slabs.at[0])
        for b in range(2 * layers):
            load_pack(pack_sem, src_ref, b, wts, packs.at[b])
        bias_v[...] = jnp.where(segc_ref[...] == segr_ref[...], 0.0, -1e30)
        y_v[1] = x_ref[...]
        for b in range(2 * layers):
            pltpu.make_async_copy(wts[1], packs.at[b], pack_sem).wait()

        def save_a(layer):
            return [(buf, out.at[layer]) for buf, out in zip(buf_a, out_a)]

        def save_f(layer):
            return [(buf, out.at[layer]) for buf, out in zip(buf_f, out_f)]

        def wait_rows(i):
            for copy in row_copies(y_v.at[i], 0, 0, sent, rows_sems.at[i]):
                copy.wait()

        def layer_step(layer, carry):
            b = 2 * layer
            slab = slabs.at[0]

            @pl.when(layer > 0)
            def _():
                group_a.wait(*save_a(0))
                wait_rows(0)

            qkv, ctx, probs = buf_a[:3]
            project(y_v.at[1], slab, qkv, lambda i: slab_part(slab_sems[0], wts, slab, i))
            slab_part(slab_sems[0], wts, slab, PARTS - 1)
            for p in range(PARTS):
                load_slab(slab_sems[1], src_ref, b + 1, wts, slabs.at[1], [p])
                load_down(down_sems, down_ref, layer, down_v, p)
            attend(qkv, bias_v, probs, ctx)
            by_columns(acc, lambda cols: dot(
                ctx[...], slab[:, 3 * width + cols.start : 3 * width + cols.stop]))

            @pl.when(layer + 1 < layers)
            def _():
                load_slab(slab_sems[0], src_ref, b + 2, wts, slab)

            post_forward(packs.at[b], small_ref.at[src_ref[b, GROUP]], y_v.at[1], acc, y_v.at[0],
                         buf_a[3:], adapt)
            for copy in row_copies(y_v.at[0], b, core, sent, rows_sems.at[0]):
                copy.start()
            group_a.start(*save_a(layer))

            @pl.when(layer > 0)
            def _():
                group_slope.wait(save_f(0)[0])
                group_f.wait(*save_f(0)[1:])
                wait_rows(1)

            def ready(i):
                slab_part(slab_sems[1], wts, slabs.at[1], i)
                down_part(down_sems, down_ref, down_v, i)

            ffn_branch(y_v.at[0], slabs.at[1], down_v, buf_f[0], acc, ready)
            group_slope.start(save_f(layer)[0])
            post_forward(packs.at[b + 1], small_ref.at[src_ref[b + 1, GROUP]], y_v.at[0], acc,
                         y_v.at[1], buf_f[1:], adapt)
            for copy in row_copies(y_v.at[1], b + 1, core, sent, rows_sems.at[1]):
                copy.start()
            group_f.start(*save_f(layer)[1:])
            return carry

        lax.fori_loop(0, layers, layer_step, 0)
        group_a.wait(*save_a(0))
        group_slope.wait(save_f(0)[0])
        group_f.wait(*save_f(0)[1:])
        for i in range(2):
            wait_rows(i)

    outs = [(like((layers,) + sh, dt), ANY) for b in range(2) for sh, dt in shapes[b]]
    outs.append((like((2 * layers * GROUP, rows // GROUP, width)), ANY))
    scratch = [
        pltpu.VMEM((2,) + weights[0].shape, BF),
        pltpu.VMEM((2 * layers,) + weights[1].shape, BF),
        pltpu.VMEM((ff, width), BF), pltpu.VMEM((2, rows, width), BF),
        pltpu.VMEM((rows, width), F32), pltpu.VMEM((rows, rows), F32),
        pltpu.SemaphoreType.DMA((48,))]
    for b in range(2):
        scratch += [pltpu.VMEM(sh, dt) for sh, dt in shapes[b]]
    res = run(
        body, [(src, SMEM), (x, VMEM), (seg[:, None], VMEM), (seg[None, :], VMEM), (small, VMEM),
               (down, ANY)] + weight_ins(weights), outs, scratch, "forward", 60)
    return (res[:n_a], res[n_a:-1]), res[-1]


def backward(dy, saved, src, weights, small, down, adapt):
    rows, width = dy.shape
    ff = weights[0].shape[1]
    layers = down.shape[0]
    n_w = len(weight_ins(weights))
    saved_a, saved_f = saved
    n_a, n_f = len(saved_a), len(saved_f)

    def body(ins, outs, scratch):
        src_ref, dy_ref, small_ref, down_ref = ins[:4]
        wts = weight_refs(ins[4 : 4 + n_w], weights)
        in_a, in_f = ins[4 + n_w : 4 + n_w + n_a], ins[4 + n_w + n_a :]
        sent, grads_out = outs[0], outs[1:]
        slabs, packs, down_v, acc, db, dpt, grads, dx_v, dc_v, dqkv, dy_v, sem_ref = scratch[:12]
        buf_a, buf_f = scratch[12 : 12 + n_a], scratch[12 + n_a :]
        sems = Sems(sem_ref)
        slab_sems = [sems.run(PARTS) for i in range(2)]
        down_sems, slope_sems, pack_sems = sems.run(PARTS), sems.run(PARTS), sems.run(2)
        group_a, post_a = Group(sems, 3), Group(sems, n_a - 3)
        post_f, group_dy = Group(sems, n_f - 1), Group(sems, 1)
        rows_sems, grads_sems = sems.run(2), sems.run(2)
        core = src_ref[0, GROUP + 1]

        def pairs(refs, bufs, layer):
            return [(x.at[layer], buf) for x, buf in zip(refs, bufs)]

        def slope_part(layer, p):
            columns = part_of(ff, p)
            return pltpu.make_async_copy(in_f[0].at[layer, :, columns], buf_f[0].at[:, columns],
                                         slope_sems.at[p])

        def fetch_f(layer):
            b = 2 * layer + 1
            post_f.start(*pairs(in_f[1:], buf_f[1:], layer))
            load_pack(pack_sems.at[0], src_ref, b, wts, packs.at[0])
            for p in range(PARTS):
                load_down(down_sems, down_ref, layer, down_v, p)
                slope_part(layer, p).start()
                load_slab(slab_sems[0], src_ref, b, wts, slabs.at[0], [p])

        def wait_pack(i):
            pltpu.make_async_copy(wts[1], packs.at[i], pack_sems.at[i]).wait()

        def wait_sent(i, value_ref):
            for copy in row_copies(value_ref, 0, 0, sent, rows_sems.at[i]):
                copy.wait()
            pltpu.make_async_copy(grads.at[i], grads_out[0], grads_sems.at[i]).wait()

        group_dy.start((dy_ref, dy_v))
        fetch_f(layers - 1)
        group_dy.wait((dy_ref, dy_v))

        def layer_step(count, carry):
            layer = layers - 1 - count
            b = 2 * layer + 1

            @pl.when(count > 0)
            def _():
                wait_sent(0, dx_v)

            post_f.wait(*pairs(in_f[1:], buf_f[1:], 0))
            wait_pack(0)
            post_backward(packs.at[0], small_ref.at[src_ref[b, GROUP]], dy_v, buf_f[1:], acc, db,
                          grads.at[0], dpt, adapt)
            send_grads(grads_sems.at[0], grads.at[0], src_ref[b, GROUP], grads_out)
            load_pack(pack_sems.at[1], src_ref, b - 1, wts, packs.at[1])
            post_a.start(*pairs(in_a[3:], buf_a[3:], layer))
            load_slab(slab_sems[1], src_ref, b - 1, wts, slabs.at[1], [PARTS - 1])
            group_a.start(*pairs(in_a[:3], buf_a[:3], layer))
            load_slab(slab_sems[1], src_ref, b - 1, wts, slabs.at[1], range(PARTS - 1))

            def ready(i):
                slab_part(slab_sems[0], wts, slabs.at[0], i)
                down_part(down_sems, down_ref, down_v, i)
                slope_part(0, i).wait()

            ffn_branch_back(db, slabs.at[0], down_v, buf_f[0], acc, ready)
            dx_v[...] = acc[...].astype(BF)
            for copy in row_copies(dx_v, b, core, sent, rows_sems.at[0]):
                copy.start()

            @pl.when(count > 0)
            def _():
                wait_sent(1, dy_v)

            post_a.wait(*pairs(in_a[3:], buf_a[3:], 0))
            wait_pack(1)

            @pl.when(layer > 0)
            def _():
                fetch_f(layer - 1)

            post_backward(packs.at[1], small_ref.at[src_ref[b - 1, GROUP]], dx_v, buf_a[3:], acc,
                          db, grads.at[1], dpt, adapt)
            send_grads(grads_sems.at[1], grads.at[1], src_ref[b - 1, GROUP], grads_out)
            slab = slabs.at[1]
            slab_part(slab_sems[1], wts, slab, PARTS - 1)
            by_columns(dc_v, lambda cols: dot_t(db[...], slab[cols, 3 * width :]))
            group_a.wait(*pairs(in_a[:3], buf_a[:3], 0))
            attend_back(buf_a[0], buf_a[1], dc_v, buf_a[2], dqkv)
            for i in range(PARTS - 1):
                slab_part(slab_sems[1], wts, slab, i)
            by_columns(dy_v, lambda cols: acc[:, cols] + dot_t(dqkv[...], slab[cols, : 3 * width]))
            for copy in row_copies(dy_v, b - 1, core, sent, rows_sems.at[1]):
                copy.start()
            return carry

        lax.fori_loop(0, layers, layer_step, 0)
        wait_sent(0, dx_v)
        wait_sent(1, dy_v)

    grad_shape = (2 * adapt + SUMS, width)
    outs = [(like((2 * layers * GROUP, rows // GROUP, width)), ANY)]
    outs += [(like(grad_shape), ANY)] * (2 * layers)
    scratch = [
        pltpu.VMEM((2,) + weights[0].shape, BF), pltpu.VMEM((2,) + weights[1].shape, BF),
        pltpu.VMEM((ff, width), BF), pltpu.VMEM((rows, width), F32), pltpu.VMEM((rows, width), BF),
        pltpu.VMEM((128, rows), BF), pltpu.VMEM((2,) + grad_shape, BF),
        pltpu.VMEM((rows, width), BF), pltpu.VMEM((rows, width), BF),
        pltpu.VMEM((rows, 3 * width), BF), pltpu.VMEM((rows, width), BF),
        pltpu.SemaphoreType.DMA((48,))]
    scratch += [pltpu.VMEM(x.shape[1:], x.dtype) for x in tuple(saved_a) + tuple(saved_f)]
    res = run(
        body, [(src, SMEM), (dy, ANY), (small, VMEM), (down, ANY)] + weight_ins(weights)
        + [(x, ANY) for x in tuple(saved_a) + tuple(saved_f)], outs, scratch, "backward", 60)
    return res[0], res[1:]


def settle(x):
    def body(ins, outs, scratch):
        buf, sems = scratch
        loads = [pltpu.make_async_copy(ins[0].at[i], buf.at[i], sems.at[i])
                 for i in range(x.shape[0])]
        stores = [pltpu.make_async_copy(buf.at[i], outs[0].at[i], sems.at[i])
                  for i in range(x.shape[0])]
        for load in loads:
            load.start()
        for load, store in zip(loads, stores):
            load.wait()
            store.start()
        for store in stores:
            store.wait()

    return run(body, [(x, ANY)], [(like(x.shape), ANY)],
               [pltpu.VMEM(x.shape, BF), pltpu.SemaphoreType.DMA((x.shape[0],))], "settle", 3)[0]


def per_device(tokens, cotangent, segment_ids, slabs, ffn_down,
               ad_down, ad_down_bias, ad_up, ad_up_bias, ln_gain, ln_bias):
    n_section, n_group = lax.axis_size("section"), lax.axis_size("group")
    s, group, core = (lax.axis_index(name) for name in ("section", "group", "core"))
    n_micro, rows_dev, width = tokens.shape
    adapt = ad_down.shape[2]
    sections = range(n_section)

    def sect(x, apart):
        return lax.ppermute(x, "section", [(i, i ^ apart) for i in sections])

    def peer(x):
        return lax.ppermute(x, "core", [(0, 1), (1, 0)])

    def by_core(x, apart):
        pairs = [(i * GROUP + c, (i ^ apart[c]) * GROUP + c) for i in sections for c in range(GROUP)]
        return lax.ppermute(x, ("section", "core"), pairs)

    slab = slabs[0]
    half = slab.shape[0] // GROUP
    mats = jnp.concatenate([ad_down[0].T, ad_up[0]], axis=0).astype(BF)
    own_pack = jnp.concatenate([mats[i : i + EXTRA] for i in range(0, 2 * adapt, EXTRA)], axis=1)
    own_small = jnp.concatenate([jnp.pad(ad_down_bias, ((0, 0), (0, width - adapt))), ad_up_bias,
                                 ln_gain, ln_bias, jnp.zeros((4, width), F32)], axis=0)
    small = [own_small] + [sect(own_small, d) for d in range(1, n_section)]
    size = own_pack.shape[0] // GROUP
    plane = group % 2
    pack_half = lax.dynamic_slice_in_dim(own_pack, core * size, size, 0)
    quarter = lax.dynamic_slice_in_dim(slab, core * half + plane * (half // 2), half // 2, 0)
    given = jnp.concatenate([lax.dynamic_slice_in_dim(slab, core * half, half, 0), pack_half],
                            axis=0)
    own_micro = s * GROUP + core
    peer_micro = s * GROUP + 1 - core

    def gather_item(x):
        mine = lax.dynamic_index_in_dim(x, own_micro, 0, keepdims=False)
        given = lax.dynamic_index_in_dim(x, peer_micro, 0, keepdims=False)
        return jnp.concatenate([mine, peer(given)], axis=0)

    hidden = gather_item(tokens)
    cot = gather_item(cotangent)
    second = by_core(given, (2, 1))
    first = by_core(jnp.concatenate([quarter, pack_half], axis=0), (1, 2))
    second, first, hidden, cot, *small = lax.optimization_barrier(
        (second, first, hidden, cot, *small))
    first_z = lax.ppermute(first, "group", [(i, i ^ 1) for i in range(n_group)])
    third = by_core(second, (1, 2))
    bufs = [(first, first_z), (second,), (third,)]
    bufs += [tuple(peer(x) for x in parts) for parts in bufs]
    small = jnp.stack(small)

    item_start = group * GROUP * rows_dev
    seg = jnp.concatenate([
        lax.dynamic_slice(segment_ids, (own_micro, item_start + c * rows_dev), (1, rows_dev))[0]
        for c in (core, 1 - core)])

    def source(b):
        d = s ^ b
        at = []
        for h in range(GROUP):
            i = jnp.where(d == 3, 3, jnp.where((d == 1) == (h == 0), 1, 2))
            at.append(jnp.where(d == 0, 0, jnp.where(core == h, i, i + 3)))
        return jnp.stack(at + [d, core, plane]).astype(jnp.int32)

    src = jnp.stack([source(b) for b in sections])
    weights = (slab, own_pack, bufs)

    def to_owners(x):
        return lax.all_to_all(x, ("section", "core"), 0, 0, tiled=True)

    saved, sent = forward(hidden, seg, src, weights, small, ffn_down, adapt)
    block_outputs = to_owners(sent)
    leaving, grads = backward(cot, saved, src, weights, small, ffn_down, adapt)
    block_outputs, leaving, *grads = lax.optimization_barrier((block_outputs, leaving, *grads))
    block_outputs = settle(block_outputs)

    coming = [sect(grads[d], d) for d in range(1, n_section)]
    *coming, leaving = lax.optimization_barrier((*coming, leaving))
    total = grads[0].astype(F32)
    for part in coming:
        total = total + part.astype(F32)
    total = total.astype(BF)
    input_grads = settle(to_owners(leaving))
    total = (total.astype(F32) + peer(total).astype(F32)).astype(BF)
    apart = 1
    while apart < n_group:
        other = lax.ppermute(total, "group", [(i, i ^ apart) for i in range(n_group)])
        total = (total.astype(F32) + other.astype(F32)).astype(BF)
        apart *= 2
    total = total.astype(F32)
    return (block_outputs[None], input_grads[None], total[:adapt].T[None],
            total[2 * adapt + 3, :adapt][None], total[adapt : 2 * adapt][None],
            total[2 * adapt][None], total[2 * adapt + 1][None], total[2 * adapt + 2][None])


def solution(mesh):
    n_section, n_rows = mesh.devices.shape
    cores = Mesh(mesh.devices.reshape(n_section, n_rows // GROUP, GROUP),
                 ("section", "group", "core"))
    rows = ("group", "core")
    in_specs = (
        P(None, rows, None), P(None, rows, None), P(), P("section", None, None), P(),
        P("section", None, None), P("section", None), P("section", None, None),
        P("section", None), P("section", None), P("section", None),
    )
    out_specs = (
        P("section", None, rows, None), P("section", None, rows, None),
        P("section", None, None), P("section", None), P("section", None, None),
        P("section", None), P("section", None), P("section", None),
    )
    return jax.shard_map(
        per_device, mesh=cores, in_specs=in_specs, out_specs=out_specs, check_vma=False
    )
```

```python
import jax
import jax.numpy as jnp
from jax import lax
from jax.experimental import pallas as pl
from jax.experimental.pallas import tpu as pltpu
from jax.sharding import Mesh, PartitionSpec as P

HEADS = 12
GROUP = 2
PARTS = 4
EXTRA = 32
SUMS = 16
COST = 1e8
BF = jnp.bfloat16
F32 = jnp.float32
VMEM = pl.BlockSpec(memory_space=pltpu.VMEM)
ANY = pl.BlockSpec(memory_space=pl.ANY)
SMEM = pl.BlockSpec(memory_space=pltpu.SMEM)
LIMIT = 56 * 1024 * 1024


def dot(left, right):
    return jnp.dot(left, right, preferred_element_type=F32)


def dot_t(left, right):
    return lax.dot_general(left, right, (((1,), (1,)), ((), ())), preferred_element_type=F32)


def gelu_pair(x):
    size = jnp.abs(x)
    base = 1.0 + 0.23164188 * size
    t = 1.0 / base
    poly = 0.127414796 + t * (-0.142248368 + t * (0.710706871 + t * (
        -0.726576014 + t * 0.530702715)))
    bell = jnp.exp2(-0.7213475204444817 * (x * x))
    tail = (t * poly) * bell
    phi = jnp.where(x < 0, tail, 1.0 - tail)
    return x * phi, phi + x * (0.3989422804014327 * bell)


def like(shape, dtype=BF):
    return jax.ShapeDtypeStruct(shape, dtype)


def run(body, ins, outs, scratch, name, micros):
    n_in, n_out = len(ins), len(outs)

    def wrapped(*refs):
        body(refs[:n_in], refs[n_in : n_in + n_out], refs[n_in + n_out :])

    return pl.pallas_call(
        wrapped,
        out_shape=[shape for shape, _ in outs],
        in_specs=[spec for _, spec in ins],
        out_specs=[spec for _, spec in outs],
        scratch_shapes=scratch,
        name=name,
        cost_estimate=pl.CostEstimate(flops=int(micros * COST), bytes_accessed=0, transcendentals=0),
        compiler_params=pltpu.CompilerParams(vmem_limit_bytes=LIMIT),
    )(*[array for array, _ in ins])


class Group:
    def __init__(self, sems, count):
        self.sems, self.first, self.pairs = sems, sems.used, []
        sems.used += count

    def start(self, *pairs):
        for i, (source, target) in enumerate(pairs):
            pltpu.make_async_copy(source, target, self.sems.ref.at[self.first + i]).start()

    def wait(self, *pairs):
        for i, (source, target) in enumerate(pairs):
            pltpu.make_async_copy(source, target, self.sems.ref.at[self.first + i]).wait()


class Sems:
    def __init__(self, ref):
        self.ref, self.used = ref, 0

    def run(self, count):
        self.used += count
        return self.ref.at[pl.ds(self.used - count, count)]


def load_slab(sems, src, block, weights, slab_v, order=range(PARTS)):
    own, own_pack, bufs = weights
    rows = own.shape[0] // GROUP
    plane = src[block, GROUP + 2]
    for h in range(GROUP):
        for i, parts in enumerate([(own,)] + list(bufs)):
            size = rows // len(parts)

            @pl.when(src[block, h] == i)
            def _():
                for p in order:
                    columns = pl.ds(p * (own.shape[1] // PARTS), own.shape[1] // PARTS)
                    for n, buf in enumerate(parts):
                        first = h * rows if i == 0 else 0
                        to = h * rows
                        if len(parts) > 1:
                            to += size * (plane if n == 0 else 1 - plane)
                        pltpu.make_async_copy(
                            buf.at[pl.ds(first, size), columns],
                            slab_v.at[pl.ds(pl.multiple_of(to, 64), size), columns],
                            sems.at[p]).start()


def slab_part(sems, weights, slab_v, p):
    own = weights[0]
    columns = part_of(own.shape[1], p)
    pltpu.make_async_copy(own.at[:, columns], slab_v.at[:, columns], sems.at[p]).wait()


def load_down(sems, down, layer, down_v, p):
    rows = pl.ds(p * (down_v.shape[0] // PARTS), down_v.shape[0] // PARTS)
    pltpu.make_async_copy(down.at[layer, rows], down_v.at[rows], sems.at[p]).start()


def down_part(sems, down, down_v, p):
    rows = part_of(down_v.shape[0], p)
    pltpu.make_async_copy(down.at[0, rows], down_v.at[rows], sems.at[p]).wait()


def load_pack(sem, src, block, weights, pack_v):
    own, own_pack, bufs = weights
    rows = own.shape[0] // GROUP
    size = own_pack.shape[0] // GROUP
    for h in range(GROUP):
        at = pl.ds(h * size, size)
        for i, parts in enumerate([(own_pack,)] + list(bufs)):
            buf = parts[0]
            first = h * size if i == 0 else rows // len(parts)

            @pl.when(src[block, h] == i)
            def _():
                pltpu.make_async_copy(buf.at[pl.ds(first, size)], pack_v.at[at], sem).start()


def send_grads(sem, value_ref, apart, outs):
    for d, out in enumerate(outs):
        @pl.when(apart == d)
        def _():
            pltpu.make_async_copy(value_ref, out, sem).start()


def row_copies(value_ref, block, core, out, sem):
    half = value_ref.shape[0] // GROUP
    return [pltpu.make_async_copy(
        value_ref.at[pl.ds(i * half, half)],
        out.at[GROUP * block + (core if i == 0 else GROUP - 1 - core)], sem) for i in range(GROUP)]


def adapters(pack, width, adapt):
    rows = [pack[:, i * width : (i + 1) * width] for i in range(2 * adapt // EXTRA)]
    zeros = jnp.zeros((128 - adapt, width), BF)
    per = adapt // EXTRA
    down_t = jnp.concatenate(rows[:per] + [zeros], axis=0)
    up = jnp.concatenate(rows[per:] + [zeros], axis=0)
    return down_t, up


def post_forward(pack, small, x_ref, b_ref, y_ref, saved, adapt):
    low_ref, ut_ref, slope_ref, zhat_ref, rstd_ref = saved
    rows, width = x_ref.shape
    down_t, up = adapters(pack, width, adapt)
    down_bias, up_bias, gain, bias = [small[i : i + 1, :] for i in range(4)]
    step = 512

    def body(i, carry):
        at = pl.ds(pl.multiple_of(i * step, step), step)
        branch = b_ref[at, :]
        low = branch.astype(BF)
        low_ref[at, :] = low
        pre = dot_t(low, down_t) + down_bias[:, :128]
        inner, slope = gelu_pair(pre)
        slope_ref[at, :] = slope
        ut_ref[:, at] = inner.T.astype(BF)
        mixed = x_ref[at, :].astype(F32) + branch + dot(inner.astype(BF), up) + up_bias
        center = mixed - jnp.mean(mixed, axis=-1, keepdims=True)
        rstd = lax.rsqrt(jnp.mean(center * center, axis=-1, keepdims=True) + 1e-05)
        zhat = center * rstd
        y_ref[at, :] = (zhat * gain + bias).astype(BF)
        zhat_ref[at, :] = zhat.astype(BF)
        rstd_ref[at, :] = jnp.broadcast_to(rstd, (step, 128))
        return carry

    lax.fori_loop(0, rows // step, body, 0)


def post_backward(pack, small, dy_ref, saved, dz_ref, db_ref, grads_ref, dpt_ref, adapt):
    low_ref, ut_ref, slope_ref, zhat_ref, rstd_ref = saved
    rows, width = dy_ref.shape
    down_t, up = adapters(pack, width, adapt)
    gain = small[2:3, :]
    step = 512

    def fold(v):
        return jnp.sum(v.reshape(v.shape[0] // 8, 8, v.shape[1]), axis=0)

    def body(i, carry):
        s_bias, s_gain, s_upb, s_downb = carry
        at = pl.ds(pl.multiple_of(i * step, step), step)
        d_out = dy_ref[at, :].astype(F32)
        zhat = zhat_ref[at, :].astype(F32)
        s_bias = s_bias + fold(d_out)
        s_gain = s_gain + fold(d_out * zhat)
        dz = d_out * gain
        dz = rstd_ref[at, :1] * (dz - jnp.mean(dz, axis=-1, keepdims=True)
                                 - zhat * jnp.mean(dz * zhat, axis=-1, keepdims=True))
        s_upb = s_upb + fold(dz)
        low = dz.astype(BF)
        db_ref[at, :] = low
        d_pre = dot_t(low, up) * slope_ref[at, :]
        s_downb = s_downb + fold(d_pre)
        dpt_ref[:, at] = d_pre.T.astype(BF)
        dz_ref[at, :] = dz
        return s_bias, s_gain, s_upb, s_downb

    zero = jnp.zeros((8, width), F32)
    s_bias, s_gain, s_upb, s_downb = lax.fori_loop(
        0, rows // step, body, (zero, zero, zero, jnp.zeros((8, 128), F32)))
    g_down = dot(dpt_ref[...], low_ref[...])
    g_up = dot(ut_ref[...], db_ref[...])
    grads_ref[0:adapt, :] = g_down[:adapt].astype(BF)
    grads_ref[adapt : 2 * adapt, :] = g_up[:adapt].astype(BF)
    tail = jnp.concatenate(
        [jnp.sum(v, axis=0, keepdims=True) for v in (s_upb, s_gain, s_bias)]
        + [jnp.concatenate([jnp.sum(s_downb, axis=0, keepdims=True),
                            jnp.zeros((1, width - 128), F32)], axis=1),
           jnp.zeros((SUMS - 4, width), F32)], axis=0)
    grads_ref[2 * adapt :, :] = tail.astype(BF)

    def body2(i, carry):
        at = pl.ds(pl.multiple_of(i * step, step), step)
        d_pre = dpt_ref[:, at].astype(F32).T.astype(BF)
        db_ref[at, :] = (dz_ref[at, :] + dot(d_pre, down_t)).astype(BF)
        return carry

    lax.fori_loop(0, rows // step, body2, 0)


def tile(i, size):
    return pl.ds(pl.multiple_of(i * size, size), size)


def part_of(size, i):
    return tile(i, size // PARTS)


def ffn_branch(x_ref, slab, down, slope_ref, acc, ready, step=256):
    size = slab.shape[1] // PARTS
    before = None
    for i in range(PARTS + 1):
        if i < PARTS:
            ready(i)
            acts = []
            for j in range(size // step):
                cols = slice(i * size + j * step, i * size + (j + 1) * step)
                values, slope = gelu_pair(dot(x_ref[...], slab[:, cols]))
                slope_ref[:, cols] = slope.astype(BF)
                acts.append(values.astype(BF))
        if i == 1:
            acc[...] = dot(before, down[:size, :])
        elif i > 1:
            acc[...] += dot(before, down[(i - 1) * size : i * size, :])
        before = jnp.concatenate(acts, axis=1)


def ffn_branch_back(db, slab, down, slope_ref, acc, ready, step=256):
    size = slab.shape[1] // PARTS

    def part(i, carry):
        ready(i)
        df, before = None, None
        for j in range(size // step):
            cols = pl.ds(pl.multiple_of(i * size + j * step, step), step)
            dg = dot_t(db[...], down[cols, :])
            if df is not None:
                acc[...] += dot_t(df, slab[:, before])
            df, before = (dg * slope_ref[:, cols].astype(F32)).astype(BF), cols
        acc[...] += dot_t(df, slab[:, before])
        return carry

    lax.fori_loop(0, PARTS, part, 0, unroll=2)


def project(x_ref, slab, qkv_ref, ready, step=256):
    width = x_ref.shape[1]

    def part(i, carry):
        ready(i)
        scale = jnp.where(i == 0, (width // HEADS) ** -0.5, 1.0)
        for j in range(width // step):
            cols = pl.ds(pl.multiple_of(i * width + j * step, step), step)
            qkv_ref[:, cols] = (dot(x_ref[...], slab[:, cols]) * scale).astype(BF)
        return carry

    lax.fori_loop(0, 3, part, 0, unroll=True)


def attend(qkv_ref, bias_v, p_v, c_ref):
    rows, width = c_ref.shape
    head = width // HEADS
    lower = lax.broadcasted_iota(jnp.int32, (rows, 2 * head), 1) < head

    def body(i, carry):
        def part(n):
            return qkv_ref[:, pl.ds(pl.multiple_of(n * width + i * 2 * head, 2 * head), 2 * head)]

        q, k, v = part(0), part(1), part(2)
        parts = []
        for h in range(2):
            q_h = jnp.where(lower == (h == 0), q, jnp.zeros_like(q))
            s = dot_t(q_h, k) + bias_v[...]
            e = jnp.exp(s - jnp.max(s, axis=-1, keepdims=True))
            p = (e * (1.0 / jnp.sum(e, axis=-1, keepdims=True))).astype(BF)
            p_v[2 * i + h] = p
            parts.append(dot(p, v))
        c_ref[:, tile(i, 2 * head)] = jnp.where(lower, parts[0], parts[1]).astype(BF)
        return carry

    lax.fori_loop(0, HEADS // 2, body, 0, unroll=6)


def attend_back(qkv_ref, c_ref, dc_ref, p_v, dqkv):
    rows, width = c_ref.shape
    head = width // HEADS
    lower = lax.broadcasted_iota(jnp.int32, (rows, 2 * head), 1) < head

    def body(i, carry):
        def cols(n):
            return pl.ds(pl.multiple_of(n * width + i * 2 * head, 2 * head), 2 * head)

        q, k, v = qkv_ref[:, cols(0)], qkv_ref[:, cols(1)], qkv_ref[:, cols(2)]
        dc = dc_ref[:, cols(0)]
        dc_wide = dc.astype(F32)
        prod = dc_wide * c_ref[:, cols(0)].astype(F32)
        q_t = q.astype(F32).T.astype(BF)
        dc_t = dc_wide.T.astype(BF)
        dq, dk, dv = [], [], []
        for h in range(2):
            mine = lower == (h == 0)
            p = p_v[2 * i + h]
            delta = jnp.sum(jnp.where(mine, prod, 0.0), axis=-1, keepdims=True)
            dp = dot_t(jnp.where(mine, dc, jnp.zeros_like(dc)), v)
            ds = (p.astype(F32) * (dp - delta)).astype(BF)
            dq.append(dot(ds, k))
            dk.append(dot(q_t[h * head : (h + 1) * head], ds))
            dv.append(dot(dc_t[h * head : (h + 1) * head], p))
        dqkv[:, cols(0)] = (jnp.where(lower, dq[0], dq[1]) * head ** -0.5).astype(BF)
        dqkv[:, cols(1)] = jnp.concatenate(dk, axis=0).T.astype(BF)
        dqkv[:, cols(2)] = jnp.concatenate(dv, axis=0).T.astype(BF)
        return carry

    lax.fori_loop(0, HEADS // 2, body, 0, unroll=3)


def by_columns(target, value, step=256):
    for j in range(target.shape[1] // step):
        cols = slice(j * step, (j + 1) * step)
        target[:, cols] = value(cols).astype(target.dtype)


def post_saved(rows, width):
    return [((rows, width), BF), ((128, rows), BF), ((rows, 128), F32), ((rows, width), BF),
            ((rows, 128), F32)]


def block_saved(block, rows, width, ff):
    if block % 2 == 0:
        first = [((rows, 3 * width), BF), ((rows, width), BF), ((HEADS, rows, rows), BF)]
    else:
        first = [((rows, ff), BF)]
    return first + post_saved(rows, width)


def weight_ins(weights):
    own, own_pack, bufs = weights
    return [(own, ANY), (own_pack, ANY)] + [(x, ANY) for parts in bufs for x in parts]


def weight_refs(refs, weights):
    refs, parts = list(refs), []
    for group in weights[2]:
        parts.append(tuple(refs[2 + sum(map(len, parts)) :][: len(group)]))
    return refs[0], refs[1], parts


def forward(x, seg, src, weights, small, down, adapt):
    rows, width = x.shape
    ff = weights[0].shape[1]
    layers = down.shape[0]
    n_w = len(weight_ins(weights))
    shapes = [block_saved(b, rows, width, ff) for b in range(2)]
    n_a = len(shapes[0])

    def body(ins, outs, scratch):
        src_ref, x_ref, segc_ref, segr_ref, small_ref, down_ref = ins[:6]
        wts = weight_refs(ins[6 : 6 + n_w], weights)
        out_a, out_f, sent = outs[:n_a], outs[n_a:-1], outs[-1]
        slabs, packs, down_v, y_v, acc, bias_v, sem_ref = scratch[:7]
        buf_a, buf_f = scratch[7 : 7 + n_a], scratch[7 + n_a :]
        sems = Sems(sem_ref)
        slab_sems = [sems.run(PARTS) for b in range(2)]
        down_sems, pack_sem = sems.run(PARTS), sems.run(1).at[0]
        group_a, group_f = Group(sems, n_a), Group(sems, len(buf_f) - 1)
        group_slope = Group(sems, 1)
        rows_sems = sems.run(2)
        core = src_ref[0, GROUP + 1]

        load_slab(slab_sems[0], src_ref, 0, wts, slabs.at[0])
        for b in range(2 * layers):
            load_pack(pack_sem, src_ref, b, wts, packs.at[b])
        bias_v[...] = jnp.where(segc_ref[...] == segr_ref[...], 0.0, -1e30)
        y_v[1] = x_ref[...]
        for b in range(2 * layers):
            pltpu.make_async_copy(wts[1], packs.at[b], pack_sem).wait()

        def save_a(layer):
            return [(buf, out.at[layer]) for buf, out in zip(buf_a, out_a)]

        def save_f(layer):
            return [(buf, out.at[layer]) for buf, out in zip(buf_f, out_f)]

        def wait_rows(i):
            for copy in row_copies(y_v.at[i], 0, 0, sent, rows_sems.at[i]):
                copy.wait()

        def layer_step(layer, carry):
            b = 2 * layer
            slab = slabs.at[0]

            @pl.when(layer > 0)
            def _():
                group_a.wait(*save_a(0))
                wait_rows(0)

            qkv, ctx, probs = buf_a[:3]
            project(y_v.at[1], slab, qkv, lambda i: slab_part(slab_sems[0], wts, slab, i))
            slab_part(slab_sems[0], wts, slab, PARTS - 1)
            for p in range(PARTS):
                load_slab(slab_sems[1], src_ref, b + 1, wts, slabs.at[1], [p])
                load_down(down_sems, down_ref, layer, down_v, p)
            attend(qkv, bias_v, probs, ctx)
            by_columns(acc, lambda cols: dot(
                ctx[...], slab[:, 3 * width + cols.start : 3 * width + cols.stop]))

            @pl.when(layer + 1 < layers)
            def _():
                load_slab(slab_sems[0], src_ref, b + 2, wts, slab)

            post_forward(packs.at[b], small_ref.at[src_ref[b, GROUP]], y_v.at[1], acc, y_v.at[0],
                         buf_a[3:], adapt)
            for copy in row_copies(y_v.at[0], b, core, sent, rows_sems.at[0]):
                copy.start()
            group_a.start(*save_a(layer))

            @pl.when(layer > 0)
            def _():
                group_slope.wait(save_f(0)[0])
                group_f.wait(*save_f(0)[1:])
                wait_rows(1)

            def ready(i):
                slab_part(slab_sems[1], wts, slabs.at[1], i)
                down_part(down_sems, down_ref, down_v, i)

            ffn_branch(y_v.at[0], slabs.at[1], down_v, buf_f[0], acc, ready)
            group_slope.start(save_f(layer)[0])
            post_forward(packs.at[b + 1], small_ref.at[src_ref[b + 1, GROUP]], y_v.at[0], acc,
                         y_v.at[1], buf_f[1:], adapt)
            for copy in row_copies(y_v.at[1], b + 1, core, sent, rows_sems.at[1]):
                copy.start()
            group_f.start(*save_f(layer)[1:])
            return carry

        lax.fori_loop(0, layers, layer_step, 0)
        group_a.wait(*save_a(0))
        group_slope.wait(save_f(0)[0])
        group_f.wait(*save_f(0)[1:])
        for i in range(2):
            wait_rows(i)

    outs = [(like((layers,) + sh, dt), ANY) for b in range(2) for sh, dt in shapes[b]]
    outs.append((like((2 * layers * GROUP, rows // GROUP, width)), ANY))
    scratch = [
        pltpu.VMEM((2,) + weights[0].shape, BF),
        pltpu.VMEM((2 * layers,) + weights[1].shape, BF),
        pltpu.VMEM((ff, width), BF), pltpu.VMEM((2, rows, width), BF),
        pltpu.VMEM((rows, width), F32), pltpu.VMEM((rows, rows), F32),
        pltpu.SemaphoreType.DMA((48,))]
    for b in range(2):
        scratch += [pltpu.VMEM(sh, dt) for sh, dt in shapes[b]]
    res = run(
        body, [(src, SMEM), (x, VMEM), (seg[:, None], VMEM), (seg[None, :], VMEM), (small, VMEM),
               (down, ANY)] + weight_ins(weights), outs, scratch, "forward", 60)
    return (res[:n_a], res[n_a:-1]), res[-1]


def backward(dy, saved, src, weights, small, down, adapt):
    rows, width = dy.shape
    ff = weights[0].shape[1]
    layers = down.shape[0]
    n_w = len(weight_ins(weights))
    saved_a, saved_f = saved
    n_a, n_f = len(saved_a), len(saved_f)

    def body(ins, outs, scratch):
        src_ref, dy_ref, small_ref, down_ref = ins[:4]
        wts = weight_refs(ins[4 : 4 + n_w], weights)
        in_a, in_f = ins[4 + n_w : 4 + n_w + n_a], ins[4 + n_w + n_a :]
        sent, grads_out = outs[0], outs[1:]
        slabs, packs, down_v, acc, db, dpt, grads, dx_v, dc_v, dqkv, dy_v, sem_ref = scratch[:12]
        buf_a, buf_f = scratch[12 : 12 + n_a], scratch[12 + n_a :]
        sems = Sems(sem_ref)
        slab_sems = [sems.run(PARTS) for i in range(2)]
        down_sems, slope_sems, pack_sems = sems.run(PARTS), sems.run(PARTS), sems.run(2)
        group_a, post_a = Group(sems, 3), Group(sems, n_a - 3)
        post_f, group_dy = Group(sems, n_f - 1), Group(sems, 1)
        rows_sems, grads_sems = sems.run(2), sems.run(2)
        core = src_ref[0, GROUP + 1]

        def pairs(refs, bufs, layer):
            return [(x.at[layer], buf) for x, buf in zip(refs, bufs)]

        def slope_part(layer, p):
            columns = part_of(ff, p)
            return pltpu.make_async_copy(in_f[0].at[layer, :, columns], buf_f[0].at[:, columns],
                                         slope_sems.at[p])

        def fetch_f(layer):
            b = 2 * layer + 1
            post_f.start(*pairs(in_f[1:], buf_f[1:], layer))
            load_pack(pack_sems.at[0], src_ref, b, wts, packs.at[0])
            for p in range(PARTS):
                load_down(down_sems, down_ref, layer, down_v, p)
                slope_part(layer, p).start()
                load_slab(slab_sems[0], src_ref, b, wts, slabs.at[0], [p])

        def wait_pack(i):
            pltpu.make_async_copy(wts[1], packs.at[i], pack_sems.at[i]).wait()

        def wait_sent(i, value_ref):
            for copy in row_copies(value_ref, 0, 0, sent, rows_sems.at[i]):
                copy.wait()
            pltpu.make_async_copy(grads.at[i], grads_out[0], grads_sems.at[i]).wait()

        group_dy.start((dy_ref, dy_v))
        fetch_f(layers - 1)
        group_dy.wait((dy_ref, dy_v))

        def layer_step(count, carry):
            layer = layers - 1 - count
            b = 2 * layer + 1

            @pl.when(count > 0)
            def _():
                wait_sent(0, dx_v)

            post_f.wait(*pairs(in_f[1:], buf_f[1:], 0))
            wait_pack(0)
            post_backward(packs.at[0], small_ref.at[src_ref[b, GROUP]], dy_v, buf_f[1:], acc, db,
                          grads.at[0], dpt, adapt)
            send_grads(grads_sems.at[0], grads.at[0], src_ref[b, GROUP], grads_out)
            load_pack(pack_sems.at[1], src_ref, b - 1, wts, packs.at[1])
            post_a.start(*pairs(in_a[3:], buf_a[3:], layer))
            load_slab(slab_sems[1], src_ref, b - 1, wts, slabs.at[1], [PARTS - 1])
            group_a.start(*pairs(in_a[:3], buf_a[:3], layer))
            load_slab(slab_sems[1], src_ref, b - 1, wts, slabs.at[1], range(PARTS - 1))

            def ready(i):
                slab_part(slab_sems[0], wts, slabs.at[0], i)
                down_part(down_sems, down_ref, down_v, i)
                slope_part(0, i).wait()

            ffn_branch_back(db, slabs.at[0], down_v, buf_f[0], acc, ready)
            dx_v[...] = acc[...].astype(BF)
            for copy in row_copies(dx_v, b, core, sent, rows_sems.at[0]):
                copy.start()

            @pl.when(count > 0)
            def _():
                wait_sent(1, dy_v)

            post_a.wait(*pairs(in_a[3:], buf_a[3:], 0))
            wait_pack(1)

            @pl.when(layer > 0)
            def _():
                fetch_f(layer - 1)

            post_backward(packs.at[1], small_ref.at[src_ref[b - 1, GROUP]], dx_v, buf_a[3:], acc,
                          db, grads.at[1], dpt, adapt)
            send_grads(grads_sems.at[1], grads.at[1], src_ref[b - 1, GROUP], grads_out)
            slab = slabs.at[1]
            slab_part(slab_sems[1], wts, slab, PARTS - 1)
            by_columns(dc_v, lambda cols: dot_t(db[...], slab[cols, 3 * width :]))
            group_a.wait(*pairs(in_a[:3], buf_a[:3], 0))
            attend_back(buf_a[0], buf_a[1], dc_v, buf_a[2], dqkv)
            for i in range(PARTS - 1):
                slab_part(slab_sems[1], wts, slab, i)
            by_columns(dy_v, lambda cols: acc[:, cols] + dot_t(dqkv[...], slab[cols, : 3 * width]))
            for copy in row_copies(dy_v, b - 1, core, sent, rows_sems.at[1]):
                copy.start()
            return carry

        lax.fori_loop(0, layers, layer_step, 0)
        wait_sent(0, dx_v)
        wait_sent(1, dy_v)

    grad_shape = (2 * adapt + SUMS, width)
    outs = [(like((2 * layers * GROUP, rows // GROUP, width)), ANY)]
    outs += [(like(grad_shape), ANY)] * (2 * layers)
    scratch = [
        pltpu.VMEM((2,) + weights[0].shape, BF), pltpu.VMEM((2,) + weights[1].shape, BF),
        pltpu.VMEM((ff, width), BF), pltpu.VMEM((rows, width), F32), pltpu.VMEM((rows, width), BF),
        pltpu.VMEM((128, rows), BF), pltpu.VMEM((2,) + grad_shape, BF),
        pltpu.VMEM((rows, width), BF), pltpu.VMEM((rows, width), BF),
        pltpu.VMEM((rows, 3 * width), BF), pltpu.VMEM((rows, width), BF),
        pltpu.SemaphoreType.DMA((48,))]
    scratch += [pltpu.VMEM(x.shape[1:], x.dtype) for x in tuple(saved_a) + tuple(saved_f)]
    res = run(
        body, [(src, SMEM), (dy, ANY), (small, VMEM), (down, ANY)] + weight_ins(weights)
        + [(x, ANY) for x in tuple(saved_a) + tuple(saved_f)], outs, scratch, "backward", 60)
    return res[0], res[1:]


def settle(x):
    def body(ins, outs, scratch):
        buf, sems = scratch
        loads = [pltpu.make_async_copy(ins[0].at[i], buf.at[i], sems.at[i])
                 for i in range(x.shape[0])]
        stores = [pltpu.make_async_copy(buf.at[i], outs[0].at[i], sems.at[i])
                  for i in range(x.shape[0])]
        for load in loads:
            load.start()
        for load, store in zip(loads, stores):
            load.wait()
            store.start()
        for store in stores:
            store.wait()

    return run(body, [(x, ANY)], [(like(x.shape), ANY)],
               [pltpu.VMEM(x.shape, BF), pltpu.SemaphoreType.DMA((x.shape[0],))], "settle", 3)[0]


def per_device(tokens, cotangent, segment_ids, slabs, ffn_down,
               ad_down, ad_down_bias, ad_up, ad_up_bias, ln_gain, ln_bias):
    n_section, n_group = lax.axis_size("section"), lax.axis_size("group")
    s, group, core = (lax.axis_index(name) for name in ("section", "group", "core"))
    n_micro, rows_dev, width = tokens.shape
    adapt = ad_down.shape[2]
    sections = range(n_section)

    def sect(x, apart):
        return lax.ppermute(x, "section", [(i, i ^ apart) for i in sections])

    def peer(x):
        return lax.ppermute(x, "core", [(0, 1), (1, 0)])

    def by_core(x, apart):
        pairs = [(i * GROUP + c, (i ^ apart[c]) * GROUP + c) for i in sections for c in range(GROUP)]
        return lax.ppermute(x, ("section", "core"), pairs)

    slab = slabs[0]
    half = slab.shape[0] // GROUP
    mats = jnp.concatenate([ad_down[0].T, ad_up[0]], axis=0).astype(BF)
    own_pack = jnp.concatenate([mats[i : i + EXTRA] for i in range(0, 2 * adapt, EXTRA)], axis=1)
    own_small = jnp.concatenate([jnp.pad(ad_down_bias, ((0, 0), (0, width - adapt))), ad_up_bias,
                                 ln_gain, ln_bias, jnp.zeros((4, width), F32)], axis=0)
    small = [own_small] + [sect(own_small, d) for d in range(1, n_section)]
    size = own_pack.shape[0] // GROUP
    plane = group % 2
    pack_half = lax.dynamic_slice_in_dim(own_pack, core * size, size, 0)
    quarter = lax.dynamic_slice_in_dim(slab, core * half + plane * (half // 2), half // 2, 0)
    given = jnp.concatenate([lax.dynamic_slice_in_dim(slab, core * half, half, 0), pack_half],
                            axis=0)
    own_micro = s * GROUP + core
    peer_micro = s * GROUP + 1 - core

    def gather_item(x):
        mine = lax.dynamic_index_in_dim(x, own_micro, 0, keepdims=False)
        given = lax.dynamic_index_in_dim(x, peer_micro, 0, keepdims=False)
        return jnp.concatenate([mine, peer(given)], axis=0)

    hidden = gather_item(tokens)
    cot = gather_item(cotangent)
    second = by_core(given, (2, 1))
    first = by_core(jnp.concatenate([quarter, pack_half], axis=0), (1, 2))
    second, first, hidden, cot, *small = lax.optimization_barrier(
        (second, first, hidden, cot, *small))
    first_z = lax.ppermute(first, "group", [(i, i ^ 1) for i in range(n_group)])
    third = by_core(second, (1, 2))
    bufs = [(first, first_z), (second,), (third,)]
    bufs += [tuple(peer(x) for x in parts) for parts in bufs]
    small = jnp.stack(small)

    item_start = group * GROUP * rows_dev
    seg = jnp.concatenate([
        lax.dynamic_slice(segment_ids, (own_micro, item_start + c * rows_dev), (1, rows_dev))[0]
        for c in (core, 1 - core)])

    def source(b):
        d = s ^ b
        at = []
        for h in range(GROUP):
            i = jnp.where(d == 3, 3, jnp.where((d == 1) == (h == 0), 1, 2))
            at.append(jnp.where(d == 0, 0, jnp.where(core == h, i, i + 3)))
        return jnp.stack(at + [d, core, plane]).astype(jnp.int32)

    src = jnp.stack([source(b) for b in sections])
    weights = (slab, own_pack, bufs)

    def to_owners(x):
        return lax.all_to_all(x, ("section", "core"), 0, 0, tiled=True)

    saved, sent = forward(hidden, seg, src, weights, small, ffn_down, adapt)
    block_outputs = to_owners(sent)
    leaving, grads = backward(cot, saved, src, weights, small, ffn_down, adapt)
    block_outputs, leaving, *grads = lax.optimization_barrier((block_outputs, leaving, *grads))
    block_outputs = settle(block_outputs)

    coming = [sect(grads[d], d) for d in range(1, n_section)]
    *coming, leaving = lax.optimization_barrier((*coming, leaving))
    total = grads[0].astype(F32)
    for part in coming:
        total = total + part.astype(F32)
    total = total.astype(BF)
    input_grads = settle(to_owners(leaving))
    total = (total.astype(F32) + peer(total).astype(F32)).astype(BF)
    apart = 1
    while apart < n_group:
        other = lax.ppermute(total, "group", [(i, i ^ apart) for i in range(n_group)])
        total = (total.astype(F32) + other.astype(F32)).astype(BF)
        apart *= 2
    total = total.astype(F32)
    return (block_outputs[None], input_grads[None], total[:adapt].T[None],
            total[2 * adapt + 3, :adapt][None], total[adapt : 2 * adapt][None],
            total[2 * adapt][None], total[2 * adapt + 1][None], total[2 * adapt + 2][None])


def solution(mesh):
    n_section, n_rows = mesh.devices.shape
    cores = Mesh(mesh.devices.reshape(n_section, n_rows // GROUP, GROUP),
                 ("section", "group", "core"))
    rows = ("group", "core")
    in_specs = (
        P(None, rows, None), P(None, rows, None), P(), P("section", None, None), P(),
        P("section", None, None), P("section", None), P("section", None, None),
        P("section", None), P("section", None), P("section", None),
    )
    out_specs = (
        P("section", None, rows, None), P("section", None, rows, None),
        P("section", None, None), P("section", None), P("section", None, None),
        P("section", None), P("section", None), P("section", None),
    )
    return jax.shard_map(
        per_device, mesh=cores, in_specs=in_specs, out_specs=out_specs, check_vma=False
    )
```
